32 devices in a mesh: dp: 8 (over y, x, core), mp: 4 (over z).
Axes of the slice: x: 2, y: 2, z: 4, core: 2. Of those that a mesh axis runs over, the one named last changes fastest.
Arguments:
- hidden_in: float32 [8192, 1280], P(('dp', 'mp')), may hold values from -6 to 6
- pre_gain: float32 [2, 1280], P(None, ('dp', 'mp')), may hold values from 0.1 to 1.9
- pre_bias: float32 [2, 1280], P(None, ('dp', 'mp')), may hold values from -3 to 3
- qkv_weight: bfloat16 [2, 3, 1280, 1280], P(None, None, 'dp', 'mp'), may hold values from -0.15625 to 0.15625
- qkv_bias: float32 [2, 3, 1280], P(None, None, ('dp', 'mp')), may hold values from -3 to 3
- proj_weight: bfloat16 [2, 1280, 1280], P(None, 'mp', 'dp'), may hold values from -0.625 to 0.625
- proj_bias: float32 [2, 1280], P(None, ('dp', 'mp')), may hold values from -2 to 2
- mid_gain: float32 [2, 1280], P(None, ('dp', 'mp')), may hold values from 0.1 to 1.9
- mid_bias: float32 [2, 1280], P(None, ('dp', 'mp')), may hold values from -3 to 3
- up_weight: bfloat16 [2, 1280, 5120], P(None, 'dp', 'mp'), may hold values from -0.15625 to 0.15625
- up_bias: float32 [2, 5120], P(None, ('dp', 'mp')), may hold values from -3 to 3
- down_weight: bfloat16 [2, 5120, 1280], P(None, 'mp', 'dp'), may hold values from -0.15625 to 0.15625
- down_bias: float32 [2, 1280], P(None, ('dp', 'mp')), may hold values from -2 to 2
- picture_ids: int32 [8192], P('dp'), may hold values from 0 to 5, as said below
- positions: int32 [2, 8192], P(None, 'dp'), may hold values from 0 to 31, as said below
- pad_mask: int32 [8192], P('dp'), may hold values from 0 to 1, as said below
- cotangent: float32 [8192, 1280], P(('dp', 'mp')), may hold values from -6 to 6
Outputs:
- out_hidden: float32 [8192, 1280], P(('dp', 'mp'))
- grad_hidden: float32 [8192, 1280], P(('dp', 'mp'))
- pre_gain_grad: float32 [2, 1280], P(None, ('dp', 'mp'))
- pre_bias_grad: float32 [2, 1280], P(None, ('dp', 'mp'))
- qkv_weight_grad: float32 [2, 3, 1280, 1280], P(None, None, 'dp', 'mp')
- qkv_bias_grad: float32 [2, 3, 1280], P(None, None, ('dp', 'mp'))
- proj_weight_grad: float32 [2, 1280, 1280], P(None, 'mp', 'dp')
- proj_bias_grad: float32 [2, 1280], P(None, ('dp', 'mp'))
- mid_gain_grad: float32 [2, 1280], P(None, ('dp', 'mp'))
- mid_bias_grad: float32 [2, 1280], P(None, ('dp', 'mp'))
- up_weight_grad: float32 [2, 1280, 5120], P(None, 'dp', 'mp')
- up_bias_grad: float32 [2, 5120], P(None, ('dp', 'mp'))
- down_weight_grad: float32 [2, 5120, 1280], P(None, 'mp', 'dp')
- down_bias_grad: float32 [2, 1280], P(None, ('dp', 'mp'))
The draws below stay inside these ranges and needn't reach their ends.
Inputs may be any that keep to these rules, and one draw needn't show every extreme that they name: `picture_ids`: within each row of 1024 patches the ids never fall and each picture's patches stand together; the padding at a row's end carries one id beyond its pictures; each row begins with a picture 32 patches high and one 32 patches wide. `positions`: each picture is 10 to 32 patches high and wide, its patches in row-major order; padding has 0. `pad_mask`: 1 on a leading run of each row, 0 after it.
All inputs are finite; a program needn't handle non-finite values.
Results may differ from the reference program's by a relative error of at most 0.02.
Values may be sent and summed in bfloat16 or wider, within the bound.
A program may use at most 192 MiB of HBM per device.

```python
import jax
import jax.numpy as jnp
from jax import lax

D = 1280
HEADS = 16
HD = 80
FF = 5120
LAYERS = 2
SIDE_MIN = 10
SIDE_MAX = 32
ROW_LEN = 1024
TOKENS = 8192


def packing(key):
    row_count = TOKENS // ROW_LEN
    slot_count = ROW_LEN // (SIDE_MIN * SIDE_MIN) + 2
    key_parts = jax.random.split(key, 3)
    heights = jax.random.randint(key_parts[0], (row_count, slot_count), SIDE_MIN, SIDE_MAX + 1)
    widths = jax.random.randint(key_parts[1], (row_count, slot_count), SIDE_MIN, SIDE_MAX + 1)
    leading = jax.random.randint(key_parts[2], (row_count, 2), SIDE_MIN, SIDE_MAX // 2 + 1)
    first_row = jnp.arange(row_count, dtype=jnp.int32)[:, None] == 0
    leading = jnp.where(first_row, SIDE_MIN, leading)
    heights = jnp.where(first_row, SIDE_MIN, heights)
    widths = jnp.where(first_row, SIDE_MIN, widths)
    slot_at = jnp.arange(slot_count, dtype=jnp.int32)[None, :]
    heights = jnp.where(slot_at == 0, SIDE_MAX, jnp.where(slot_at == 1, leading[:, 1:2], heights))
    widths = jnp.where(slot_at == 0, leading[:, 0:1], jnp.where(slot_at == 1, SIDE_MAX, widths))
    end_at = jnp.cumsum(heights * widths, axis=1)
    fitting = end_at <= ROW_LEN
    bounds = jnp.where(fitting, end_at, ROW_LEN + 1)
    filled = jnp.max(jnp.where(fitting, end_at, 0), axis=1)
    starts = jnp.concatenate([jnp.zeros((row_count, 1), jnp.int32), bounds[:, :-1]], axis=1)
    patch_at = jnp.arange(ROW_LEN, dtype=jnp.int32)[None, :]
    picture = jnp.sum((bounds[:, None, :] <= patch_at[:, :, None]).astype(jnp.int32), axis=2)
    picked = picture[:, :, None] == slot_at[:, None, :]
    begin_at = jnp.sum(jnp.where(picked, starts[:, None, :], 0), axis=2)
    width_at = jnp.sum(jnp.where(picked, widths[:, None, :], 0), axis=2)
    offset = patch_at - begin_at
    inside = patch_at < filled[:, None]
    row_pos = jnp.where(inside, offset // width_at, 0)
    col_pos = jnp.where(inside, offset % width_at, 0)
    return (picture.reshape(-1), jnp.stack([row_pos.reshape(-1), col_pos.reshape(-1)]), inside.astype(jnp.int32).reshape(-1))


def draw_picture_ids(key, part):
    return packing(jax.random.fold_in(key, 11))[0]


def draw_positions(key, part):
    return packing(jax.random.fold_in(key, 11))[1]


def draw_pad_mask(key, part):
    return packing(jax.random.fold_in(key, 11))[2]


def levels(stream_key, dims, shards, smallest, top_value):
    factor_of = 1.0
    for axis_at, parts in shards:
        steps = jax.random.uniform(jax.random.fold_in(jax.random.fold_in(stream_key, 6), axis_at), (parts,), jnp.float32, smallest / len(shards), top_value / len(shards))
        factor_of = factor_of * jnp.repeat(jnp.exp(steps), dims[axis_at] // parts).reshape((-1,) + (1,) * (len(dims) - 1 - axis_at))
    return factor_of


def gaussian(key, shape, deviation, limit, pieces=(), kind=jnp.bfloat16):
    values = deviation * jax.random.normal(key, shape, jnp.float32)
    if pieces:
        values = values * levels(key, shape, pieces, -0.22, 0.18)
    return jnp.clip(values, -limit, limit).astype(kind)


def setup_inputs(seed: int = 0) -> dict:
    seeds = jax.random.split(jax.random.key(seed), 18)
    return {
        "hidden_in": gaussian(seeds[0], (TOKENS, D), 1.0, 6.0, ((0, 32),), jnp.float32),
        "pre_gain": jnp.clip(1.0 + 0.18 * jax.random.normal(seeds[1], (LAYERS, D), jnp.float32), 0.1, 1.9),
        "pre_bias": gaussian(seeds[2], (LAYERS, D), 0.5, 3.0, ((1, 32),), jnp.float32),
        "qkv_weight": gaussian(seeds[3], (LAYERS, 3, D, D), D ** -0.5, 0.15625, ((2, 8), (3, 4))),
        "qkv_bias": gaussian(seeds[4], (LAYERS, 3, D), 0.5, 3.0, ((2, 32),), jnp.float32),
        "proj_weight": gaussian(seeds[5], (LAYERS, D, D), (D // 16) ** -0.5, 0.625, ((1, 4), (2, 8))),
        "proj_bias": gaussian(seeds[6], (LAYERS, D), 0.3, 2.0, ((1, 32),), jnp.float32),
        "mid_gain": jnp.clip(1.0 + 0.18 * jax.random.normal(seeds[7], (LAYERS, D), jnp.float32), 0.1, 1.9),
        "mid_bias": gaussian(seeds[8], (LAYERS, D), 0.5, 3.0, ((1, 32),), jnp.float32),
        "up_weight": gaussian(seeds[9], (LAYERS, D, FF), D ** -0.5, 0.15625, ((1, 8), (2, 4))),
        "up_bias": gaussian(seeds[10], (LAYERS, FF), 0.5, 3.0, ((1, 32),), jnp.float32),
        "down_weight": gaussian(seeds[11], (LAYERS, FF, D), (FF // 4) ** -0.5, 0.15625, ((1, 4), (2, 8))),
        "down_bias": gaussian(seeds[12], (LAYERS, D), 0.3, 2.0, ((1, 32),), jnp.float32),
        "picture_ids": draw_picture_ids(jax.random.fold_in(seeds[17], 71), 0),
        "positions": draw_positions(jax.random.fold_in(seeds[17], 71), 0),
        "pad_mask": draw_pad_mask(jax.random.fold_in(seeds[17], 71), 0),
        "cotangent": gaussian(seeds[16], (TOKENS, D), 1.0, 6.0, ((0, 32),), jnp.float32),
    }


@jax.custom_vjp
def low(v):
    return lax.optimization_barrier(v.astype(jnp.bfloat16)).astype(jnp.float32)

@jax.custom_vjp
def low_back(v):
    return v

def low_keep(v):
    return (low(v), None)

def low_pass(kept, grad):
    return (grad,)

def back_keep(v):
    return (v, None)

def back_low(kept, grad):
    return (low(grad),)
low.defvjp(low_keep, low_pass)
low_back.defvjp(back_keep, back_low)
EPSILON = 1e-06

def matmul(left_side, right_side):
    return jnp.dot(left_side, right_side, precision=lax.Precision.HIGHEST)

def layer_norm(values, gain, shift):
    centre = values - lax.optimization_barrier(jnp.mean(values, axis=-1, keepdims=True))
    spread = lax.optimization_barrier(jnp.mean(centre * centre, axis=-1, keepdims=True))
    return centre * lax.rsqrt(spread + EPSILON) * gain + shift

def rotary_tables(coords):
    quarter = HD // 4
    powers = jnp.arange(quarter, dtype=jnp.float32) * (4.0 / HD)
    inverse = 10000.0 ** (-powers)
    height_angle = coords[0].astype(jnp.float32)[:, None] * inverse[None, :]
    width_angle = coords[1].astype(jnp.float32)[:, None] * inverse[None, :]
    angles = jnp.concatenate([height_angle, width_angle], axis=1)
    angles = jnp.concatenate([angles, angles], axis=1)
    return (jnp.cos(angles)[:, None, :], jnp.sin(angles)[:, None, :])

def rotate(values, cosine, sine):
    half_size = HD // 2
    turned = jnp.concatenate([-values[..., half_size:], values[..., :half_size]], axis=-1)
    return values * cosine + turned * sine

def quick_gelu(values):
    return values / (1.0 + jnp.exp(-1.702 * values))

def block(hidden, weights, layer_index, cosine, sine, allowed):
    pre_gain, pre_bias, qkv_weight, qkv_bias, proj_weight, proj_bias, mid_gain, mid_bias, up_weight, up_bias, down_weight, down_bias = weights
    length = hidden.shape[0]
    normed = low(layer_norm(hidden, pre_gain[layer_index], pre_bias[layer_index]))
    linear = [low_back(matmul(normed, qkv_weight[layer_index, which]) + qkv_bias[layer_index, which]).reshape(length, HEADS, HD) for which in range(3)]
    queries = low(rotate(linear[0], cosine, sine))
    key_rows = low(rotate(linear[1], cosine, sine))
    value_rows = low(linear[2])
    scores = low_back(jnp.einsum('qhe,khe->hqk', queries, key_rows, precision=lax.Precision.HIGHEST) * HD ** (-0.5))
    scores = jnp.where(allowed[None], scores, -1e+30)
    row_max = lax.optimization_barrier(jnp.max(scores, axis=-1, keepdims=True))
    exponent = jnp.exp(scores - row_max)
    chances = low(exponent / lax.optimization_barrier(jnp.sum(exponent, axis=-1, keepdims=True)))
    mixed = low(low_back(jnp.einsum('hqk,khe->qhe', chances, value_rows, precision=lax.Precision.HIGHEST).reshape(length, D)))
    attended = low_back(matmul(mixed, proj_weight[layer_index]) + proj_bias[layer_index])
    middle = hidden + attended
    normed_mid = low(layer_norm(middle, mid_gain[layer_index], mid_bias[layer_index]))
    upward = low_back(matmul(normed_mid, up_weight[layer_index]) + up_bias[layer_index])
    active = low(quick_gelu(upward))
    output = low_back(matmul(active, down_weight[layer_index]) + down_bias[layer_index])
    return middle + output

def reference(hidden_in, pre_gain, pre_bias, qkv_weight, qkv_bias, proj_weight, proj_bias, mid_gain, mid_bias, up_weight, up_bias, down_weight, down_bias, picture_ids, positions, pad_mask, cotangent):
    weights = tuple((item.astype(jnp.float32) for item in (pre_gain, pre_bias, qkv_weight, qkv_bias, proj_weight, proj_bias, mid_gain, mid_bias, up_weight, up_bias, down_weight, down_bias)))
    row_count = hidden_in.shape[0] // ROW_LEN

    def one_row(totals, row_index):
        begin_row = (row_index * ROW_LEN).astype(jnp.int32)
        hidden = lax.dynamic_slice_in_dim(hidden_in, begin_row, ROW_LEN, 0)
        row_ids = lax.dynamic_slice_in_dim(picture_ids, begin_row, ROW_LEN, 0)
        row_keep = lax.dynamic_slice_in_dim(pad_mask, begin_row, ROW_LEN, 0)
        coords = lax.dynamic_slice_in_dim(positions, begin_row, ROW_LEN, 1)
        seats = jnp.arange(ROW_LEN, dtype=jnp.int32)
        allowed = (row_ids[:, None] == row_ids[None, :]) & (row_keep[None, :] == 1) | (seats[:, None] == seats[None, :])
        cosine, sine = rotary_tables(coords)

        def tower(hidden_row, *params):
            for layer_index in range(LAYERS):
                hidden_row = block(hidden_row, params, layer_index, cosine, sine, allowed)
            return hidden_row
        result, pullback = jax.vjp(tower, hidden, *weights)
        grads = pullback(lax.dynamic_slice_in_dim(cotangent, begin_row, ROW_LEN, 0))
        totals = tuple((total + grad_part for total, grad_part in zip(totals, grads[1:])))
        return (totals, (result, grads[0]))
    zeros = tuple((jnp.zeros_like(item) for item in weights))
    totals, (outputs, input_grads) = lax.scan(one_row, zeros, jnp.arange(row_count, dtype=jnp.int32))
    return (outputs.reshape(-1, D), input_grads.reshape(-1, D), totals[0], totals[1], totals[2], totals[3], totals[4], totals[5], totals[6], totals[7], totals[8], totals[9], totals[10], totals[11])
```

```python
import jax
import jax.numpy as jnp
from jax import lax
from jax.sharding import PartitionSpec as P

D = 1280
HD = 80
LAYERS = 2
EPSILON = 1e-06
F32 = jnp.float32
BF16 = jnp.bfloat16
HIGHEST = lax.Precision.HIGHEST


def normalise(values):
    centre = values - jnp.mean(values, axis=-1, keepdims=True)
    spread = jnp.mean(centre * centre, axis=-1, keepdims=True)
    scale = lax.rsqrt(spread + EPSILON)
    return centre * scale, scale


def norm_backward(values, gain, grad):
    normed, scale = normalise(values)
    inner = grad * gain
    mean_inner = jnp.mean(inner, axis=-1, keepdims=True)
    mean_cross = jnp.mean(inner * normed, axis=-1, keepdims=True)
    grad_values = scale * (inner - mean_inner - normed * mean_cross)
    return grad_values, jnp.sum(grad * normed, axis=0), jnp.sum(grad, axis=0)


def dot(left, right, left_dim, right_dim, kind=F32, precision=None):
    return lax.dot_general(
        left,
        right,
        (((left_dim,), (right_dim,)), ((), ())),
        preferred_element_type=F32,
        precision=precision,
    ).astype(kind)


def rotary_tables(coords):
    quarter = HD // 4
    powers = jnp.arange(quarter, dtype=F32) * (4.0 / HD)
    inverse = 10000.0 ** (-powers)
    height_angle = coords[0].astype(F32)[:, None] * inverse[None, :]
    width_angle = coords[1].astype(F32)[:, None] * inverse[None, :]
    angles = jnp.concatenate([height_angle, width_angle], axis=1)
    angles = jnp.concatenate([angles, angles], axis=1)
    return (jnp.cos(angles)[:, None, :], jnp.sin(angles)[:, None, :])


def rotate(values, cosine, sine):
    half_size = HD // 2
    turned = jnp.concatenate([-values[..., half_size:], values[..., :half_size]], axis=-1)
    return values * cosine + turned * sine


def rotate_back(values, cosine, sine):
    half_size = HD // 2
    turned = jnp.concatenate([-values[..., half_size:], values[..., :half_size]], axis=-1)
    return values * cosine - turned * sine


def masked_scores(queries, key_rows, codes):
    scores = jnp.einsum("qhe,khe->hqk", queries, key_rows, preferred_element_type=F32)
    scores = scores * HD ** (-0.5)
    return jnp.where((codes[:, None] == codes[None, :])[None], scores, -1e30)


def attend_forward(linear, cosine, sine, codes):
    length = linear.shape[0]
    parts = linear.reshape(length, 3, -1, HD)
    queries = rotate(parts[:, 0], cosine, sine).astype(BF16)
    key_rows = rotate(parts[:, 1], cosine, sine).astype(BF16)
    value_rows = parts[:, 2].astype(BF16)
    scores = masked_scores(queries, key_rows, codes)
    row_max = jnp.max(scores, axis=-1, keepdims=True)
    exponent = jnp.exp(scores - row_max)
    totals = jnp.sum(exponent, axis=-1, keepdims=True)
    chances = (exponent / totals).astype(BF16)
    mixed = jnp.einsum("hqk,khe->qhe", chances, value_rows, preferred_element_type=F32)
    return mixed.astype(BF16).reshape(length, -1), (
        queries,
        key_rows,
        value_rows,
        row_max + jnp.log(totals),
    )


def attend_backward(saved, mixed, grad_mixed, cosine, sine, codes):
    queries, key_rows, value_rows, log_totals = saved
    length = queries.shape[0]
    scale = HD ** (-0.5)
    grad_mixed = grad_mixed.reshape(value_rows.shape)
    scores = masked_scores(queries, key_rows, codes)
    chances = jnp.exp(scores - log_totals)
    grad_chance = jnp.einsum("qhe,khe->hqk", grad_mixed, value_rows, preferred_element_type=F32)
    centre = jnp.sum(chances * grad_chance, axis=-1, keepdims=True)
    grad_scores = (chances * (grad_chance - centre)).astype(BF16)
    grad_query = scale * jnp.einsum(
        "hqk,khe->qhe", grad_scores, key_rows, preferred_element_type=F32
    )
    grad_key = scale * jnp.einsum("hqk,qhe->khe", grad_scores, queries, preferred_element_type=F32)
    grad_value = jnp.einsum(
        "hqk,qhe->khe", chances.astype(BF16), grad_mixed, preferred_element_type=F32
    )
    return jnp.concatenate(
        [
            rotate_back(grad_query, cosine, sine).reshape(length, -1),
            rotate_back(grad_key, cosine, sine).reshape(length, -1),
            grad_value.reshape(length, -1),
        ],
        axis=1,
    ).astype(BF16)


def make_body(dp, mp):
    assert mp == 4 and dp >= 2 and dp & (dp - 1) == 0
    count = dp * mp
    high_bits = [1 << b for b in range(1, dp.bit_length() - 1)]

    def across(value, bit):
        return lax.ppermute(value, "dp", [(i, i ^ bit) for i in range(dp)])

    def core_side(value):
        return across(value, 1)

    def line_side(value):
        return lax.ppermute(value, "mp", [(i, i ^ 1) for i in range(mp)])

    def swapped(d, m):
        return (d & ~1 | m >> 1) * mp + ((d & 1) << 1 | m & 1)

    swap_pairs = [(d * mp + m, swapped(d, m)) for d in range(dp) for m in range(mp)]

    def swap(value):
        return lax.ppermute(value, ("dp", "mp"), swap_pairs)

    def gather_weight(mine):
        pair = swap(jnp.stack([mine, core_side(mine)]))
        if len(high_bits) == 2:
            low, high = high_bits
            by_low, by_high = across(pair, low), across(pair, high)
            pieces = [pair, by_low, by_high, across(by_low[:1], high), across(by_high[1:], low)]
        else:
            pieces = [pair]
            for bit in high_bits:
                pieces = pieces + [across(piece, bit) for piece in pieces]
        return jnp.concatenate(pieces, axis=0).reshape(D, mine.shape[-1])

    def scatter_weight(grad):
        blocks = grad.reshape(dp, D // dp, grad.shape[-1])

        def add(*terms):
            total = terms[0].astype(F32)
            for term in terms[1:]:
                total = total + term.astype(F32)
            return total.astype(BF16)

        if len(high_bits) == 2:
            low, high = high_bits
            first = across(blocks[6:7], high)
            second = across(blocks[7:8], low)
            by_low = jnp.concatenate([add(blocks[2:3], first), blocks[3:4]], axis=0)
            by_high = jnp.concatenate([blocks[4:5], add(blocks[5:6], second)], axis=0)
            blocks = add(blocks[:2], across(by_low, low), across(by_high, high))
        else:
            for bit in high_bits[::-1]:
                half = blocks.shape[0] // 2
                blocks = add(blocks[:half], across(blocks[half:], bit))
        blocks = swap(blocks)
        return blocks[0].astype(F32) + core_side(blocks[1]).astype(F32)

    def scatter_vectors(values):
        index = lax.axis_index("dp") * mp + lax.axis_index("mp")
        bit = count // 2
        while bit:
            half = values.shape[0] // 2
            top = (index & bit) != 0
            low, high = values[:half], values[half:]
            sent = jnp.where(top, low, high)
            if bit >= mp:
                got = across(sent, bit // mp)
            else:
                got = lax.ppermute(sent, "mp", [(i, i ^ bit) for i in range(mp)])
            values = jnp.where(top, high, low) + got
            bit //= 2
        return values[0]

    def gather_rows(mine):
        near = core_side(mine)
        far = line_side(mine)
        return [mine, near, far, core_side(far)]

    def scatter_rows(part):
        far = part(2) + core_side(part(3).astype(BF16)).astype(F32)
        far = line_side(far.astype(BF16))
        near = part(0) + core_side(part(1).astype(BF16)).astype(F32)
        return near + far.astype(F32)

    def body(
        hidden_in,
        pre_gain,
        pre_bias,
        qkv_weight,
        qkv_bias,
        proj_weight,
        proj_bias,
        mid_gain,
        mid_bias,
        up_weight,
        up_bias,
        down_weight,
        down_bias,
        picture_ids,
        positions,
        pad_mask,
        cotangent,
    ):
        dp_at, mp_at = lax.axis_index("dp"), lax.axis_index("mp")
        group_at = (dp_at & ~1) | (mp_at >> 1)
        quarter_at = ((dp_at & 1) << 1) | (mp_at & 1)
        depth = D // dp
        columns = qkv_weight.shape[3]
        units = up_weight.shape[2]
        heads = columns // HD

        place = jnp.arange(D, dtype=jnp.int32)
        moved = ((place // depth) ^ group_at) * depth + place % depth
        reorder = place[:, None] == moved[None, :]
        reorder_low = reorder.astype(BF16)
        reorder_full = reorder.astype(F32)

        def turn_low(values):
            return dot(values.astype(BF16), reorder_low, 1, 0)

        hidden = turn_low(swap(hidden_in.astype(BF16)))
        weights = []
        for layer in range(LAYERS):
            weights.append(
                (
                    gather_weight(qkv_weight[layer].transpose(1, 0, 2).reshape(depth, 3 * columns)),
                    gather_weight(proj_weight[layer].T),
                    gather_weight(up_weight[layer]),
                    gather_weight(down_weight[layer].T),
                )
            )

        wide = (pre_gain, pre_bias, proj_bias, mid_gain, mid_bias, down_bias)
        packed = jnp.concatenate(
            [item.reshape(-1) for item in wide] + [qkv_bias.reshape(-1), up_bias.reshape(-1)]
        )
        packed = lax.all_gather(packed, ("dp", "mp"), axis=0, tiled=False)
        each = D // count
        wide_count = len(wide) * LAYERS
        split = (wide_count + 3 * LAYERS) * each
        vectors = packed[:, :split].reshape(count, -1, each).transpose(1, 0, 2).reshape(-1, D)
        wide_all = dot(vectors[:wide_count], reorder_full, 1, 0, precision=HIGHEST)
        wide_all = wide_all.reshape(len(wide), LAYERS, D)
        pre_gain_all, pre_bias_all, proj_bias_all, mid_gain_all, mid_bias_all, down_bias_all = (
            wide_all[i] for i in range(len(wide))
        )
        qkv_bias_mine = lax.dynamic_slice_in_dim(
            vectors[wide_count:], quarter_at * columns, columns, 1
        ).reshape(LAYERS, 3 * columns)
        up_all = packed[:, split:].reshape(count, LAYERS, -1).transpose(1, 0, 2)
        up_bias_mine = lax.dynamic_slice_in_dim(
            up_all.reshape(LAYERS, -1), quarter_at * units, units, 1
        )

        length = picture_ids.shape[0]
        quarter = length // mp
        row_at = jnp.arange(length, dtype=jnp.int32)
        codes = jnp.where(pad_mask == 1, picture_ids, 1024 + row_at)
        row_facts = swap(jnp.concatenate([codes[None], positions], axis=0))
        row_facts = jnp.concatenate(
            [
                lax.dynamic_slice_in_dim(row_facts, (quarter_at ^ which) * quarter, quarter, 1)
                for which in (0, 2, 1, 3)
            ],
            axis=1,
        )
        codes = row_facts[0]
        cosine, sine = rotary_tables(row_facts[1:])

        kept = []
        for layer in range(LAYERS):
            w_qkv, w_proj, w_up, w_down = weights[layer]
            start = hidden
            normed = normalise(hidden)[0] * pre_gain_all[layer] + pre_bias_all[layer]
            rows = gather_rows(normed.astype(BF16))
            attn_rows = jnp.concatenate(rows, axis=0)
            linear = dot(attn_rows, w_qkv, 1, 0) + qkv_bias_mine[layer]
            mixed, saved = attend_forward(linear, cosine, sine, codes)
            attended = scatter_rows(
                lambda i, a=mixed, w=w_proj: dot(a[i * quarter : (i + 1) * quarter], w, 1, 1)
            )
            middle = hidden + (attended + proj_bias_all[layer])
            normed = normalise(middle)[0] * mid_gain_all[layer] + mid_bias_all[layer]
            rows = gather_rows(normed.astype(BF16))
            mid_rows = jnp.concatenate(rows, axis=0)
            upward = dot(mid_rows, w_up, 1, 0) + up_bias_mine[layer]
            sigmoid = 1.0 / (1.0 + jnp.exp(-1.702 * upward))
            active = (upward * sigmoid).astype(BF16)
            slope = (sigmoid + 1.702 * upward * sigmoid * (1.0 - sigmoid)).astype(BF16)
            output = scatter_rows(
                lambda i, a=active, w=w_down: dot(a[i * quarter : (i + 1) * quarter], w, 1, 1)
            )
            hidden = middle + (output + down_bias_all[layer])
            kept.append((start, attn_rows, mixed, saved, middle, mid_rows, active, slope))

        out_hidden = swap(turn_low(hidden).astype(BF16)).astype(F32)
        gradient = turn_low(swap(cotangent.astype(BF16)))
        grads = []
        parts = []
        for layer in reversed(range(LAYERS)):
            w_qkv, w_proj, w_up, w_down = weights[layer]
            start, attn_rows, mixed, saved, middle, mid_rows, active, slope = kept[layer]
            grad_out = gradient.astype(BF16)
            down_bias_part = jnp.sum(grad_out.astype(F32), axis=0)
            grad_rows = jnp.concatenate(gather_rows(grad_out), axis=0)
            grad_up = (dot(grad_rows, w_down, 1, 0) * slope.astype(F32)).astype(BF16)
            grad_normed = scatter_rows(
                lambda i, a=grad_up, w=w_up: dot(a[i * quarter : (i + 1) * quarter], w, 1, 1)
            )
            down_grad = scatter_weight(dot(grad_rows, active, 0, 0, BF16))
            up_bias_part = jnp.sum(grad_up.astype(F32), axis=0)
            up_grad = scatter_weight(dot(mid_rows, grad_up, 0, 0, BF16))
            grad_middle, mid_gain_part, mid_bias_part = norm_backward(
                middle, mid_gain_all[layer], grad_normed
            )
            gradient = gradient + grad_middle
            grad_out = gradient.astype(BF16)
            proj_bias_part = jnp.sum(grad_out.astype(F32), axis=0)
            grad_rows = jnp.concatenate(gather_rows(grad_out), axis=0)
            grad_mixed = dot(grad_rows, w_proj, 1, 0, BF16)
            proj_grad = scatter_weight(dot(grad_rows, mixed, 0, 0, BF16))
            grad_linear = attend_backward(saved, mixed, grad_mixed, cosine, sine, codes)
            grad_normed = scatter_rows(
                lambda i, a=grad_linear, w=w_qkv: dot(a[i * quarter : (i + 1) * quarter], w, 1, 1)
            )
            qkv_bias_part = jnp.sum(grad_linear.astype(F32), axis=0)
            qkv_grad = scatter_weight(dot(attn_rows, grad_linear, 0, 0, BF16))
            grad_start, pre_gain_part, pre_bias_part = norm_backward(
                start, pre_gain_all[layer], grad_normed
            )
            gradient = gradient + grad_start
            grads.append(
                (
                    qkv_grad.reshape(depth, 3, columns).transpose(1, 0, 2),
                    proj_grad.T,
                    up_grad,
                    down_grad.T,
                )
            )
            parts.append(
                (
                    (
                        pre_gain_part,
                        pre_bias_part,
                        proj_bias_part,
                        mid_gain_part,
                        mid_bias_part,
                        down_bias_part,
                    ),
                    qkv_bias_part.reshape(3, columns),
                    up_bias_part,
                )
            )
        grads, parts = grads[::-1], parts[::-1]
        grad_hidden = swap(turn_low(gradient).astype(BF16)).astype(F32)

        stacked = jnp.stack([part[0][i] for i in range(len(wide)) for part in parts])
        stacked = dot(stacked, reorder_full, 1, 0, precision=HIGHEST)
        qkv_padded = lax.dynamic_update_slice_in_dim(
            jnp.zeros((LAYERS * 3, D), F32),
            jnp.concatenate([part[1] for part in parts], axis=0),
            quarter_at * columns,
            1,
        )
        up_padded = lax.dynamic_update_slice_in_dim(
            jnp.zeros((LAYERS, units * mp), F32),
            jnp.stack([part[2] for part in parts]),
            quarter_at * units,
            1,
        )
        by_owner = jnp.concatenate([stacked, qkv_padded], axis=0).reshape(-1, count, each)
        by_owner = jnp.concatenate(
            [
                by_owner.transpose(1, 0, 2).reshape(count, -1),
                up_padded.reshape(LAYERS, count, -1).transpose(1, 0, 2).reshape(count, -1),
            ],
            axis=1,
        )
        mine = scatter_vectors(by_owner)
        wide_grads = mine[: wide_count * each].reshape(len(wide), LAYERS, each)
        qkv_bias_grad = mine[wide_count * each : split].reshape(LAYERS, 3, each)
        up_bias_grad = mine[split:].reshape(LAYERS, -1)
        matrices = [jnp.stack([entry[i] for entry in grads]) for i in range(4)]
        return (
            out_hidden,
            grad_hidden,
            wide_grads[0],
            wide_grads[1],
            matrices[0],
            qkv_bias_grad,
            matrices[1],
            wide_grads[2],
            wide_grads[3],
            wide_grads[4],
            matrices[2],
            up_bias_grad,
            matrices[3],
            wide_grads[5],
        )

    return body


def solution(mesh):
    rows = P(("dp", "mp"), None)
    vector = P(None, ("dp", "mp"))
    vectors = P(None, None, ("dp", "mp"))
    qkv = P(None, None, "dp", "mp")
    tall = P(None, "mp", "dp")
    broad = P(None, "dp", "mp")
    return jax.shard_map(
        make_body(mesh.shape["dp"], mesh.shape["mp"]),
        mesh=mesh,
        in_specs=(
            rows,
            vector,
            vector,
            qkv,
            vectors,
            tall,
            vector,
            vector,
            vector,
            broad,
            vector,
            tall,
            vector,
            P("dp"),
            P(None, "dp"),
            P("dp"),
            rows,
        ),
        out_specs=(
            rows,
            rows,
            vector,
            vector,
            qkv,
            vectors,
            tall,
            vector,
            vector,
            vector,
            broad,
            vector,
            tall,
            vector,
        ),
        check_vma=False,
    )
```

```python
import jax
import jax.numpy as jnp
from jax import lax
from jax.experimental import pallas as pl
from jax.experimental.pallas import tpu as pltpu
from jax.sharding import PartitionSpec as P

D = 1280
HD = 80
LAYERS = 2
EPSILON = 1e-06
F32 = jnp.float32
BF16 = jnp.bfloat16
HIGHEST = lax.Precision.HIGHEST


def normalise(values):
    centre = values - jnp.mean(values, axis=-1, keepdims=True)
    spread = jnp.mean(centre * centre, axis=-1, keepdims=True)
    scale = lax.rsqrt(spread + EPSILON)
    return centre * scale, scale


def norm_backward(values, gain, grad):
    normed, scale = normalise(values)
    inner = grad * gain
    mean_inner = jnp.mean(inner, axis=-1, keepdims=True)
    mean_cross = jnp.mean(inner * normed, axis=-1, keepdims=True)
    grad_values = scale * (inner - mean_inner - normed * mean_cross)
    return grad_values, jnp.sum(grad * normed, axis=0), jnp.sum(grad, axis=0)


def dot(left, right, left_dim, right_dim, kind=F32, precision=None):
    return lax.dot_general(
        left,
        right,
        (((left_dim,), (right_dim,)), ((), ())),
        preferred_element_type=F32,
        precision=precision,
    ).astype(kind)


def rotary_tables(coords):
    quarter = HD // 4
    powers = jnp.arange(quarter, dtype=F32) * (4.0 / HD)
    inverse = 10000.0 ** (-powers)
    height_angle = inverse[:, None] * coords[0].astype(F32)[None, :]
    width_angle = inverse[:, None] * coords[1].astype(F32)[None, :]
    angles = jnp.concatenate([height_angle, width_angle], axis=0)
    return (jnp.cos(angles), jnp.sin(angles))


TILE = 256
MASKED = -1e30
LOG2E = 1.4426950408889634
SCORE_SCALE = HD**-0.5 * LOG2E


def mat(left, right):
    return lax.dot_general(left, right, (((1,), (0,)), ((), ())), preferred_element_type=F32)


def mat_turned(left, right):
    return lax.dot_general(left, right, (((1,), (1,)), ((), ())), preferred_element_type=F32)


def tile_bias(code_col, code_row, keys, queries):
    same = code_col[keys, :] == code_row[:, queries]
    return jnp.where(same, 0.0, MASKED)


def tiles(at):
    return pl.ds(pl.multiple_of(at * TILE, TILE), TILE)


def forward_kernel(active, lin, cosine, sine, code_row, code_col, qkv, mixed, log_sum, k_rows, top, total, acc):
    heads, length = k_rows.shape[0], k_rows.shape[1]
    blocks = length // TILE
    cos, sin = cosine[...], sine[...]
    half = HD // 2
    for head in range(heads):
        for which in range(2):
            base = (which * heads + head) * HD
            low, high = lin[base : base + half, :], lin[base + half : base + HD, :]
            turned = jnp.concatenate([low * cos - high * sin, high * cos + low * sin], axis=0)
            qkv[base : base + HD, :] = turned.astype(BF16)
            if which == 1:
                k_rows[head] = turned.T.astype(BF16)
        base = (2 * heads + head) * HD
        qkv[base : base + HD, :] = lin[base : base + HD, :].astype(BF16)

    def query_block(q_at, carry):
        queries = tiles(q_at)
        top[...] = jnp.full(top.shape, MASKED, F32)
        total[...] = jnp.zeros(total.shape, F32)
        acc[...] = jnp.zeros(acc.shape, F32)

        def key_block(k_at, carry):
            @pl.when(active[q_at * blocks + k_at] != 0)
            def _():
                keys = tiles(k_at)
                bias = tile_bias(code_col, code_row, keys, queries)
                for head in range(heads):
                    q_base, v_base = head * HD, (2 * heads + head) * HD
                    scores = mat(k_rows[head, keys, :], qkv[q_base : q_base + HD, queries]) + bias
                    old = top[head]
                    new = jnp.maximum(old, jnp.max(scores, axis=0, keepdims=True))
                    chance = jnp.exp2((scores - new) * SCORE_SCALE)
                    fade = jnp.exp2((old - new) * SCORE_SCALE)
                    top[head] = new
                    total[head] = total[head] * fade + jnp.sum(chance, axis=0, keepdims=True)
                    acc[head] = acc[head] * fade + mat(
                        qkv[v_base : v_base + HD, keys], chance.astype(BF16)
                    )

            return carry

        lax.fori_loop(0, blocks, key_block, 0)
        for head in range(heads):
            mixed[head * HD : (head + 1) * HD, queries] = (acc[head] / total[head]).astype(BF16)
            log_sum[head, :, queries] = top[head] * SCORE_SCALE + jnp.log2(total[head])
        return carry

    lax.fori_loop(0, blocks, query_block, 0)


def backward_kernel(active, qkv, mixed, grad_mixed, log_sum, cosine, sine, code_row, code_col, out, k_rows, v_rows, centre, grad_q, grad_k, grad_v):
    heads, length = k_rows.shape[0], k_rows.shape[1]
    blocks = length // TILE
    for head in range(heads):
        k_base, v_base = (heads + head) * HD, (2 * heads + head) * HD
        k_rows[head] = qkv[k_base : k_base + HD, :].astype(F32).T.astype(BF16)
        v_rows[head] = qkv[v_base : v_base + HD, :].astype(F32).T.astype(BF16)
        rows = slice(head * HD, (head + 1) * HD)
        centre[head] = jnp.sum(
            grad_mixed[rows, :].astype(F32) * mixed[rows, :].astype(F32), axis=0, keepdims=True
        )
    grad_q[...] = jnp.zeros(grad_q.shape, F32)
    grad_k[...] = jnp.zeros(grad_k.shape, F32)
    grad_v[...] = jnp.zeros(grad_v.shape, F32)

    def query_block(q_at, carry):
        queries = tiles(q_at)

        def key_block(k_at, carry):
            @pl.when(active[q_at * blocks + k_at] != 0)
            def _():
                keys = tiles(k_at)
                bias = tile_bias(code_col, code_row, keys, queries)
                for head in range(heads):
                    rows = slice(head * HD, (head + 1) * HD)
                    k_base = (heads + head) * HD
                    scores = mat(k_rows[head, keys, :], qkv[rows, queries]) + bias
                    chance = jnp.exp2(scores * SCORE_SCALE - log_sum[head, :, queries])
                    grad_chance = mat(v_rows[head, keys, :], grad_mixed[rows, queries])
                    grad_score = (chance * (grad_chance - centre[head, :, queries])).astype(BF16)
                    grad_v[head, :, keys] += mat_turned(grad_mixed[rows, queries], chance.astype(BF16))
                    grad_k[head, :, keys] += mat_turned(qkv[rows, queries], grad_score)
                    grad_q[head, :, queries] += mat(qkv[k_base : k_base + HD, keys], grad_score)

            return carry

        return lax.fori_loop(0, blocks, key_block, carry)

    lax.fori_loop(0, blocks, query_block, 0)
    half = HD // 2
    scale = HD**-0.5
    cos, sin = cosine[...] * scale, sine[...] * scale
    for head in range(heads):
        for which, grad in ((0, grad_q), (1, grad_k)):
            base = (which * heads + head) * HD
            low, high = grad[head, :half, :], grad[head, half:, :]
            turned = jnp.concatenate([low * cos + high * sin, high * cos - low * sin], axis=0)
            out[base : base + HD, :] = turned.astype(BF16)
        base = (2 * heads + head) * HD
        out[base : base + HD, :] = grad_v[head].astype(BF16)


def whole(count):
    return [pl.BlockSpec(memory_space=pltpu.VMEM)] * count


def attend_forward(linear, facts):
    active, cosine, sine, code_row, code_col = facts
    width, length = linear.shape
    heads = width // (3 * HD)
    return pl.pallas_call(
        forward_kernel,
        name="attend_forward",
        out_shape=(
            jax.ShapeDtypeStruct((width, length), BF16),
            jax.ShapeDtypeStruct((heads * HD, length), BF16),
            jax.ShapeDtypeStruct((heads, 1, length), F32),
        ),
        in_specs=[pl.BlockSpec(memory_space=pltpu.SMEM)] + whole(5),
        out_specs=tuple(whole(3)),
        scratch_shapes=[
            pltpu.VMEM((heads, length, HD), BF16),
            pltpu.VMEM((heads, 1, TILE), F32),
            pltpu.VMEM((heads, 1, TILE), F32),
            pltpu.VMEM((heads, HD, TILE), F32),
        ],
        compiler_params=pltpu.CompilerParams(vmem_limit_bytes=40 << 20),
        cost_estimate=pl.CostEstimate(
            flops=heads * length * length * HD * 4, bytes_accessed=10 << 20, transcendentals=heads * length * length
        ),
    )(active, linear, cosine, sine, code_row, code_col)


def attend_backward(qkv, mixed, grad_mixed, log_sum, facts):
    active, cosine, sine, code_row, code_col = facts
    width, length = qkv.shape
    heads = width // (3 * HD)
    return pl.pallas_call(
        backward_kernel,
        name="attend_backward",
        out_shape=jax.ShapeDtypeStruct((width, length), BF16),
        in_specs=[pl.BlockSpec(memory_space=pltpu.SMEM)] + whole(8),
        out_specs=pl.BlockSpec(memory_space=pltpu.VMEM),
        scratch_shapes=[
            pltpu.VMEM((heads, length, HD), BF16),
            pltpu.VMEM((heads, length, HD), BF16),
            pltpu.VMEM((heads, 1, length), F32),
            pltpu.VMEM((heads, HD, length), F32),
            pltpu.VMEM((heads, HD, length), F32),
            pltpu.VMEM((heads, HD, length), F32),
        ],
        compiler_params=pltpu.CompilerParams(vmem_limit_bytes=40 << 20),
        cost_estimate=pl.CostEstimate(
            flops=heads * length * length * HD * 10, bytes_accessed=10 << 20, transcendentals=heads * length * length
        ),
    )(active, qkv, mixed, grad_mixed, log_sum, cosine, sine, code_row, code_col)


def tile_overlap(codes):
    blocks = codes.reshape(-1, TILE)
    least, most = jnp.min(blocks, axis=1), jnp.max(blocks, axis=1)
    meet = (least[:, None] <= most[None, :]) & (least[None, :] <= most[:, None])
    return meet.astype(jnp.int32).reshape(-1)


def make_body(dp, mp):
    assert mp == 4 and dp >= 2 and dp & (dp - 1) == 0
    count = dp * mp
    high_bits = [1 << b for b in range(1, dp.bit_length() - 1)]

    def across(value, bit):
        return lax.ppermute(value, "dp", [(i, i ^ bit) for i in range(dp)])

    def core_side(value):
        return across(value, 1)

    def line_side(value):
        return lax.ppermute(value, "mp", [(i, i ^ 1) for i in range(mp)])

    def swapped(d, m):
        return (d & ~1 | m >> 1) * mp + ((d & 1) << 1 | m & 1)

    swap_pairs = [(d * mp + m, swapped(d, m)) for d in range(dp) for m in range(mp)]

    def swap(value):
        return lax.ppermute(value, ("dp", "mp"), swap_pairs)

    def gather_blocks(mine):
        pair = swap(jnp.stack([mine, core_side(mine)]))
        if len(high_bits) == 2:
            low, high = high_bits
            by_low, by_high = across(pair, low), across(pair, high)
            pieces = [pair, by_low, by_high, across(by_low[:1], high), across(by_high[1:], low)]
        else:
            pieces = [pair]
            for bit in high_bits:
                pieces = pieces + [across(piece, bit) for piece in pieces]
        return [
            jnp.concatenate([piece[:, g] for piece in pieces], axis=0).reshape(D, mine.shape[-1])
            for g in range(mine.shape[0])
        ]

    def scatter_blocks(grads):
        blocks = [grad.reshape(dp, D // dp, grad.shape[-1]) for grad in grads]

        def pick(begin, end):
            return jnp.stack([block[begin:end] for block in blocks], axis=1)

        def add(*terms):
            total = terms[0].astype(F32)
            for term in terms[1:]:
                total = total + term.astype(F32)
            return total.astype(BF16)

        if len(high_bits) == 2:
            low, high = high_bits
            first = across(pick(6, 7), high)
            second = across(pick(7, 8), low)
            by_low = jnp.concatenate([add(pick(2, 3), first), pick(3, 4)], axis=0)
            by_high = jnp.concatenate([pick(4, 5), add(pick(5, 6), second)], axis=0)
            total = add(pick(0, 2), across(by_low, low), across(by_high, high))
        else:
            total = pick(0, dp)
            for bit in high_bits[::-1]:
                half = total.shape[0] // 2
                total = add(total[:half], across(total[half:], bit))
        total = swap(total)
        return total[0].astype(F32) + core_side(total[1]).astype(F32)

    def gather_vectors(mine):
        index = lax.axis_index("dp") * mp + lax.axis_index("mp")
        values = mine[None]
        bit = 1
        while bit < count:
            if bit >= mp:
                got = across(values, bit // mp)
            else:
                got = lax.ppermute(values, "mp", [(i, i ^ bit) for i in range(mp)])
            values = jnp.concatenate([values, got], axis=0)
            bit *= 2
        at = jnp.arange(count, dtype=jnp.int32)
        order = (at[:, None] ^ index) == at[None, :]
        return dot(order.astype(F32), values, 1, 0, precision=HIGHEST)

    def scatter_vectors(values):
        index = lax.axis_index("dp") * mp + lax.axis_index("mp")
        bit = count // 2
        while bit:
            half = values.shape[0] // 2
            top = (index & bit) != 0
            low, high = values[:half], values[half:]
            sent = jnp.where(top, low, high)
            if bit >= mp:
                got = across(sent, bit // mp)
            else:
                got = lax.ppermute(sent, "mp", [(i, i ^ bit) for i in range(mp)])
            values = jnp.where(top, high, low) + got
            bit //= 2
        return values[0]

    def gather_rows(mine):
        near = core_side(mine)
        far = line_side(mine)
        return [mine, near, far, core_side(far)]

    def scatter_rows(part):
        far = part(2) + core_side(part(3).astype(BF16)).astype(F32)
        far = line_side(far.astype(BF16))
        near = part(0) + core_side(part(1).astype(BF16)).astype(F32)
        return near + far.astype(F32)

    def body(
        hidden_in,
        pre_gain,
        pre_bias,
        qkv_weight,
        qkv_bias,
        proj_weight,
        proj_bias,
        mid_gain,
        mid_bias,
        up_weight,
        up_bias,
        down_weight,
        down_bias,
        picture_ids,
        positions,
        pad_mask,
        cotangent,
    ):
        dp_at, mp_at = lax.axis_index("dp"), lax.axis_index("mp")
        group_at = (dp_at & ~1) | (mp_at >> 1)
        quarter_at = ((dp_at & 1) << 1) | (mp_at & 1)
        depth = D // dp
        columns = qkv_weight.shape[3]
        units = up_weight.shape[2]
        heads = columns // HD

        place = jnp.arange(D, dtype=jnp.int32)
        moved = ((place // depth) ^ group_at) * depth + place % depth
        reorder = place[:, None] == moved[None, :]
        reorder_low = reorder.astype(BF16)
        reorder_full = reorder.astype(F32)

        def turn_low(values):
            return dot(values.astype(BF16), reorder_low, 1, 0)

        hidden = turn_low(swap(hidden_in.astype(BF16)))
        qkv_width, proj_width = 3 * columns, columns
        qkv_space, proj_space = -(-qkv_width // 128) * 128, -(-proj_width // 128) * 128

        def pack_attention(for_qkv, for_proj):
            return jnp.concatenate(
                [
                    jnp.pad(for_qkv, ((0, 0), (0, qkv_space - qkv_width))),
                    jnp.pad(for_proj, ((0, 0), (0, proj_space - proj_width))),
                ],
                axis=1,
            )

        def unpack_attention(packed):
            return packed[:, :qkv_width], packed[:, qkv_space : qkv_space + proj_width]

        weights = []
        for layer in range(LAYERS):
            mine = pack_attention(
                qkv_weight[layer].transpose(1, 0, 2).reshape(depth, qkv_width),
                proj_weight[layer].T,
            )
            w_qkv, w_proj = unpack_attention(gather_blocks(mine[None])[0])
            w_up, w_down = gather_blocks(jnp.stack([up_weight[layer], down_weight[layer].T]))
            weights.append((w_qkv, w_proj, w_up, w_down))

        wide = (pre_gain, pre_bias, proj_bias, mid_gain, mid_bias, down_bias)
        packed = jnp.concatenate(
            [item.reshape(-1) for item in wide] + [qkv_bias.reshape(-1), up_bias.reshape(-1)]
        )
        packed = gather_vectors(packed)
        each = D // count
        wide_count = len(wide) * LAYERS
        split = (wide_count + 3 * LAYERS) * each
        vectors = packed[:, :split].reshape(count, -1, each).transpose(1, 0, 2).reshape(-1, D)
        wide_all = dot(vectors[:wide_count], reorder_full, 1, 0, precision=HIGHEST)
        wide_all = wide_all.reshape(len(wide), LAYERS, D)
        pre_gain_all, pre_bias_all, proj_bias_all, mid_gain_all, mid_bias_all, down_bias_all = (
            wide_all[i] for i in range(len(wide))
        )
        qkv_bias_mine = lax.dynamic_slice_in_dim(
            vectors[wide_count:], quarter_at * columns, columns, 1
        ).reshape(LAYERS, 3 * columns)
        up_all = packed[:, split:].reshape(count, LAYERS, -1).transpose(1, 0, 2)
        up_bias_mine = lax.dynamic_slice_in_dim(
            up_all.reshape(LAYERS, -1), quarter_at * units, units, 1
        )

        length = picture_ids.shape[0]
        quarter = length // mp
        row_at = jnp.arange(length, dtype=jnp.int32)
        codes = jnp.where(pad_mask == 1, picture_ids, 1024 + row_at)
        row_facts = swap(jnp.concatenate([codes[None], positions], axis=0))
        row_facts = jnp.concatenate(
            [
                lax.dynamic_slice_in_dim(row_facts, (quarter_at ^ which) * quarter, quarter, 1)
                for which in (0, 2, 1, 3)
            ],
            axis=1,
        )
        codes = row_facts[0]
        facts = (tile_overlap(codes), *rotary_tables(row_facts[1:]), codes[None], codes[:, None])

        kept = []
        for layer in range(LAYERS):
            w_qkv, w_proj, w_up, w_down = weights[layer]
            start = hidden
            normed = normalise(hidden)[0] * pre_gain_all[layer] + pre_bias_all[layer]
            rows = gather_rows(normed.astype(BF16))
            attn_rows = jnp.concatenate(rows, axis=0)
            linear = dot(w_qkv, attn_rows, 0, 1) + qkv_bias_mine[layer][:, None]
            qkv, mixed, log_sum = attend_forward(linear, facts)
            attended = scatter_rows(
                lambda i, a=mixed, w=w_proj: dot(a[:, i * quarter : (i + 1) * quarter], w, 0, 1)
            )
            middle = hidden + (attended + proj_bias_all[layer])
            normed = normalise(middle)[0] * mid_gain_all[layer] + mid_bias_all[layer]
            rows = gather_rows(normed.astype(BF16))
            mid_rows = jnp.concatenate(rows, axis=0)
            upward = dot(mid_rows, w_up, 1, 0) + up_bias_mine[layer]
            sigmoid = 1.0 / (1.0 + jnp.exp(-1.702 * upward))
            active = (upward * sigmoid).astype(BF16)
            slope = (sigmoid + 1.702 * upward * sigmoid * (1.0 - sigmoid)).astype(BF16)
            output = scatter_rows(
                lambda i, a=active, w=w_down: dot(a[i * quarter : (i + 1) * quarter], w, 1, 1)
            )
            hidden = middle + (output + down_bias_all[layer])
            kept.append((start, attn_rows, qkv, mixed, log_sum, middle, mid_rows, active, slope))

        out_hidden = swap(turn_low(hidden).astype(BF16)).astype(F32)
        gradient = turn_low(swap(cotangent.astype(BF16)))
        grads = []
        parts = []
        for layer in reversed(range(LAYERS)):
            w_qkv, w_proj, w_up, w_down = weights[layer]
            start, attn_rows, qkv, mixed, log_sum, middle, mid_rows, active, slope = kept[layer]
            grad_out = gradient.astype(BF16)
            down_bias_part = jnp.sum(grad_out.astype(F32), axis=0)
            grad_rows = jnp.concatenate(gather_rows(grad_out), axis=0)
            grad_up = (dot(grad_rows, w_down, 1, 0) * slope.astype(F32)).astype(BF16)
            grad_normed = scatter_rows(
                lambda i, a=grad_up, w=w_up: dot(a[i * quarter : (i + 1) * quarter], w, 1, 1)
            )
            down_grad = dot(grad_rows, active, 0, 0, BF16)
            up_bias_part = jnp.sum(grad_up.astype(F32), axis=0)
            up_grad = dot(mid_rows, grad_up, 0, 0, BF16)
            ffn_grads = scatter_blocks([up_grad, down_grad])
            grad_middle, mid_gain_part, mid_bias_part = norm_backward(
                middle, mid_gain_all[layer], grad_normed
            )
            gradient = gradient + grad_middle
            grad_out = gradient.astype(BF16)
            proj_bias_part = jnp.sum(grad_out.astype(F32), axis=0)
            grad_rows = jnp.concatenate(gather_rows(grad_out), axis=0)
            grad_mixed = dot(w_proj, grad_rows, 0, 1, BF16)
            proj_grad = dot(grad_rows, mixed, 0, 1, BF16)
            grad_linear = attend_backward(qkv, mixed, grad_mixed, log_sum, facts)
            grad_normed = scatter_rows(
                lambda i, a=grad_linear, w=w_qkv: dot(
                    a[:, i * quarter : (i + 1) * quarter], w, 0, 1
                )
            )
            qkv_bias_part = jnp.sum(grad_linear.astype(F32), axis=1)
            qkv_grad = dot(attn_rows, grad_linear, 0, 1, BF16)
            attn_grads = scatter_blocks([pack_attention(qkv_grad, proj_grad)])[0]
            qkv_grad, proj_grad = unpack_attention(attn_grads)
            grad_start, pre_gain_part, pre_bias_part = norm_backward(
                start, pre_gain_all[layer], grad_normed
            )
            gradient = gradient + grad_start
            grads.append(
                (
                    qkv_grad.reshape(depth, 3, columns).transpose(1, 0, 2),
                    proj_grad.T,
                    ffn_grads[0],
                    ffn_grads[1].T,
                )
            )
            parts.append(
                (
                    (
                        pre_gain_part,
                        pre_bias_part,
                        proj_bias_part,
                        mid_gain_part,
                        mid_bias_part,
                        down_bias_part,
                    ),
                    qkv_bias_part.reshape(3, columns),
                    up_bias_part,
                )
            )
        grads, parts = grads[::-1], parts[::-1]
        grad_hidden = swap(turn_low(gradient).astype(BF16)).astype(F32)

        stacked = jnp.stack([part[0][i] for i in range(len(wide)) for part in parts])
        stacked = dot(stacked, reorder_full, 1, 0, precision=HIGHEST)
        qkv_padded = lax.dynamic_update_slice_in_dim(
            jnp.zeros((LAYERS * 3, D), F32),
            jnp.concatenate([part[1] for part in parts], axis=0),
            quarter_at * columns,
            1,
        )
        up_padded = lax.dynamic_update_slice_in_dim(
            jnp.zeros((LAYERS, units * mp), F32),
            jnp.stack([part[2] for part in parts]),
            quarter_at * units,
            1,
        )
        by_owner = jnp.concatenate([stacked, qkv_padded], axis=0).reshape(-1, count, each)
        by_owner = jnp.concatenate(
            [
                by_owner.transpose(1, 0, 2).reshape(count, -1),
                up_padded.reshape(LAYERS, count, -1).transpose(1, 0, 2).reshape(count, -1),
            ],
            axis=1,
        )
        mine = scatter_vectors(by_owner)
        wide_grads = mine[: wide_count * each].reshape(len(wide), LAYERS, each)
        qkv_bias_grad = mine[wide_count * each : split].reshape(LAYERS, 3, each)
        up_bias_grad = mine[split:].reshape(LAYERS, -1)
        matrices = [jnp.stack([entry[i] for entry in grads]) for i in range(4)]
        return (
            out_hidden,
            grad_hidden,
            wide_grads[0],
            wide_grads[1],
            matrices[0],
            qkv_bias_grad,
            matrices[1],
            wide_grads[2],
            wide_grads[3],
            wide_grads[4],
            matrices[2],
            up_bias_grad,
            matrices[3],
            wide_grads[5],
        )

    return body


def solution(mesh):
    rows = P(("dp", "mp"), None)
    vector = P(None, ("dp", "mp"))
    vectors = P(None, None, ("dp", "mp"))
    qkv = P(None, None, "dp", "mp")
    tall = P(None, "mp", "dp")
    broad = P(None, "dp", "mp")
    return jax.shard_map(
        make_body(mesh.shape["dp"], mesh.shape["mp"]),
        mesh=mesh,
        in_specs=(
            rows,
            vector,
            vector,
            qkv,
            vectors,
            tall,
            vector,
            vector,
            vector,
            broad,
            vector,
            tall,
            vector,
            P("dp"),
            P(None, "dp"),
            P("dp"),
            rows,
        ),
        out_specs=(
            rows,
            rows,
            vector,
            vector,
            qkv,
            vectors,
            tall,
            vector,
            vector,
            vector,
            broad,
            vector,
            tall,
            vector,
        ),
        check_vma=False,
    )
```

```python
import functools

import jax
import jax.numpy as jnp
from jax import lax
from jax.experimental import pallas as pl
from jax.experimental.pallas import tpu as pltpu
from jax.sharding import PartitionSpec as P

D = 1280
HD = 80
LAYERS = 2
EPSILON = 1e-06
F32 = jnp.float32
BF16 = jnp.bfloat16
HIGHEST = lax.Precision.HIGHEST


def normalise(values):
    centre = values - jnp.mean(values, axis=-1, keepdims=True)
    spread = jnp.mean(centre * centre, axis=-1, keepdims=True)
    scale = lax.rsqrt(spread + EPSILON)
    return centre * scale, scale


def norm_backward(values, gain, grad):
    normed, scale = normalise(values)
    inner = grad * gain
    mean_inner = jnp.mean(inner, axis=-1, keepdims=True)
    mean_cross = jnp.mean(inner * normed, axis=-1, keepdims=True)
    grad_values = scale * (inner - mean_inner - normed * mean_cross)
    return grad_values, jnp.sum(grad * normed, axis=0), jnp.sum(grad, axis=0)


def dot(left, right, left_dim, right_dim, kind=F32, precision=None):
    return lax.dot_general(
        left,
        right,
        (((left_dim,), (right_dim,)), ((), ())),
        preferred_element_type=F32,
        precision=precision,
    ).astype(kind)


def rotary_tables(coords):
    quarter = HD // 4
    powers = jnp.arange(quarter, dtype=F32) * (4.0 / HD)
    inverse = 10000.0 ** (-powers)
    height_angle = inverse[:, None] * coords[0].astype(F32)[None, :]
    width_angle = inverse[:, None] * coords[1].astype(F32)[None, :]
    angles = jnp.concatenate([height_angle, width_angle], axis=0)
    return (jnp.cos(angles), jnp.sin(angles))


TILE = 256
MASKED = -1e30
LOG2E = 1.4426950408889634
SCORE_SCALE = HD**-0.5 * LOG2E


def mat(left, right):
    return lax.dot_general(left, right, (((1,), (0,)), ((), ())), preferred_element_type=F32)


def mat_turned(left, right):
    return lax.dot_general(left, right, (((1,), (1,)), ((), ())), preferred_element_type=F32)


def tile_bias(code_col, code_row, keys, queries):
    same = code_col[keys, :] == code_row[:, queries]
    return jnp.where(same, 0.0, MASKED)


def tiles(at):
    return pl.ds(pl.multiple_of(at * TILE, TILE), TILE)


def forward_kernel(active, qkv, code_row, code_col, mixed, log_sum, k_rows, top, total, acc):
    heads, length = k_rows.shape[0], k_rows.shape[1]
    blocks = length // TILE
    for head in range(heads):
        base = (heads + head) * HD
        k_rows[head] = turned(qkv[base : base + HD, :]).astype(BF16)

    def query_block(q_at, carry):
        queries = tiles(q_at)
        top[...] = jnp.full(top.shape, MASKED, F32)
        total[...] = jnp.zeros(total.shape, F32)
        acc[...] = jnp.zeros(acc.shape, F32)

        def key_block(k_at, carry):
            @pl.when(active[q_at * blocks + k_at] != 0)
            def _():
                keys = tiles(k_at)
                bias = tile_bias(code_col, code_row, keys, queries)
                for head in range(heads):
                    q_base, v_base = head * HD, (2 * heads + head) * HD
                    scores = mat(k_rows[head, keys, :], qkv[q_base : q_base + HD, queries]) + bias
                    old = top[head]
                    new = jnp.maximum(old, jnp.max(scores, axis=0, keepdims=True))
                    chance = jnp.exp2((scores - new) * SCORE_SCALE)
                    fade = jnp.exp2((old - new) * SCORE_SCALE)
                    top[head] = new
                    total[head] = total[head] * fade + jnp.sum(chance, axis=0, keepdims=True)
                    acc[head] = acc[head] * fade + mat(
                        qkv[v_base : v_base + HD, keys], chance.astype(BF16)
                    )

            return carry

        lax.fori_loop(0, blocks, key_block, 0)
        for head in range(heads):
            mixed[head * HD : (head + 1) * HD, queries] = (acc[head] / total[head]).astype(BF16)
            log_sum[head, :, queries] = top[head] * SCORE_SCALE + jnp.log2(total[head])
        return carry

    lax.fori_loop(0, blocks, query_block, 0)


def backward_kernel(active, qkv, mixed, grad_mixed, log_sum, cosine, sine, code_row, code_col, out, k_rows, v_rows, centre, grad_q, grad_k, grad_v):
    heads, length = k_rows.shape[0], k_rows.shape[1]
    blocks = length // TILE
    for head in range(heads):
        k_base, v_base = (heads + head) * HD, (2 * heads + head) * HD
        k_rows[head] = qkv[k_base : k_base + HD, :].astype(F32).T.astype(BF16)
        v_rows[head] = qkv[v_base : v_base + HD, :].astype(F32).T.astype(BF16)
        rows = slice(head * HD, (head + 1) * HD)
        centre[head] = jnp.sum(
            grad_mixed[rows, :].astype(F32) * mixed[rows, :].astype(F32), axis=0, keepdims=True
        )
    grad_q[...] = jnp.zeros(grad_q.shape, F32)
    grad_k[...] = jnp.zeros(grad_k.shape, F32)
    grad_v[...] = jnp.zeros(grad_v.shape, F32)

    def query_block(q_at, carry):
        queries = tiles(q_at)

        def key_block(k_at, carry):
            @pl.when(active[q_at * blocks + k_at] != 0)
            def _():
                keys = tiles(k_at)
                bias = tile_bias(code_col, code_row, keys, queries)
                for head in range(heads):
                    rows = slice(head * HD, (head + 1) * HD)
                    k_base = (heads + head) * HD
                    scores = mat(k_rows[head, keys, :], qkv[rows, queries]) + bias
                    chance = jnp.exp2(scores * SCORE_SCALE - log_sum[head, :, queries])
                    grad_chance = mat(v_rows[head, keys, :], grad_mixed[rows, queries])
                    grad_score = (chance * (grad_chance - centre[head, :, queries])).astype(BF16)
                    grad_v[head, :, keys] += mat_turned(grad_mixed[rows, queries], chance.astype(BF16))
                    grad_k[head, :, keys] += mat_turned(qkv[rows, queries], grad_score)
                    grad_q[head, :, queries] += mat(qkv[k_base : k_base + HD, keys], grad_score)

            return carry

        return lax.fori_loop(0, blocks, key_block, carry)

    lax.fori_loop(0, blocks, query_block, 0)
    half = HD // 2
    scale = HD**-0.5
    cos, sin = cosine[...] * scale, sine[...] * scale
    for head in range(heads):
        for which, grad in ((0, grad_q), (1, grad_k)):
            base = (which * heads + head) * HD
            low, high = grad[head, :half, :], grad[head, half:, :]
            turned = jnp.concatenate([low * cos + high * sin, high * cos - low * sin], axis=0)
            out[base : base + HD, :] = turned.astype(BF16)
        base = (2 * heads + head) * HD
        out[base : base + HD, :] = grad_v[head].astype(BF16)


def whole(count):
    return [pl.BlockSpec(memory_space=pltpu.VMEM)] * count


def attend_forward(qkv, facts):
    active, _, _, code_row, code_col = facts
    width, length = qkv.shape
    heads = width // (3 * HD)
    return pl.pallas_call(
        forward_kernel,
        name="attend_forward",
        out_shape=(
            jax.ShapeDtypeStruct((heads * HD, length), BF16),
            jax.ShapeDtypeStruct((heads, 1, length), F32),
        ),
        in_specs=[pl.BlockSpec(memory_space=pltpu.SMEM)] + whole(3),
        out_specs=tuple(whole(2)),
        scratch_shapes=[
            pltpu.VMEM((heads, length, HD), BF16),
            pltpu.VMEM((heads, 1, TILE), F32),
            pltpu.VMEM((heads, 1, TILE), F32),
            pltpu.VMEM((heads, HD, TILE), F32),
        ],
        compiler_params=pltpu.CompilerParams(vmem_limit_bytes=40 << 20),
        cost_estimate=pl.CostEstimate(
            flops=heads * length * length * HD * 4,
            bytes_accessed=4 << 20,
            transcendentals=heads * length * length,
        ),
    )(active, qkv, code_row, code_col)


def attend_backward(qkv, mixed, grad_mixed, log_sum, facts):
    active, cosine, sine, code_row, code_col = facts
    width, length = qkv.shape
    heads = width // (3 * HD)
    return pl.pallas_call(
        backward_kernel,
        name="attend_backward",
        out_shape=jax.ShapeDtypeStruct((width, length), BF16),
        in_specs=[pl.BlockSpec(memory_space=pltpu.SMEM)] + whole(8),
        out_specs=pl.BlockSpec(memory_space=pltpu.VMEM),
        scratch_shapes=[
            pltpu.VMEM((heads, length, HD), BF16),
            pltpu.VMEM((heads, length, HD), BF16),
            pltpu.VMEM((heads, 1, length), F32),
            pltpu.VMEM((heads, HD, length), F32),
            pltpu.VMEM((heads, HD, length), F32),
            pltpu.VMEM((heads, HD, length), F32),
        ],
        compiler_params=pltpu.CompilerParams(vmem_limit_bytes=40 << 20),
        cost_estimate=pl.CostEstimate(
            flops=heads * length * length * HD * 10, bytes_accessed=10 << 20, transcendentals=heads * length * length
        ),
    )(active, qkv, mixed, grad_mixed, log_sum, cosine, sine, code_row, code_col)


def tile_overlap(codes):
    blocks = codes.reshape(-1, TILE)
    least, most = jnp.min(blocks, axis=1), jnp.max(blocks, axis=1)
    meet = (least[:, None] <= most[None, :]) & (least[None, :] <= most[:, None])
    return meet.astype(jnp.int32).reshape(-1)


(
    ACT, ALL, ATTN, BACKWARD, CORE, CORNER, CORNERS, CROSS, DIAGONAL, DOWN, ENDS, ENTER, ENTERED,
    ENTER_AT, ENTER_BIAS, ENTER_GAIN, ENTER_W, FAR_IN, FAR_OUT, FAR_OWN, FINAL, FIRST,
    FIRST_BIAS, FORWARD, FROM_HIGH, FROM_LOW, GRAD, HELD, HERE, HIGH, LEAVE, LEAVE_BIAS,
    LEAVE_GAIN, LEAVE_SHIFT, LEAVE_W, LINE, LINE_IN, LINE_OUT, LOW, MINE, MIX, MIXED, MIX_AT,
    MIX_GAIN, MIX_SHIFT, NEAR_IN, NEAR_OUT, OWN, OWNED, PAIR, PROJ, QKV, REMOTE, REORDER, RESULT,
    ROWS, ROWS2, ROWS_OUT, SECOND, SECOND_BIAS, SLOPE, SOURCE, STATE, SUMS, TARGET, UNIT_SUMS,
    UP, VALUE, WIDE_SUMS,
) = range(69)
COTANGENT, COSINE, SINE = 100, 101, 102
FIRST_HBM = 200
COTANGENT_HBM = FIRST_HBM + 50
(
    ACT_HBM, FACTS_HBM, HIDDEN_HBM, MOVED_HBM, ROWS2_HBM, ROWS_HBM, ROW_FACTS_HBM, SLOPE_HBM,
    VECTORS_HBM, VECTOR_HBM,
) = range(FIRST_HBM, FIRST_HBM + 10)


STRIP = 256
PARTS = 2
MESH_ID = pl.DeviceIdType.MESH


def strips(at):
    return pl.ds(pl.multiple_of(at * STRIP, STRIP), STRIP)


def partners():
    dp_at, mp_at = lax.axis_index("dp"), lax.axis_index("mp")
    core = dp_at + 1 - 2 * lax.rem(dp_at, 2)
    cross = mp_at + 2 - 4 * (mp_at // 2)
    return {
        CORE: {"dp": core},
        LINE: {"mp": mp_at + 1 - 2 * lax.rem(mp_at, 2)},
        CROSS: {"mp": cross},
        DIAGONAL: {"dp": core, "mp": cross},
        LOW: {"dp": dp_at + 2 - 4 * lax.rem(dp_at // 2, 2)},
        HIGH: {"dp": dp_at + 4 - 8 * lax.rem(dp_at // 4, 2)},
    }


def greet(names):
    barrier, devices = pltpu.get_barrier_semaphore(), partners()
    for name in names:
        pl.semaphore_signal(barrier, inc=1, device_id=devices[name], device_id_type=MESH_ID)
    return lambda: pl.semaphore_wait(barrier, len(names))


class Courier:
    def __init__(self, ref):
        self.ref, self.devices = ref, partners()
        self.remotes, self.locals = 0, 0
        self.open = {}
        self.aligned = lax.rem(lax.axis_index("dp"), 2) == lax.axis_index("mp") // 2

    def slot(self):
        self.remotes += 1
        return self.remotes - 1

    def remote(self, source, target, partner, at, received=None):
        sems = self.ref[REMOTE]
        received = at if received is None else received
        return pltpu.make_async_remote_copy(
            src_ref=source,
            dst_ref=target,
            send_sem=sems.at[0, at],
            recv_sem=sems.at[1, received],
            device_id=self.devices[partner],
            device_id_type=MESH_ID,
        )

    def send(self, source, target, partner):
        copy = self.remote(source, target, partner, self.slot())
        copy.start()
        return copy

    def near(self, source, target):
        return pltpu.make_async_copy(source, target, self.ref[HERE].at[self.locals])

    def local(self, source, target):
        copy = self.near(source, target)
        self.locals += 1
        copy.start()
        return copy

    def swap(self, source, target):
        at, copy = self.slot(), self.near(source, target)
        self.locals += 1
        away = lambda: self.remote(source, target, DIAGONAL, at)
        pl.when(self.aligned)(copy.start)
        pl.when(jnp.logical_not(self.aligned))(lambda: away().start())

        def finish():
            pl.when(self.aligned)(copy.wait)
            pl.when(jnp.logical_not(self.aligned))(lambda: away().wait())

        return finish

    def begin(self, pack, step):
        ref = self.ref
        buffer = lambda part: ref[(pack, part)]
        if step == 1:
            mine, pair = buffer(MINE), buffer(PAIR)
            first, second, copy = self.slot(), self.slot(), self.near(mine, pair.at[0])
            self.locals += 1
            across = lambda: self.remote(mine, pair.at[1], CROSS, first)
            beside = lambda: self.remote(mine, pair.at[1], CORE, first)
            over = lambda: self.remote(mine, pair.at[0], DIAGONAL, second)

            def start_aligned():
                copy.start()
                across().start()

            def start_other():
                beside().start()
                over().start()

            def wait_aligned():
                copy.wait()
                across().wait()

            def wait_other():
                beside().wait()
                over().wait()

            pl.when(self.aligned)(start_aligned)
            pl.when(jnp.logical_not(self.aligned))(start_other)

            def finish():
                pl.when(self.aligned)(wait_aligned)
                pl.when(jnp.logical_not(self.aligned))(wait_other)

        elif step > 4:
            self.finish(pack, step - 1)
            finish = self.reduce(pack, step)
        else:
            self.finish(pack, step - 1)
            if step == 4:
                depth = buffer(CORNERS).shape[1]
                block = lambda at: buffer(GRAD).at[at * depth : (at + 1) * depth]
                copies = [
                    self.send(block(6), buffer(CORNERS).at[0], HIGH),
                    self.send(block(7), buffer(CORNERS).at[1], LOW),
                ]
            elif step == 2:
                pair = buffer(PAIR)
                copies = [self.send(pair, buffer(side), side) for side in (LOW, HIGH)]
            else:
                copies = [
                    self.send(buffer(LOW).at[0], buffer(CORNER).at[0], HIGH),
                    self.send(buffer(HIGH).at[1], buffer(CORNER).at[1], LOW),
                ]

            def finish():
                for copy in copies:
                    copy.wait()

        self.open[pack, step] = finish

    def fetch(self, columns, terms):
        held = self.ref[HELD, columns]
        loads = [self.local(term, held.at[at]) for at, term in enumerate(terms)]
        for load in loads:
            load.wait()
        return lambda at: held[at].astype(F32)

    def reduce(self, pack, step):
        ref = self.ref
        buffer = lambda part: ref[pack, part]
        if step == 7:
            ends = buffer(ENDS)
            columns = ends.shape[2]
            term = self.fetch(columns, [ends.at[0], ends.at[1]])
            result = ref[RESULT, columns, pack]
            result[...] = term(0) + term(1)
            return self.local(result, buffer(RESULT)).wait
        depth, columns = buffer(GRAD).shape[0] // 8, buffer(GRAD).shape[1]
        block = lambda at: buffer(GRAD).at[at * depth : (at + 1) * depth]
        sums = ref[SUMS, pack]
        if step == 5:
            corners, from_low, from_high = buffer(CORNERS), buffer(FROM_LOW), buffer(FROM_HIGH)
            copies = [
                self.send(block(3), from_low.at[1], LOW),
                self.send(block(4), from_high.at[0], HIGH),
            ]
            term = self.fetch(columns, [block(2), block(5), corners.at[0], corners.at[1]])
            for at in range(2):
                sums[at] = (term(at) + term(2 + at)).astype(BF16)
            copies.append(self.send(sums.at[0], from_low.at[0], LOW))
            copies.append(self.send(sums.at[1], from_high.at[1], HIGH))

            def finish():
                for copy in copies:
                    copy.wait()

            return finish
        ends, sides = buffer(ENDS), (buffer(FROM_LOW), buffer(FROM_HIGH))
        term = self.fetch(
            columns, [block(0), block(1)] + [side.at[at] for side in sides for at in range(2)]
        )
        for at in range(2):
            sums[at] = (term(at) + term(2 + at) + term(4 + at)).astype(BF16)
        first, second = self.slot(), self.slot()
        copy = self.near(sums.at[0], ends.at[0])
        self.locals += 1
        beside = lambda: self.remote(sums.at[1], ends.at[0], CORE, first)
        over = lambda: self.remote(sums.at[0], ends.at[1], DIAGONAL, second)
        across = lambda: self.remote(sums.at[1], ends.at[1], CROSS, first, second)

        def start_aligned():
            copy.start()
            beside().start()

        def start_other():
            over().start()
            across().start()

        def wait_aligned():
            copy.wait()
            beside().wait_send()
            over().wait_recv()

        def wait_other():
            over().wait()
            across().wait_send()
            beside().wait_recv()

        pl.when(self.aligned)(start_aligned)
        pl.when(jnp.logical_not(self.aligned))(start_other)

        def finish():
            pl.when(self.aligned)(wait_aligned)
            pl.when(jnp.logical_not(self.aligned))(wait_other)

        return finish

    def finish(self, pack, step):
        finish = self.open.pop((pack, step), None)
        if finish is not None:
            finish()

    def finish_all(self):
        for finish in self.open.values():
            finish()
        self.open = {}


PACK_PARTS = {
    1: (PAIR,),
    2: (LOW, HIGH),
    3: (CORNER,),
    4: (CORNERS,),
    5: (FROM_LOW, FROM_HIGH),
    6: (ENDS,),
    7: (RESULT,),
}
PACK_NEEDS = {
    1: (MINE,),
    2: (PAIR,),
    3: (LOW, HIGH),
    4: (GRAD,),
    5: (GRAD, CORNERS),
    6: (GRAD, FROM_LOW, FROM_HIGH),
    7: (ENDS,),
}


def pack_buffers(jobs, packs):
    needs, makes, scratch = {}, {}, {}
    for pack, step in jobs:
        for part in PACK_NEEDS[step]:
            name = (pack, part)
            if name not in makes:
                needs[name] = packs[name]
        if step < 4:
            depth, columns = packs[(pack, MINE)].shape
        else:
            depth, columns = packs[(pack, GRAD)].shape
            depth //= 8
            scratch[HELD, columns] = pltpu.VMEM((6, depth, columns), BF16)
            if step in (5, 6):
                scratch[SUMS, pack] = pltpu.VMEM((2, depth, columns), BF16)
        for part in PACK_PARTS[step]:
            made = jax.ShapeDtypeStruct((2, depth, columns), BF16)
            if part == RESULT:
                made = jax.ShapeDtypeStruct((depth, columns), F32)
                scratch[RESULT, columns, pack] = pltpu.VMEM((depth, columns), F32)
            makes[(pack, part)] = made
    return needs, makes, scratch, 4 * len(jobs), 9 * len(jobs)


def start_kernel(jobs, names, *refs):
    ref = dict(zip(names, refs))
    greeted = greet((CORE, LINE, CROSS, DIAGONAL, LOW, HIGH))
    courier = Courier(ref)
    greeted()
    facts = courier.swap(ref[FACTS_HBM], ref[ROW_FACTS_HBM])
    vector, vectors = ref[VECTOR_HBM], ref[VECTORS_HBM]
    courier.local(vector, vectors.at[0]).wait()
    rows = None
    size = 1
    for partner in (LINE, CROSS, CORE, LOW, HIGH):
        courier.send(vectors.at[0:size], vectors.at[size : 2 * size], partner).wait()
        size *= 2
        if partner == CROSS:
            courier.begin(*jobs[0])
            rows = courier.swap(ref[HIDDEN_HBM], ref[MOVED_HBM])
    for job in jobs[1:]:
        courier.begin(*job)
    rows()
    facts()
    courier.finish_all()


def start_call(collective, hidden, facts, vector, jobs, packs):
    anywhere = pl.BlockSpec(memory_space=pl.ANY)
    needs, makes, _, remote, here = pack_buffers(jobs, packs)
    shape = jax.ShapeDtypeStruct
    inputs = {HIDDEN_HBM: hidden, FACTS_HBM: facts, VECTOR_HBM: vector, **needs}
    outputs = {
        MOVED_HBM: shape(hidden.shape, hidden.dtype),
        ROW_FACTS_HBM: shape(facts.shape, facts.dtype),
        VECTORS_HBM: shape((32, *vector.shape), vector.dtype),
        **makes,
    }
    names = (*inputs, *outputs, REMOTE, HERE)
    results = pl.pallas_call(
        functools.partial(start_kernel, jobs, names),
        name="start_exchange",
        out_shape=tuple(outputs.values()),
        in_specs=[anywhere] * len(inputs),
        out_specs=(anywhere,) * len(outputs),
        scratch_shapes=[
            pltpu.SemaphoreType.DMA((2, remote + 7)),
            pltpu.SemaphoreType.DMA((here + 3,)),
        ],
        compiler_params=pltpu.CompilerParams(collective_id=collective, has_side_effects=True),
        cost_estimate=pl.CostEstimate(flops=0, bytes_accessed=64 << 20, transcendentals=0),
    )(*inputs.values())
    results = dict(zip(outputs, results))
    packs.update({name: results[name] for name in makes})
    return results


def turned(values):
    return values.astype(F32).T


def joined(pieces, axis=0):
    return pieces[0] if len(pieces) == 1 else jnp.concatenate(pieces, axis=axis)


def chain_kernel(stages, backward, names, plan, jobs, *refs):
    ref = dict(zip(names, refs))
    enter, mix, leave = stages
    value, state, own, far_own = ref[VALUE], ref[STATE], ref[OWN], ref[FAR_OWN]
    count, width = value.shape
    step = count // PARTS
    greeted = greet(tuple(partners()) if jobs or MOVED_HBM in ref else (CORE, LINE))
    courier = Courier(ref)
    send, local = courier.send, courier.local
    core, line = CORE, LINE
    waiting = list(jobs)

    def point(at):
        while waiting and waiting[0][0] <= at:
            courier.begin(*waiting.pop(0)[1:])

    def chunk(slot, part):
        return slice(slot * count + part * step, slot * count + (part + 1) * step)

    def place(part):
        return slice(part * step, (part + 1) * step)

    made = {(pack, part): (pack, at) for _, pack, at in jobs for part in PACK_PARTS[at]}
    loads = {}

    def load(name, blocks):
        return [
            local(ref[piece].at[index, :, begin:end], ref[name].at[row : row + depth, :])
            for piece, index, row, depth, begin, end in blocks
        ]

    for name, blocks in plan:
        loads[name] = load(name, [block for block in blocks if block[0] not in made])

    def loaded(name):
        late = [block for weight, blocks in plan if weight == name for block in blocks]
        late = [block for block in late if block[0] in made]
        for block in late:
            courier.finish(*made[block[0]])
        for copy in loads[name] + load(name, late):
            copy.wait()

    if mix and backward:
        loads[SLOPE] = [local(ref[SLOPE_HBM], ref[SLOPE])]
    saves = []
    if backward:
        ref[WIDE_SUMS][...] = jnp.zeros(ref[WIDE_SUMS].shape, F32)

    def add_wide(row, sums):
        if sums.ndim == 1:
            sums = sums[None]
        ref[WIDE_SUMS][row : row + 1, :] += sums

    def product(pieces, weight, stores, transposed_source=False):
        def strip(at, carry):
            columns = strips(at)
            result = mat_turned(pieces, weight[columns, : pieces.shape[1]])
            begin = 0
            for size, store in stores:
                store(columns, result[begin : begin + size])
                begin += size
            return carry

        lax.fori_loop(0, width // STRIP, strip, 0)

    def put(target, index):
        def store(columns, result):
            target[index, :, columns] = result.astype(target.dtype)

        return store

    def scatter(prefix, source, weight):
        far_out, far_in = ref[prefix, FAR_OUT], ref[prefix, FAR_IN]
        line_out, line_in = ref[prefix, LINE_OUT], ref[prefix, LINE_IN]
        near_out, near_in = ref[prefix, NEAR_OUT], ref[prefix, NEAR_IN]

        def far(part):
            product(
                source([(2, part), (3, part)]),
                weight,
                [(step, put(far_own, part)), (step, put(far_out, part))],
            )
            return send(far_out.at[part], far_in.at[part], core)

        def pass_on(part, passing):
            passing.wait()
            line_out[part] = (far_own[part] + far_in[part].astype(F32)).astype(BF16)
            return send(line_out.at[part], line_in.at[part], line)

        def near():
            product(
                source([(1, part) for part in range(PARTS)]),
                weight,
                [(step, put(near_out, part)) for part in range(PARTS)],
            )
            return send(near_out, near_in, core)

        def mine():
            product(
                source([(0, part) for part in range(PARTS)]),
                weight,
                [(step, put(own, part)) for part in range(PARTS)],
            )

        def total(part):
            return own[part] + near_in[part].astype(F32) + line_in[part].astype(F32)

        return far, pass_on, near, mine, total

    def lower(values, gain, shift):
        if backward:
            return values.astype(BF16)
        return (normalise(values)[0] * gain[...] + shift[...]).astype(BF16)

    def begin_rows(rows, part):
        near = send(rows.at[chunk(0, part)], rows.at[chunk(1, part)], core)
        far = send(rows.at[chunk(0, part)], rows.at[chunk(2, part)], line)
        return near, far

    def forward_rows(rows, part, far):
        far.wait()
        return send(rows.at[chunk(2, part)], rows.at[chunk(3, part)], core)

    ready = None
    if enter:
        source_t = ref[SOURCE]

        def entering(pieces):
            return turned(joined([source_t[:, chunk(*piece)] for piece in pieces], 1)).astype(BF16)

        far, pass_on, near, mine, total = scatter(ENTER, entering, ref[ENTER_W])
        loaded(ENTER_W)
        greeted()
        point(0)
        if COTANGENT_HBM in ref:
            moved = courier.swap(ref[COTANGENT_HBM], ref[MOVED_HBM])
        passing = [far(part) for part in range(PARTS)]
        lines = [pass_on(part, passing[part]) for part in range(PARTS)]
        near_sum = near()
        mine()
        point(1)
        near_sum.wait()
        point(2)

        def ready(part):
            lines[part].wait()
            at = place(part)
            if backward:
                grad, gains, shifts = norm_backward(
                    ref[ENTER_AT][at, :], ref[ENTER_GAIN][...], total(part)
                )
                state[at, :] = value[at, :] + grad
                add_wide(0, gains)
                add_wide(1, shifts)
            else:
                state[at, :] = value[at, :] + (total(part) + ref[ENTER_BIAS][...])
            ref[ENTERED][at, :] = state[at, :]

    else:
        greeted()
        point(0)

        if COTANGENT in ref:
            lowered = mat(value[...].astype(BF16), ref[REORDER][...])
            ref[ROWS_OUT][...] = lowered.astype(BF16)
            moved = courier.swap(ref[ROWS_OUT], ref[MOVED_HBM])
            state[...] = mat(ref[COTANGENT][...], ref[REORDER][...])

        def ready(part):
            at = place(part)
            if COTANGENT not in ref:
                state[at, :] = value[at, :]

    if mix:
        rows, act, slope = ref[ROWS], ref[ACT], ref[SLOPE]
        first, second = ref[FIRST], ref[SECOND]
        units = first.shape[1]
        if backward:
            ref[UNIT_SUMS][...] = jnp.zeros(ref[UNIT_SUMS].shape, F32)
        begun = []
        for part in range(PARTS):
            ready(part)
            lowered = lower(
                state[place(part), :], ref.get(MIX_GAIN), ref.get(MIX_SHIFT)
            )
            rows[chunk(0, part), :] = lowered
            begun.append(begin_rows(rows, part))
            if backward:
                add_wide(2, jnp.sum(lowered.astype(F32), axis=0))

        def expand(pieces):
            taken = joined([rows[chunk(*piece), :] for piece in pieces])

            def strip(at, carry):
                columns = strips(at)
                up = mat(taken, first[:, columns])
                tilt = None
                if backward:
                    slopes = joined([slope[chunk(*piece), columns] for piece in pieces])
                    out = (up * slopes.astype(F32)).astype(BF16)
                    ref[UNIT_SUMS][:, columns] += jnp.sum(
                        out.astype(F32), axis=0, keepdims=True
                    )
                else:
                    up = up + ref[FIRST_BIAS][:, columns]
                    sigmoid = 1.0 / (1.0 + jnp.exp(-1.702 * up))
                    out = (up * sigmoid).astype(BF16)
                    tilt = (sigmoid + 1.702 * up * sigmoid * (1.0 - sigmoid)).astype(BF16)
                for index, piece in enumerate(pieces):
                    at_rows = slice(index * step, (index + 1) * step)
                    act[chunk(*piece), columns] = out[at_rows]
                    if tilt is not None:
                        slope[chunk(*piece), columns] = tilt[at_rows]
                return carry

            lax.fori_loop(0, units // STRIP, strip, 0)

        def acting(pieces):
            return joined([act[chunk(*piece), :] for piece in pieces])

        far, pass_on, near, mine, total = scatter(MIX, acting, second)
        loaded(FIRST)
        if backward:
            loaded(SLOPE)
        expand([(0, part) for part in range(PARTS)])
        for part in range(PARTS):
            begun[part][0].wait()
        point(3)
        expand([(1, part) for part in range(PARTS)])
        loaded(SECOND)
        near_sum = near()
        point(4)
        forwards = [forward_rows(rows, 0, begun[0][1])]
        mine()
        lines = []
        for part in range(PARTS):
            forwards[part].wait()
            expand([(2, part), (3, part)])
            lines.append(pass_on(part, far(part)))
            if part + 1 < PARTS:
                forwards.append(forward_rows(rows, part + 1, begun[part + 1][1]))
            point(5 + part)
        saves.append(local(rows, ref[ROWS_HBM]))
        saves.append(local(act, ref[ACT_HBM]))
        if not backward:
            saves.append(local(slope, ref[SLOPE_HBM]))
        near_sum.wait()

        def ready(part):
            lines[part].wait()
            at = place(part)
            if backward:
                grad, gains, shifts = norm_backward(
                    ref[MIX_AT][at, :], ref[MIX_GAIN][...], total(part)
                )
                state[at, :] = state[at, :] + grad
                add_wide(3, gains)
                add_wide(4, shifts)
            else:
                state[at, :] = state[at, :] + (total(part) + ref[SECOND_BIAS][...])
            ref[MIXED][at, :] = state[at, :]

    if leave:
        rows2, weight, target = ref[ROWS2], ref[LEAVE_W], ref[TARGET]
        begun = []
        for part in range(PARTS):
            ready(part)
            lowered = lower(
                state[place(part), :], ref.get(LEAVE_GAIN), ref.get(LEAVE_SHIFT)
            )
            rows2[chunk(0, part), :] = lowered
            begun.append(begin_rows(rows2, part))
            if backward:
                add_wide(5, jnp.sum(lowered.astype(F32), axis=0))

        def leaving(pieces):
            result = mat(joined([rows2[chunk(*piece), :] for piece in pieces]), weight[...])
            if not backward:
                result = result + ref[LEAVE_BIAS][...]
            result = turned(result)
            if not backward:
                cos, sin = (
                    joined([ref[name][:, chunk(*piece)] for piece in pieces], 1)
                    for name in (COSINE, SINE)
                )
                half, third = HD // 2, result.shape[0] // 3
                blocks = []
                for base in range(0, 2 * third, HD):
                    low, high = result[base : base + half], result[base + half : base + HD]
                    blocks += [low * cos - high * sin, high * cos + low * sin]
                result = jnp.concatenate(blocks + [result[2 * third :]], axis=0)
            result = result.astype(BF16)
            for index, piece in enumerate(pieces):
                target[:, chunk(*piece)] = result[:, index * step : (index + 1) * step]

        loaded(LEAVE_W)
        point(7)
        leaving([(0, part) for part in range(PARTS)])
        for part in range(PARTS):
            begun[part][0].wait()
        leaving([(1, part) for part in range(PARTS)])
        point(8)
        forwards = [forward_rows(rows2, part, begun[part][1]) for part in range(PARTS)]
        for part in range(PARTS):
            forwards[part].wait()
            leaving([(2, part), (3, part)])
        saves.append(local(rows2, ref[ROWS2_HBM]))
    else:
        for part in range(PARTS):
            ready(part)
    if REORDER in ref and COTANGENT not in ref:
        lowered = mat(state[...].astype(BF16), ref[REORDER][...]).astype(BF16)
        rows_out = ref[ROWS_OUT]
        rows_out[...] = lowered
        moved = courier.swap(rows_out, ref[MOVED_HBM])
    point(9)
    if MOVED_HBM in ref:
        moved()
    for save in saves:
        save.wait()
    courier.finish_all()


class Weight:
    def __init__(self, pack, begin, end):
        self.pack, self.begin, self.end = pack, begin, end


def chain_call(stages, backward, collective, operands, packs, jobs=()):
    enter, mix, leave = stages
    count, width = operands[VALUE].shape
    step = count // PARTS
    shape = jax.ShapeDtypeStruct
    vmem, anywhere = pl.BlockSpec(memory_space=pltpu.VMEM), pl.BlockSpec(memory_space=pl.ANY)
    outputs, scratch = {}, {}
    buffers = lambda kind: pltpu.VMEM((PARTS, step, width), kind)
    scratch[STATE] = pltpu.VMEM((count, width), F32)
    scratch[OWN] = buffers(F32)
    scratch[FAR_OWN] = buffers(F32)
    remote, here = 0, 0
    if backward:
        outputs[WIDE_SUMS] = shape((8, width), F32)
    flops = 0
    plan = []
    passed = {}
    needs, makes, job_scratch, job_remote, job_here = pack_buffers([job[1:] for job in jobs], packs)
    scratch.update(job_scratch)
    remote, here = remote + job_remote, here + job_here
    for name, value in operands.items():
        if not isinstance(value, Weight):
            passed[name] = value
            continue
        blocks, row = [], 0
        for part in (PAIR, LOW, HIGH, CORNER, ALL):
            piece = (value.pack, part)
            if piece not in packs and piece not in makes:
                continue
            if piece not in makes:
                passed[piece] = packs[piece]
            array = makes.get(piece, packs.get(piece))
            for index in range(array.shape[0]):
                blocks.append((piece, index, row, array.shape[1], value.begin, value.end))
                row += array.shape[1]
        plan.append((name, blocks))
        scratch[name] = pltpu.VMEM((width, value.end - value.begin), BF16)
        here += len(blocks)
        flops += 8 * count * width * (value.end - value.begin)
    passed.update({name: value for name, value in needs.items() if name not in passed})
    outputs.update(makes)
    for stage, prefix in ((enter, ENTER), (mix, MIX)):
        if stage:
            for name in (FAR_OUT, FAR_IN, LINE_OUT, LINE_IN, NEAR_OUT, NEAR_IN):
                scratch[prefix, name] = buffers(BF16)
            remote += 2 * PARTS + 1
    if enter:
        outputs[ENTERED] = shape((count, width), F32)
    if mix:
        units = operands[FIRST].end - operands[FIRST].begin
        scratch[ROWS] = pltpu.VMEM((4 * count, width), BF16)
        scratch[ACT] = pltpu.VMEM((4 * count, units), BF16)
        scratch[SLOPE] = pltpu.VMEM((4 * count, units), BF16)
        outputs[MIXED] = shape((count, width), F32)
        outputs[ROWS_HBM] = shape((4 * count, width), BF16)
        outputs[ACT_HBM] = shape((4 * count, units), BF16)
        if backward:
            outputs[UNIT_SUMS] = shape((1, units), F32)
        else:
            outputs[SLOPE_HBM] = shape((4 * count, units), BF16)
        remote += 3 * PARTS
        here += 3
    if leave:
        columns = leave
        scratch[ROWS2] = pltpu.VMEM((4 * count, width), BF16)
        outputs[TARGET] = shape((columns, 4 * count), BF16)
        outputs[ROWS2_HBM] = shape((4 * count, width), BF16)
        remote += 3 * PARTS
        here += 1
    if REORDER in operands or COTANGENT_HBM in operands:
        if REORDER in operands:
            scratch[ROWS_OUT] = pltpu.VMEM((count, width), BF16)
        outputs[MOVED_HBM] = shape((count, width), BF16)
        remote, here = remote + 1, here + 1
    scratch[REMOTE] = pltpu.SemaphoreType.DMA((2, remote))
    scratch[HERE] = pltpu.SemaphoreType.DMA((here,))
    names = tuple(passed) + tuple(outputs) + tuple(scratch)
    spec = lambda name: anywhere if isinstance(name, tuple) or name >= FIRST_HBM else vmem
    results = pl.pallas_call(
        functools.partial(chain_kernel, stages, backward, names, plan, jobs),
        name="chain_backward" if backward else "chain_forward",
        out_shape=tuple(outputs.values()),
        in_specs=[spec(name) for name in passed],
        out_specs=tuple(spec(name) for name in outputs),
        scratch_shapes=list(scratch.values()),
        compiler_params=pltpu.CompilerParams(
            collective_id=collective, has_side_effects=True, vmem_limit_bytes=54 << 20
        ),
        cost_estimate=pl.CostEstimate(
            flops=flops, bytes_accessed=(16 << 20) * sum(map(bool, stages)), transcendentals=0
        ),
    )(*passed.values())
    results = dict(zip(outputs, results))
    packs.update({name: results[name] for name in makes})
    return results


def make_body(dp, mp):
    assert mp == 4 and dp >= 2 and dp & (dp - 1) == 0
    count = dp * mp
    high_bits = [1 << b for b in range(1, dp.bit_length() - 1)]

    def across(value, bit):
        return lax.ppermute(value, "dp", [(i, i ^ bit) for i in range(dp)])

    def core_side(value):
        return across(value, 1)

    def line_side(value):
        return lax.ppermute(value, "mp", [(i, i ^ 1) for i in range(mp)])

    def swapped(d, m):
        return (d & ~1 | m >> 1) * mp + ((d & 1) << 1 | m & 1)

    swap_pairs = [
        (d * mp + m, swapped(d, m)) for d in range(dp) for m in range(mp) if d & 1 != m >> 1
    ]

    def swap(value):
        stays = (lax.axis_index("dp") & 1) == (lax.axis_index("mp") >> 1)
        return jnp.where(stays, value, lax.ppermute(value, ("dp", "mp"), swap_pairs))

    balanced = len(high_bits) == 2

    def gather_pair(mine):
        return swap(jnp.stack([mine, core_side(mine)]))

    def gather_sides(pair):
        for bit in high_bits:
            pair = jnp.concatenate([pair, across(pair, bit)], axis=0)
        return (pair,)

    def add(*terms):
        total = terms[0].astype(F32)
        for term in terms[1:]:
            total = total + term.astype(F32)
        return total.astype(BF16)

    def scatter_blocks(grad):
        total = grad.reshape(dp, D // dp, -1)
        for bit in high_bits[::-1]:
            half = total.shape[0] // 2
            total = add(total[:half], across(total[half:], bit))
        total = swap(total)
        return total[0].astype(F32) + core_side(total[1]).astype(F32)

    def arranged(values):
        index = lax.axis_index("dp") * mp + lax.axis_index("mp")
        at = jnp.arange(count, dtype=jnp.int32)
        order = (at[:, None] ^ index) == at[None, :]
        return dot(order.astype(F32), values, 1, 0, precision=HIGHEST)

    def gather_vectors(mine):
        values = mine[None]
        bit = 1
        while bit < count:
            if bit >= mp:
                got = across(values, bit // mp)
            else:
                got = lax.ppermute(values, "mp", [(i, i ^ bit) for i in range(mp)])
            values = jnp.concatenate([values, got], axis=0)
            bit *= 2
        return arranged(values)

    def scatter_vectors(values):
        index = lax.axis_index("dp") * mp + lax.axis_index("mp")
        bit = count // 2
        while bit:
            half = values.shape[0] // 2
            top = (index & bit) != 0
            low, high = values[:half], values[half:]
            sent = jnp.where(top, low, high)
            if bit >= mp:
                got = across(sent, bit // mp)
            else:
                got = lax.ppermute(sent, "mp", [(i, i ^ bit) for i in range(mp)])
            values = jnp.where(top, high, low) + got
            bit //= 2
        return values[0]

    def body(
        hidden_in,
        pre_gain,
        pre_bias,
        qkv_weight,
        qkv_bias,
        proj_weight,
        proj_bias,
        mid_gain,
        mid_bias,
        up_weight,
        up_bias,
        down_weight,
        down_bias,
        picture_ids,
        positions,
        pad_mask,
        cotangent,
    ):
        dp_at, mp_at = lax.axis_index("dp"), lax.axis_index("mp")
        group_at = (dp_at & ~1) | (mp_at >> 1)
        quarter_at = ((dp_at & 1) << 1) | (mp_at & 1)
        depth = D // dp
        columns = qkv_weight.shape[3]
        units = up_weight.shape[2]
        heads = columns // HD

        place = jnp.arange(D, dtype=jnp.int32)
        moved = ((place // depth) ^ group_at) * depth + place % depth
        reorder = place[:, None] == moved[None, :]
        reorder_low = reorder.astype(BF16)
        reorder_full = reorder.astype(F32)

        def turn_low(values):
            return dot(values.astype(BF16), reorder_low, 1, 0)

        qkv_width, proj_width = 3 * columns, columns
        packs = {}
        for layer in range(LAYERS):
            mine = qkv_weight[layer].transpose(1, 0, 2).reshape(depth, qkv_width)
            packs[(QKV, layer), MINE] = mine
            packs[(PROJ, layer), MINE] = proj_weight[layer].T
            packs[(UP, layer), MINE] = up_weight[layer]
            packs[(DOWN, layer), MINE] = down_weight[layer].T

        wide = (pre_gain, pre_bias, proj_bias, mid_gain, mid_bias, down_bias)
        packed = jnp.concatenate(
            [item.reshape(-1) for item in wide] + [qkv_bias.reshape(-1), up_bias.reshape(-1)]
        )
        length = picture_ids.shape[0]
        quarter = length // mp
        row_at = jnp.arange(length, dtype=jnp.int32)
        codes = jnp.where(pad_mask == 1, picture_ids, 1024 + row_at)
        row_facts = jnp.concatenate([codes[None], positions], axis=0)
        hidden = hidden_in.astype(BF16)
        jobs = {}
        if balanced:
            space = -(-packed.shape[0] // 1024) * 1024
            begun = start_call(
                3 * LAYERS + 1,
                hidden,
                jnp.pad(row_facts, ((0, 5), (0, 0))),
                jnp.pad(packed, (0, space - packed.shape[0])).reshape(-1, 128),
                (((QKV, 0), 1), ((QKV, 0), 2), ((PROJ, 0), 1), ((UP, 0), 1), ((QKV, 0), 3)),
                packs,
            )
            hidden, row_facts = begun[MOVED_HBM], begun[ROW_FACTS_HBM][:3]
            packed = arranged(begun[VECTORS_HBM].reshape(count, space))[:, : packed.shape[0]]
            schedule = {
                (LEAVE, 0): {
                    0: ((UP, 0, 2), (PROJ, 0, 2), (DOWN, 0, 1)),
                    8: ((PROJ, 0, 3),),
                },
                (FORWARD, 0): {
                    0: ((UP, 0, 3), (DOWN, 0, 2)),
                    2: ((QKV, 1, 1), (PROJ, 1, 1)),
                    3: ((DOWN, 0, 3),),
                    4: ((UP, 1, 1), (QKV, 1, 2)),
                    6: ((QKV, 1, 3), (UP, 1, 2)),
                },
                (LEAVE, 1): {
                    0: ((UP, 1, 3), (PROJ, 1, 2), (DOWN, 1, 1)),
                    8: ((PROJ, 1, 3),),
                },
                (FORWARD, 1): {0: ((DOWN, 1, 2),), 2: ((DOWN, 1, 3),)},
                (BACKWARD, 0): {
                    0: ((UP, 1, 4), (DOWN, 1, 4)),
                    1: ((UP, 1, 5),),
                    4: ((DOWN, 1, 5), (QKV, 1, 4), (PROJ, 1, 4)),
                    5: ((UP, 1, 6),),
                    8: ((DOWN, 1, 6), (QKV, 1, 5), (PROJ, 1, 5)),
                },
                (BACKWARD, FINAL): {
                    0: ((UP, 0, 4), (DOWN, 0, 4), (QKV, 1, 6), (PROJ, 1, 6)),
                    1: ((UP, 0, 5),),
                    9: (
                        *((QKV, 0, 4), (PROJ, 0, 4), (DOWN, 0, 5), (UP, 1, 7), (DOWN, 1, 7)),
                        *((UP, 0, 6), (QKV, 0, 5), (PROJ, 0, 5), (QKV, 1, 7), (PROJ, 1, 7)),
                        *((DOWN, 0, 6), (UP, 0, 7), (QKV, 0, 6), (PROJ, 0, 6)),
                        *((DOWN, 0, 7), (QKV, 0, 7), (PROJ, 0, 7)),
                    ),
                },
            }
            jobs = {
                kernel: tuple(
                    (at, (name, layer), step)
                    for at, steps in points.items()
                    for name, layer, step in steps
                )
                for kernel, points in schedule.items()
            }
        else:
            for name in list(packs):
                packs[name[0], ALL] = gather_sides(gather_pair(packs[name]))[0].reshape(1, D, -1)
            hidden, row_facts, packed = swap(hidden), swap(row_facts), gather_vectors(packed)
        hidden = turn_low(hidden)
        each = D // count
        wide_count = len(wide) * LAYERS
        split = (wide_count + 3 * LAYERS) * each
        vectors = packed[:, :split].reshape(count, -1, each).transpose(1, 0, 2).reshape(-1, D)
        wide_all = dot(vectors[:wide_count], reorder_full, 1, 0, precision=HIGHEST)
        wide_all = wide_all.reshape(len(wide), LAYERS, D)
        pre_gain_all, pre_bias_all, proj_bias_all, mid_gain_all, mid_bias_all, down_bias_all = (
            wide_all[i] for i in range(len(wide))
        )
        qkv_bias_mine = lax.dynamic_slice_in_dim(
            vectors[wide_count:], quarter_at * columns, columns, 1
        ).reshape(LAYERS, 3 * columns)
        up_all = packed[:, split:].reshape(count, LAYERS, -1).transpose(1, 0, 2)
        up_bias_mine = lax.dynamic_slice_in_dim(
            up_all.reshape(LAYERS, -1), quarter_at * units, units, 1
        )

        row_facts = jnp.concatenate(
            [
                lax.dynamic_slice_in_dim(row_facts, (quarter_at ^ which) * quarter, quarter, 1)
                for which in (0, 2, 1, 3)
            ],
            axis=1,
        )
        codes = row_facts[0]
        facts = (tile_overlap(codes), *rotary_tables(row_facts[1:]), codes[None], codes[:, None])

        row = lambda vector: vector[None]
        weights = [
            (
                Weight((QKV, layer), 0, qkv_width),
                Weight((PROJ, layer), 0, proj_width),
                Weight((UP, layer), 0, units),
                Weight((DOWN, layer), 0, units),
            )
            for layer in range(LAYERS)
        ]

        def leave_forward(layer):
            return {
                LEAVE_W: weights[layer][0],
                LEAVE_GAIN: row(pre_gain_all[layer]),
                LEAVE_SHIFT: row(pre_bias_all[layer]),
                LEAVE_BIAS: row(qkv_bias_mine[layer]),
                COSINE: facts[1],
                SINE: facts[2],
            }

        def call_leave(layer, value):
            return chain_call(
                (False, False, qkv_width),
                False,
                layer,
                {VALUE: value, **leave_forward(layer)},
                packs,
                jobs.get((LEAVE, layer), ()),
            )

        def call_forward(layer, value, mixed, more):
            return chain_call(
                (True, True, False),
                False,
                LAYERS + layer,
                {
                    VALUE: value,
                    SOURCE: mixed,
                    ENTER_W: weights[layer][1],
                    ENTER_BIAS: row(proj_bias_all[layer]),
                    FIRST: weights[layer][2],
                    SECOND: weights[layer][3],
                    FIRST_BIAS: row(up_bias_mine[layer]),
                    SECOND_BIAS: row(down_bias_all[layer]),
                    MIX_GAIN: row(mid_gain_all[layer]),
                    MIX_SHIFT: row(mid_bias_all[layer]),
                    **more,
                },
                packs,
                jobs.get((FORWARD, layer), ()),
            )

        def call_backward(layer, value, entering, middle, slope, more):
            return chain_call(
                (bool(entering), True, proj_width),
                True,
                2 * LAYERS + layer,
                {
                    VALUE: value,
                    **entering,
                    **more,
                    FIRST: weights[layer][3],
                    SECOND: weights[layer][2],
                    SLOPE_HBM: slope,
                    MIX_AT: middle,
                    MIX_GAIN: row(mid_gain_all[layer]),
                    LEAVE_W: weights[layer][1],
                },
                packs,
                jobs.get((BACKWARD, layer), ()),
            )

        def entering(layer, grad_linear, start):
            return {
                SOURCE: grad_linear,
                ENTER_W: weights[layer][0],
                ENTER_AT: start,
                ENTER_GAIN: row(pre_gain_all[layer]),
            }

        leave0 = call_leave(0, hidden)
        qkv0 = leave0[TARGET]
        mixed0, log_sum0 = attend_forward(qkv0, facts)
        state0 = call_forward(0, hidden, mixed0, {})
        start1 = state0[MIXED]
        leave1 = call_leave(1, start1)
        qkv1 = leave1[TARGET]
        mixed1, log_sum1 = attend_forward(qkv1, facts)
        cotangent = cotangent.astype(BF16)
        if balanced:
            state1 = call_forward(1, start1, mixed1, {COTANGENT_HBM: cotangent})
            back1 = call_backward(
                1,
                state1[MIXED],
                {},
                state1[ENTERED],
                state1[SLOPE_HBM],
                {COTANGENT: state1[MOVED_HBM], REORDER: reorder_low},
            )
            out_hidden = back1[MOVED_HBM]
        else:
            state1 = call_forward(1, start1, mixed1, {})
            out_hidden = swap(turn_low(state1[MIXED]).astype(BF16))
            gradient = turn_low(swap(cotangent))
            back1 = call_backward(1, gradient, {}, state1[ENTERED], state1[SLOPE_HBM], {})
        packs[(UP, 1), GRAD] = dot(state1[ROWS_HBM], back1[ACT_HBM], 0, 0, BF16)
        packs[(DOWN, 1), GRAD] = dot(back1[ROWS_HBM], state1[ACT_HBM], 0, 0, BF16)
        linear1 = attend_backward(qkv1, mixed1, back1[TARGET], log_sum1, facts)
        packs[(QKV, 1), GRAD] = dot(leave1[ROWS2_HBM], linear1, 0, 1, BF16)
        packs[(PROJ, 1), GRAD] = dot(back1[ROWS2_HBM], mixed1, 0, 1, BF16)
        back0 = call_backward(
            0,
            back1[MIXED],
            entering(1, linear1, start1),
            state0[ENTERED],
            state0[SLOPE_HBM],
            {},
        )
        packs[(UP, 0), GRAD] = dot(state0[ROWS_HBM], back0[ACT_HBM], 0, 0, BF16)
        packs[(DOWN, 0), GRAD] = dot(back0[ROWS_HBM], state0[ACT_HBM], 0, 0, BF16)
        linear0 = attend_backward(qkv0, mixed0, back0[TARGET], log_sum0, facts)
        packs[(QKV, 0), GRAD] = dot(leave0[ROWS2_HBM], linear0, 0, 1, BF16)
        packs[(PROJ, 0), GRAD] = dot(back0[ROWS2_HBM], mixed0, 0, 1, BF16)
        final = chain_call(
            (True, False, False),
            True,
            3 * LAYERS,
            {
                VALUE: back0[MIXED],
                **entering(0, linear0, hidden),
                **({REORDER: reorder_low} if balanced else {}),
            },
            packs,
            jobs.get((BACKWARD, FINAL), ()),
        )
        if balanced:
            grad_hidden = final[MOVED_HBM].astype(F32)
        else:
            grad_hidden = swap(turn_low(final[ENTERED]).astype(BF16)).astype(F32)
            for name in list(packs):
                if name[1] == GRAD:
                    packs[name[0], RESULT] = scatter_blocks(packs[name])
        out_hidden = out_hidden.astype(F32)
        grads, parts = [], []
        for layer, back, linear in ((0, back0, linear0), (1, back1, linear1)):
            result = lambda which: packs[(which, layer), RESULT]
            grads.append(
                (
                    result(QKV).reshape(depth, 3, columns).transpose(1, 0, 2),
                    result(PROJ).T,
                    result(UP),
                    result(DOWN).T,
                )
            )
            qkv_bias_part = jnp.sum(linear.astype(F32), axis=1)
            parts.append((qkv_bias_part.reshape(3, columns), back[UNIT_SUMS][0]))
        sums = [back1[WIDE_SUMS], back0[WIDE_SUMS], final[WIDE_SUMS]]

        stacked = jnp.stack(
            [
                sums[LAYERS - layer - which][at]
                for which, at in ((0, 0), (0, 1), (1, 5), (1, 3), (1, 4), (1, 2))
                for layer in range(LAYERS)
            ]
        )
        stacked = dot(stacked, reorder_full, 1, 0, precision=HIGHEST)
        qkv_padded = lax.dynamic_update_slice_in_dim(
            jnp.zeros((LAYERS * 3, D), F32),
            jnp.concatenate([part[0] for part in parts], axis=0),
            quarter_at * columns,
            1,
        )
        up_padded = lax.dynamic_update_slice_in_dim(
            jnp.zeros((LAYERS, units * mp), F32),
            jnp.stack([part[1] for part in parts]),
            quarter_at * units,
            1,
        )
        by_owner = jnp.concatenate([stacked, qkv_padded], axis=0).reshape(-1, count, each)
        by_owner = jnp.concatenate(
            [
                by_owner.transpose(1, 0, 2).reshape(count, -1),
                up_padded.reshape(LAYERS, count, -1).transpose(1, 0, 2).reshape(count, -1),
            ],
            axis=1,
        )
        mine = scatter_vectors(by_owner)
        wide_grads = mine[: wide_count * each].reshape(len(wide), LAYERS, each)
        qkv_bias_grad = mine[wide_count * each : split].reshape(LAYERS, 3, each)
        up_bias_grad = mine[split:].reshape(LAYERS, -1)
        matrices = [jnp.stack([entry[i] for entry in grads]) for i in range(4)]
        return (
            out_hidden,
            grad_hidden,
            wide_grads[0],
            wide_grads[1],
            matrices[0],
            qkv_bias_grad,
            matrices[1],
            wide_grads[2],
            wide_grads[3],
            wide_grads[4],
            matrices[2],
            up_bias_grad,
            matrices[3],
            wide_grads[5],
        )

    return body


def solution(mesh):
    rows = P(("dp", "mp"), None)
    vector = P(None, ("dp", "mp"))
    vectors = P(None, None, ("dp", "mp"))
    qkv = P(None, None, "dp", "mp")
    tall = P(None, "mp", "dp")
    broad = P(None, "dp", "mp")
    return jax.shard_map(
        make_body(mesh.shape["dp"], mesh.shape["mp"]),
        mesh=mesh,
        in_specs=(
            rows,
            vector,
            vector,
            qkv,
            vectors,
            tall,
            vector,
            vector,
            vector,
            broad,
            vector,
            tall,
            vector,
            P("dp"),
            P(None, "dp"),
            P("dp"),
            rows,
        ),
        out_specs=(
            rows,
            rows,
            vector,
            vector,
            qkv,
            vectors,
            tall,
            vector,
            vector,
            vector,
            broad,
            vector,
            tall,
            vector,
        ),
        check_vma=False,
    )
```

```python
import functools

import jax
import jax.numpy as jnp
from jax import lax
from jax.experimental import pallas as pl
from jax.experimental.layout import Layout, with_layout_constraint
from jax.experimental.pallas import tpu as pltpu
from jax.sharding import PartitionSpec as P

D = 1280
HD = 80
LAYERS = 2
EPSILON = 1e-06
AXES = ("dp", "mp")
F32 = jnp.float32
BF16 = jnp.bfloat16
HIGHEST = lax.Precision.HIGHEST


def normalise(values):
    centre = values - jnp.mean(values, axis=-1, keepdims=True)
    spread = jnp.mean(centre * centre, axis=-1, keepdims=True)
    scale = lax.rsqrt(spread + EPSILON)
    return centre * scale, scale


def norm_backward(values, gain, grad):
    normed, scale = normalise(values)
    inner = grad * gain
    mean_inner = jnp.mean(inner, axis=-1, keepdims=True)
    mean_cross = jnp.mean(inner * normed, axis=-1, keepdims=True)
    grad_values = scale * (inner - mean_inner - normed * mean_cross)
    return grad_values, jnp.sum(grad * normed, axis=0), jnp.sum(grad, axis=0)


def dot(left, right, left_dim, right_dim, kind=F32, precision=None):
    return lax.dot_general(
        left,
        right,
        (((left_dim,), (right_dim,)), ((), ())),
        preferred_element_type=F32,
        precision=precision,
    ).astype(kind)


def grad_dot(left, right, left_dim, right_dim):
    return with_layout_constraint(dot(left, right, left_dim, right_dim, BF16), Layout((0, 1)))


def rotary_tables(coords):
    quarter = HD // 4
    powers = jnp.arange(quarter, dtype=F32) * (4.0 / HD)
    inverse = 10000.0 ** (-powers)
    height_angle = inverse[:, None] * coords[0].astype(F32)[None, :]
    width_angle = inverse[:, None] * coords[1].astype(F32)[None, :]
    angles = jnp.concatenate([height_angle, width_angle], axis=0)
    return (jnp.cos(angles), jnp.sin(angles))


TILE = 256
MASKED = -1e30
LOG2E = 1.4426950408889634
SCORE_SCALE = HD**-0.5 * LOG2E


def mat(left, right):
    return lax.dot_general(left, right, (((1,), (0,)), ((), ())), preferred_element_type=F32)


def mat_turned(left, right):
    return lax.dot_general(left, right, (((1,), (1,)), ((), ())), preferred_element_type=F32)


def tile_bias(code_col, code_row, keys, queries):
    same = code_col[keys, :] == code_row[:, queries]
    return jnp.where(same, 0.0, MASKED)


def tiles(at):
    return pl.ds(pl.multiple_of(at * TILE, TILE), TILE)


def forward_kernel(active, qkv, code_row, code_col, mixed, log_sum, k_rows, top, total, acc):
    heads, length = k_rows.shape[0], k_rows.shape[1]
    blocks = length // TILE
    for head in range(heads):
        base = (heads + head) * HD
        k_rows[head] = turned(qkv[base : base + HD, :]).astype(BF16)

    def query_block(q_at, carry):
        queries = tiles(q_at)
        top[...] = jnp.full(top.shape, MASKED, F32)
        total[...] = jnp.zeros(total.shape, F32)
        acc[...] = jnp.zeros(acc.shape, F32)

        def key_block(k_at, carry):
            @pl.when(active[q_at * blocks + k_at] != 0)
            def _():
                keys = tiles(k_at)
                bias = tile_bias(code_col, code_row, keys, queries)
                for head in range(heads):
                    q_base, v_base = head * HD, (2 * heads + head) * HD
                    scores = mat(k_rows[head, keys, :], qkv[q_base : q_base + HD, queries]) + bias
                    old = top[head]
                    new = jnp.maximum(old, jnp.max(scores, axis=0, keepdims=True))
                    chance = jnp.exp2((scores - new) * SCORE_SCALE)
                    fade = jnp.exp2((old - new) * SCORE_SCALE)
                    top[head] = new
                    total[head] = total[head] * fade + jnp.sum(chance, axis=0, keepdims=True)
                    acc[head] = acc[head] * fade + mat(
                        qkv[v_base : v_base + HD, keys], chance.astype(BF16)
                    )

            return carry

        lax.fori_loop(0, blocks, key_block, 0)
        for head in range(heads):
            mixed[head * HD : (head + 1) * HD, queries] = (acc[head] / total[head]).astype(BF16)
            log_sum[head, :, queries] = top[head] * SCORE_SCALE + jnp.log2(total[head])
        return carry

    lax.fori_loop(0, blocks, query_block, 0)


def backward_kernel(active, qkv, mixed, grad_mixed, log_sum, cosine, sine, code_row, code_col, out, k_rows, v_rows, centre, grad_q, grad_k, grad_v):
    heads, length = k_rows.shape[0], k_rows.shape[1]
    blocks = length // TILE
    for head in range(heads):
        k_base, v_base = (heads + head) * HD, (2 * heads + head) * HD
        k_rows[head] = qkv[k_base : k_base + HD, :].astype(F32).T.astype(BF16)
        v_rows[head] = qkv[v_base : v_base + HD, :].astype(F32).T.astype(BF16)
        rows = slice(head * HD, (head + 1) * HD)
        centre[head] = jnp.sum(
            grad_mixed[rows, :].astype(F32) * mixed[rows, :].astype(F32), axis=0, keepdims=True
        )
    grad_q[...] = jnp.zeros(grad_q.shape, F32)
    grad_k[...] = jnp.zeros(grad_k.shape, F32)
    grad_v[...] = jnp.zeros(grad_v.shape, F32)

    def query_block(q_at, carry):
        queries = tiles(q_at)

        def key_block(k_at, carry):
            @pl.when(active[q_at * blocks + k_at] != 0)
            def _():
                keys = tiles(k_at)
                bias = tile_bias(code_col, code_row, keys, queries)
                for head in range(heads):
                    rows = slice(head * HD, (head + 1) * HD)
                    k_base = (heads + head) * HD
                    scores = mat(k_rows[head, keys, :], qkv[rows, queries]) + bias
                    chance = jnp.exp2(scores * SCORE_SCALE - log_sum[head, :, queries])
                    grad_chance = mat(v_rows[head, keys, :], grad_mixed[rows, queries])
                    grad_score = (chance * (grad_chance - centre[head, :, queries])).astype(BF16)
                    grad_v[head, :, keys] += mat_turned(grad_mixed[rows, queries], chance.astype(BF16))
                    grad_k[head, :, keys] += mat_turned(qkv[rows, queries], grad_score)
                    grad_q[head, :, queries] += mat(qkv[k_base : k_base + HD, keys], grad_score)

            return carry

        return lax.fori_loop(0, blocks, key_block, carry)

    lax.fori_loop(0, blocks, query_block, 0)
    half = HD // 2
    scale = HD**-0.5
    cos, sin = cosine[...] * scale, sine[...] * scale
    for head in range(heads):
        for which, grad in ((0, grad_q), (1, grad_k)):
            base = (which * heads + head) * HD
            low, high = grad[head, :half, :], grad[head, half:, :]
            turned = jnp.concatenate([low * cos + high * sin, high * cos - low * sin], axis=0)
            out[base : base + HD, :] = turned.astype(BF16)
        base = (2 * heads + head) * HD
        out[base : base + HD, :] = grad_v[head].astype(BF16)


def whole(count):
    return [pl.BlockSpec(memory_space=pltpu.VMEM)] * count


def attend_forward(qkv, facts):
    active, _, _, code_row, code_col = facts
    width, length = qkv.shape
    heads = width // (3 * HD)
    return pl.pallas_call(
        forward_kernel,
        name="attend_forward",
        out_shape=(
            jax.ShapeDtypeStruct((heads * HD, length), BF16),
            jax.ShapeDtypeStruct((heads, 1, length), F32),
        ),
        in_specs=[pl.BlockSpec(memory_space=pltpu.SMEM)] + whole(3),
        out_specs=tuple(whole(2)),
        scratch_shapes=[
            pltpu.VMEM((heads, length, HD), BF16),
            pltpu.VMEM((heads, 1, TILE), F32),
            pltpu.VMEM((heads, 1, TILE), F32),
            pltpu.VMEM((heads, HD, TILE), F32),
        ],
        compiler_params=pltpu.CompilerParams(vmem_limit_bytes=40 << 20),
        cost_estimate=pl.CostEstimate(
            flops=heads * length * length * HD * 4,
            bytes_accessed=4 << 20,
            transcendentals=heads * length * length,
        ),
    )(active, qkv, code_row, code_col)


def attend_backward(qkv, mixed, grad_mixed, log_sum, facts):
    active, cosine, sine, code_row, code_col = facts
    width, length = qkv.shape
    heads = width // (3 * HD)
    return pl.pallas_call(
        backward_kernel,
        name="attend_backward",
        out_shape=jax.ShapeDtypeStruct((width, length), BF16),
        in_specs=[pl.BlockSpec(memory_space=pltpu.SMEM)] + whole(8),
        out_specs=pl.BlockSpec(memory_space=pltpu.VMEM),
        scratch_shapes=[
            pltpu.VMEM((heads, length, HD), BF16),
            pltpu.VMEM((heads, length, HD), BF16),
            pltpu.VMEM((heads, 1, length), F32),
            pltpu.VMEM((heads, HD, length), F32),
            pltpu.VMEM((heads, HD, length), F32),
            pltpu.VMEM((heads, HD, length), F32),
        ],
        compiler_params=pltpu.CompilerParams(vmem_limit_bytes=40 << 20),
        cost_estimate=pl.CostEstimate(
            flops=heads * length * length * HD * 10, bytes_accessed=10 << 20, transcendentals=heads * length * length
        ),
    )(active, qkv, mixed, grad_mixed, log_sum, cosine, sine, code_row, code_col)


def tile_overlap(codes):
    blocks = codes.reshape(-1, TILE)
    least, most = jnp.min(blocks, axis=1), jnp.max(blocks, axis=1)
    meet = (least[:, None] <= most[None, :]) & (least[None, :] <= most[:, None])
    return meet.astype(jnp.int32).reshape(-1)


(
    ACT, ALL, ATTN, BACKWARD, CORE, CORNER, CORNERS, CROSS, DIAGONAL, DOWN, ENDS, ENTER, ENTERED,
    ENTER_AT, ENTER_BIAS, ENTER_GAIN, ENTER_W, FAR_IN, FAR_OUT, FAR_OWN, FINAL, FIRST,
    FIRST_BIAS, FORWARD, FROM_HIGH, FROM_LOW, GRAD, HELD, HERE, HIGH, LEAVE, LEAVE_BIAS,
    LEAVE_GAIN, LEAVE_SHIFT, LEAVE_W, LINE, LINE_IN, LINE_OUT, LOW, MINE, MIX, MIXED, MIX_AT,
    MIX_GAIN, MIX_SHIFT, NEAR_IN, NEAR_OUT, OWN, OWNED, PAIR, PROJ, QKV, REMOTE, REORDER, RESULT,
    ROWS, ROWS2, ROWS_OUT, SECOND, SECOND_BIAS, SLOPE, SOURCE, STATE, SUMS, TARGET, UNIT_SUMS,
    UP, VALUE, WIDE_SUMS,
) = range(69)
ONE, OTHER = 103, 104
COTANGENT, COSINE, SINE = 100, 101, 102
FIRST_HBM = 200
COTANGENT_HBM = FIRST_HBM + 50
(
    ACT_HBM, FACTS_HBM, HIDDEN_HBM, MOVED_HBM, ROWS2_HBM, ROWS_HBM, ROW_FACTS_HBM, SLOPE_HBM,
    VECTORS_HBM, VECTOR_HBM,
) = range(FIRST_HBM, FIRST_HBM + 10)


STRIP = 256
PARTS = 2
MESH_ID = pl.DeviceIdType.MESH


def strips(at):
    return pl.ds(pl.multiple_of(at * STRIP, STRIP), STRIP)


def partners():
    dp_at, mp_at = lax.axis_index("dp"), lax.axis_index("mp")
    core = dp_at + 1 - 2 * lax.rem(dp_at, 2)
    cross = mp_at + 2 - 4 * (mp_at // 2)
    return {
        CORE: {"dp": core},
        LINE: {"mp": mp_at + 1 - 2 * lax.rem(mp_at, 2)},
        CROSS: {"mp": cross},
        DIAGONAL: {"dp": core, "mp": cross},
        LOW: {"dp": dp_at + 2 - 4 * lax.rem(dp_at // 2, 2)},
        HIGH: {"dp": dp_at + 4 - 8 * lax.rem(dp_at // 4, 2)},
    }


def greet(names):
    barrier, devices = pltpu.get_barrier_semaphore(), partners()
    for name in names:
        pl.semaphore_signal(barrier, inc=1, device_id=devices[name], device_id_type=MESH_ID)
    return lambda: pl.semaphore_wait(barrier, len(names))


class Courier:
    def __init__(self, ref):
        self.ref, self.devices = ref, partners()
        self.remotes, self.locals = 0, 0
        self.open = {}
        self.aligned = lax.rem(lax.axis_index("dp"), 2) == lax.axis_index("mp") // 2

    def slot(self):
        self.remotes += 1
        return self.remotes - 1

    def remote(self, source, target, partner, at, received=None):
        sems = self.ref[REMOTE]
        received = at if received is None else received
        return pltpu.make_async_remote_copy(
            src_ref=source,
            dst_ref=target,
            send_sem=sems.at[0, at],
            recv_sem=sems.at[1, received],
            device_id=self.devices[partner],
            device_id_type=MESH_ID,
        )

    def send(self, source, target, partner):
        copy = self.remote(source, target, partner, self.slot())
        copy.start()
        return copy

    def near(self, source, target):
        return pltpu.make_async_copy(source, target, self.ref[HERE].at[self.locals])

    def local(self, source, target):
        copy = self.near(source, target)
        self.locals += 1
        copy.start()
        return copy

    def swap(self, source, target):
        at, copy = self.slot(), self.near(source, target)
        self.locals += 1
        away = lambda: self.remote(source, target, DIAGONAL, at)
        pl.when(self.aligned)(copy.start)
        pl.when(jnp.logical_not(self.aligned))(lambda: away().start())

        def finish():
            pl.when(self.aligned)(copy.wait)
            pl.when(jnp.logical_not(self.aligned))(lambda: away().wait())

        return finish

    def begin(self, pack, step):
        ref = self.ref
        buffer = lambda part: ref[(pack, part)]
        if step == 1:
            mine, pair = buffer(MINE), buffer(PAIR)
            first, second, copy = self.slot(), self.slot(), self.near(mine, pair.at[0])
            self.locals += 1
            across = lambda: self.remote(mine, pair.at[1], CROSS, first)
            beside = lambda: self.remote(mine, pair.at[1], CORE, first)
            over = lambda: self.remote(mine, pair.at[0], DIAGONAL, second)

            def start_aligned():
                copy.start()
                across().start()

            def start_other():
                beside().start()
                over().start()

            def wait_aligned():
                copy.wait()
                across().wait()

            def wait_other():
                beside().wait()
                over().wait()

            pl.when(self.aligned)(start_aligned)
            pl.when(jnp.logical_not(self.aligned))(start_other)

            def finish():
                pl.when(self.aligned)(wait_aligned)
                pl.when(jnp.logical_not(self.aligned))(wait_other)

        elif step > 4:
            self.finish(pack, step - 1)
            finish = self.reduce(pack, step)
        else:
            self.finish(pack, step - 1)
            if step == 4:
                depth = buffer(CORNERS).shape[1]
                block = lambda at: buffer(GRAD).at[at * depth : (at + 1) * depth]
                copies = [
                    self.send(block(6), buffer(CORNERS).at[0], HIGH),
                    self.send(block(7), buffer(CORNERS).at[1], LOW),
                ]
            elif step == 2:
                pair = buffer(PAIR)
                copies = [self.send(pair, buffer(side), side) for side in (LOW, HIGH)]
            else:
                copies = [
                    self.send(buffer(LOW).at[0], buffer(CORNER).at[0], HIGH),
                    self.send(buffer(HIGH).at[1], buffer(CORNER).at[1], LOW),
                ]

            def finish():
                for copy in copies:
                    copy.wait()

        self.open[pack, step] = finish

    def fetch(self, columns, terms):
        held = self.ref[HELD, columns]
        loads = [self.local(term, held.at[at]) for at, term in enumerate(terms)]
        for load in loads:
            load.wait()
        return lambda at: held[at].astype(F32)

    def reduce(self, pack, step):
        ref = self.ref
        buffer = lambda part: ref[pack, part]
        if step == 7:
            ends = buffer(ENDS)
            columns = ends.shape[2]
            term = self.fetch(columns, [ends.at[0], ends.at[1]])
            result = ref[RESULT, columns, pack]
            result[...] = term(0) + term(1)
            return self.local(result, buffer(RESULT)).wait
        depth, columns = buffer(GRAD).shape[0] // 8, buffer(GRAD).shape[1]
        block = lambda at: buffer(GRAD).at[at * depth : (at + 1) * depth]
        sums = ref[SUMS, pack]
        if step == 5:
            from_low, from_high = buffer(FROM_LOW), buffer(FROM_HIGH)
            corners = [buffer(CORNERS).at[at] for at in range(2)]
            copies = [
                self.send(block(3), from_low.at[1], LOW),
                self.send(block(4), from_high.at[0], HIGH),
            ]
            term = self.fetch(columns, [block(2), block(5), *corners])
            for at in range(2):
                sums[at] = (term(at) + term(2 + at)).astype(BF16)
            copies.append(self.send(sums.at[0], from_low.at[0], LOW))
            copies.append(self.send(sums.at[1], from_high.at[1], HIGH))

            def finish():
                for copy in copies:
                    copy.wait()

            return finish
        ends, sides = buffer(ENDS), (buffer(FROM_LOW), buffer(FROM_HIGH))
        term = self.fetch(
            columns, [block(0), block(1)] + [side.at[at] for side in sides for at in range(2)]
        )
        for at in range(2):
            sums[at] = (term(at) + term(2 + at) + term(4 + at)).astype(BF16)
        first, second = self.slot(), self.slot()
        copy = self.near(sums.at[0], ends.at[0])
        self.locals += 1
        beside = lambda: self.remote(sums.at[1], ends.at[0], CORE, first)
        over = lambda: self.remote(sums.at[0], ends.at[1], DIAGONAL, second)
        across = lambda: self.remote(sums.at[1], ends.at[1], CROSS, first, second)

        def start_aligned():
            copy.start()
            beside().start()

        def start_other():
            over().start()
            across().start()

        def wait_aligned():
            copy.wait()
            beside().wait_send()
            over().wait_recv()

        def wait_other():
            over().wait()
            across().wait_send()
            beside().wait_recv()

        pl.when(self.aligned)(start_aligned)
        pl.when(jnp.logical_not(self.aligned))(start_other)

        def finish():
            pl.when(self.aligned)(wait_aligned)
            pl.when(jnp.logical_not(self.aligned))(wait_other)

        return finish

    def finish(self, pack, step):
        finish = self.open.pop((pack, step), None)
        if finish is not None:
            finish()

    def finish_all(self):
        for finish in self.open.values():
            finish()
        self.open = {}


PACK_PARTS = {
    1: (PAIR,),
    2: (LOW, HIGH),
    3: (CORNER,),
    4: (CORNERS,),
    5: (FROM_LOW, FROM_HIGH),
    6: (ENDS,),
    7: (RESULT,),
}
PACK_NEEDS = {
    1: (MINE,),
    2: (PAIR,),
    3: (LOW, HIGH),
    4: (GRAD,),
    5: (GRAD, CORNERS),
    6: (GRAD, FROM_LOW, FROM_HIGH),
    7: (ENDS,),
}


def pack_buffers(jobs, packs):
    needs, makes, scratch = {}, {}, {}
    for pack, step in jobs:
        for part in PACK_NEEDS[step]:
            if (pack, part) not in makes:
                needs[pack, part] = packs[pack, part]
        if step < 4:
            depth, columns = packs[(pack, MINE)].shape
        else:
            depth, columns = packs[(pack, GRAD)].shape
            depth //= 8
            scratch[HELD, columns] = pltpu.VMEM((6, depth, columns), BF16)
            if step in (5, 6):
                scratch[SUMS, pack] = pltpu.VMEM((2, depth, columns), BF16)
        for part in PACK_PARTS[step]:
            made = jax.ShapeDtypeStruct((2, depth, columns), BF16)
            if part == RESULT:
                made = jax.ShapeDtypeStruct((depth, columns), F32)
                scratch[RESULT, columns, pack] = pltpu.VMEM((depth, columns), F32)
            makes[(pack, part)] = made
    return needs, makes, scratch, 4 * len(jobs), 9 * len(jobs)


def start_kernel(jobs, names, *refs):
    ref = dict(zip(names, refs))
    greeted = greet((CORE, LINE, CROSS, DIAGONAL, LOW, HIGH))
    courier = Courier(ref)
    greeted()
    facts = courier.swap(ref[FACTS_HBM], ref[ROW_FACTS_HBM])
    vector, vectors = ref[VECTOR_HBM], ref[VECTORS_HBM]
    courier.local(vector, vectors.at[0]).wait()
    rows = None
    size = 1
    for partner in (LINE, CROSS, CORE, LOW, HIGH):
        courier.send(vectors.at[0:size], vectors.at[size : 2 * size], partner).wait()
        size *= 2
        if partner == CROSS:
            courier.begin(*jobs[0])
            rows = courier.swap(ref[HIDDEN_HBM], ref[MOVED_HBM])
    for job in jobs[1:]:
        courier.begin(*job)
    rows()
    facts()
    courier.finish_all()


def start_call(collective, hidden, facts, vector, jobs, packs):
    anywhere = pl.BlockSpec(memory_space=pl.ANY)
    needs, makes, _, remote, here = pack_buffers(jobs, packs)
    shape = jax.ShapeDtypeStruct
    inputs = {HIDDEN_HBM: hidden, FACTS_HBM: facts, VECTOR_HBM: vector, **needs}
    outputs = {
        MOVED_HBM: shape(hidden.shape, hidden.dtype),
        ROW_FACTS_HBM: shape(facts.shape, facts.dtype),
        VECTORS_HBM: shape((32, *vector.shape), vector.dtype),
        **makes,
    }
    names = (*inputs, *outputs, REMOTE, HERE)
    results = pl.pallas_call(
        functools.partial(start_kernel, jobs, names),
        name="start_exchange",
        out_shape=tuple(outputs.values()),
        in_specs=[anywhere] * len(inputs),
        out_specs=(anywhere,) * len(outputs),
        scratch_shapes=[
            pltpu.SemaphoreType.DMA((2, remote + 7)),
            pltpu.SemaphoreType.DMA((here + 3,)),
        ],
        compiler_params=pltpu.CompilerParams(collective_id=collective, has_side_effects=True),
        cost_estimate=pl.CostEstimate(flops=0, bytes_accessed=64 << 20, transcendentals=0),
    )(*inputs.values())
    results = dict(zip(outputs, results))
    packs.update({name: results[name] for name in makes})
    return results


def turned(values):
    return values.astype(F32).T


def joined(pieces, axis=0):
    return pieces[0] if len(pieces) == 1 else jnp.concatenate(pieces, axis=axis)


def chain_kernel(stages, backward, names, plan, jobs, *refs):
    ref = dict(zip(names, refs))
    enter, mix, leave = stages
    value, state, own, far_own = ref[VALUE], ref[STATE], ref[OWN], ref[FAR_OWN]
    count, width = value.shape
    step = count // PARTS
    greeted = greet(tuple(partners()) if jobs or MOVED_HBM in ref else (CORE, LINE))
    courier = Courier(ref)
    send, local = courier.send, courier.local
    core, line = CORE, LINE
    waiting = list(jobs)

    def point(at):
        while waiting and waiting[0][0] <= at:
            courier.begin(*waiting.pop(0)[1:])

    def chunk(slot, part):
        return slice(slot * count + part * step, slot * count + (part + 1) * step)

    def place(part):
        return slice(part * step, (part + 1) * step)

    made = {(pack, part): (pack, at) for _, pack, at in jobs for part in PACK_PARTS[at]}
    loads = {}

    def load(name, blocks):
        return [
            local(ref[piece].at[index, :, begin:end], ref[name].at[row : row + depth, :])
            for piece, index, row, depth, begin, end in blocks
        ]

    for name, blocks in plan:
        loads[name] = load(name, [block for block in blocks if block[0] not in made])

    def loaded(name):
        late = [block for weight, blocks in plan if weight == name for block in blocks]
        late = [block for block in late if block[0] in made]
        for block in late:
            courier.finish(*made[block[0]])
        for copy in loads[name] + load(name, late):
            copy.wait()

    if mix and backward:
        loads[SLOPE] = [local(ref[SLOPE_HBM], ref[SLOPE])]
    saves = []
    if backward:
        ref[WIDE_SUMS][...] = jnp.zeros(ref[WIDE_SUMS].shape, F32)

    def add_wide(row, sums):
        if sums.ndim == 1:
            sums = sums[None]
        ref[WIDE_SUMS][row : row + 1, :] += sums

    def product(pieces, weight, stores, transposed_source=False):
        def strip(at, carry):
            columns = strips(at)
            result = mat_turned(pieces, weight[columns, : pieces.shape[1]])
            begin = 0
            for size, store in stores:
                store(columns, result[begin : begin + size])
                begin += size
            return carry

        lax.fori_loop(0, width // STRIP, strip, 0)

    def put(target, index):
        def store(columns, result):
            target[index, :, columns] = result.astype(target.dtype)

        return store

    def scatter(prefix, source, weight):
        far_out, far_in = ref[prefix, FAR_OUT], ref[prefix, FAR_IN]
        line_out, line_in = ref[prefix, LINE_OUT], ref[prefix, LINE_IN]
        near_out, near_in = ref[prefix, NEAR_OUT], ref[prefix, NEAR_IN]

        def far(part):
            product(
                source([(2, part), (3, part)]),
                weight,
                [(step, put(far_own, part)), (step, put(far_out, part))],
            )
            return send(far_out.at[part], far_in.at[part], core)

        def pass_on(part, passing):
            passing.wait()
            line_out[part] = (far_own[part] + far_in[part].astype(F32)).astype(BF16)
            return send(line_out.at[part], line_in.at[part], line)

        def near():
            product(
                source([(1, part) for part in range(PARTS)]),
                weight,
                [(step, put(near_out, part)) for part in range(PARTS)],
            )
            return send(near_out, near_in, core)

        def mine():
            product(
                source([(0, part) for part in range(PARTS)]),
                weight,
                [(step, put(own, part)) for part in range(PARTS)],
            )

        def total(part):
            return own[part] + near_in[part].astype(F32) + line_in[part].astype(F32)

        return far, pass_on, near, mine, total

    def lower(values, gain, shift):
        if backward:
            return values.astype(BF16)
        return (normalise(values)[0] * gain[...] + shift[...]).astype(BF16)

    def begin_rows(rows, part):
        near = send(rows.at[chunk(0, part)], rows.at[chunk(1, part)], core)
        far = send(rows.at[chunk(0, part)], rows.at[chunk(2, part)], line)
        return near, far

    def forward_rows(rows, part, far):
        far.wait()
        return send(rows.at[chunk(2, part)], rows.at[chunk(3, part)], core)

    ready = None
    if enter:
        source_t = ref[SOURCE]

        def entering(pieces):
            return turned(joined([source_t[:, chunk(*piece)] for piece in pieces], 1)).astype(BF16)

        far, pass_on, near, mine, total = scatter(ENTER, entering, ref[ENTER_W])
        loaded(ENTER_W)
        greeted()
        point(0)
        if COTANGENT_HBM in ref:
            moved = courier.swap(ref[COTANGENT_HBM], ref[MOVED_HBM])
        passing = [far(part) for part in range(PARTS)]
        lines = [pass_on(part, passing[part]) for part in range(PARTS)]
        near_sum = near()
        mine()
        point(1)
        near_sum.wait()
        point(2)

        def ready(part):
            lines[part].wait()
            at = place(part)
            if backward:
                grad, gains, shifts = norm_backward(
                    ref[ENTER_AT][at, :], ref[ENTER_GAIN][...], total(part)
                )
                state[at, :] = value[at, :] + grad
                add_wide(0, gains)
                add_wide(1, shifts)
            else:
                state[at, :] = value[at, :] + (total(part) + ref[ENTER_BIAS][...])
            ref[ENTERED][at, :] = state[at, :]

    else:
        greeted()
        point(0)

        if COTANGENT in ref:
            lowered = mat(value[...].astype(BF16), ref[REORDER][...])
            ref[ROWS_OUT][...] = lowered.astype(BF16)
            moved = courier.swap(ref[ROWS_OUT], ref[MOVED_HBM])
            state[...] = mat(ref[COTANGENT][...], ref[REORDER][...])

        def ready(part):
            at = place(part)
            if COTANGENT not in ref:
                state[at, :] = value[at, :]

    if mix:
        rows, act, slope = ref[ROWS], ref[ACT], ref[SLOPE]
        first, second = ref[FIRST], ref[SECOND]
        units = first.shape[1]
        if backward:
            ref[UNIT_SUMS][...] = jnp.zeros(ref[UNIT_SUMS].shape, F32)
        begun = []
        for part in range(PARTS):
            ready(part)
            lowered = lower(
                state[place(part), :], ref.get(MIX_GAIN), ref.get(MIX_SHIFT)
            )
            rows[chunk(0, part), :] = lowered
            begun.append(begin_rows(rows, part))
            if backward:
                add_wide(2, jnp.sum(lowered.astype(F32), axis=0))

        def expand(pieces):
            taken = joined([rows[chunk(*piece), :] for piece in pieces])

            def strip(at, carry):
                columns = strips(at)
                up = mat(taken, first[:, columns])
                tilt = None
                if backward:
                    slopes = joined([slope[chunk(*piece), columns] for piece in pieces])
                    out = (up * slopes.astype(F32)).astype(BF16)
                    ref[UNIT_SUMS][:, columns] += jnp.sum(
                        out.astype(F32), axis=0, keepdims=True
                    )
                else:
                    up = up + ref[FIRST_BIAS][:, columns]
                    sigmoid = 1.0 / (1.0 + jnp.exp(-1.702 * up))
                    out = (up * sigmoid).astype(BF16)
                    tilt = (sigmoid + 1.702 * up * sigmoid * (1.0 - sigmoid)).astype(BF16)
                for index, piece in enumerate(pieces):
                    at_rows = slice(index * step, (index + 1) * step)
                    act[chunk(*piece), columns] = out[at_rows]
                    if tilt is not None:
                        slope[chunk(*piece), columns] = tilt[at_rows]
                return carry

            lax.fori_loop(0, units // STRIP, strip, 0)

        def acting(pieces):
            return joined([act[chunk(*piece), :] for piece in pieces])

        far, pass_on, near, mine, total = scatter(MIX, acting, second)
        loaded(FIRST)
        if backward:
            loaded(SLOPE)
        expand([(0, part) for part in range(PARTS)])
        for part in range(PARTS):
            begun[part][0].wait()
        point(3)
        expand([(1, part) for part in range(PARTS)])
        loaded(SECOND)
        near_sum = near()
        point(4)
        forwards = [forward_rows(rows, 0, begun[0][1])]
        mine()
        lines = []
        for part in range(PARTS):
            forwards[part].wait()
            expand([(2, part), (3, part)])
            lines.append(pass_on(part, far(part)))
            if part + 1 < PARTS:
                forwards.append(forward_rows(rows, part + 1, begun[part + 1][1]))
            point(5 + part)
        saves.append(local(rows, ref[ROWS_HBM]))
        saves.append(local(act, ref[ACT_HBM]))
        if not backward:
            saves.append(local(slope, ref[SLOPE_HBM]))
        near_sum.wait()

        def ready(part):
            lines[part].wait()
            at = place(part)
            if backward:
                grad, gains, shifts = norm_backward(
                    ref[MIX_AT][at, :], ref[MIX_GAIN][...], total(part)
                )
                state[at, :] = state[at, :] + grad
                add_wide(3, gains)
                add_wide(4, shifts)
            else:
                state[at, :] = state[at, :] + (total(part) + ref[SECOND_BIAS][...])
            ref[MIXED][at, :] = state[at, :]

    if leave:
        rows2, weight, target = ref[ROWS2], ref[LEAVE_W], ref[TARGET]
        begun = []
        for part in range(PARTS):
            ready(part)
            lowered = lower(
                state[place(part), :], ref.get(LEAVE_GAIN), ref.get(LEAVE_SHIFT)
            )
            rows2[chunk(0, part), :] = lowered
            begun.append(begin_rows(rows2, part))
            if backward:
                add_wide(5, jnp.sum(lowered.astype(F32), axis=0))

        def leaving(pieces):
            result = mat(joined([rows2[chunk(*piece), :] for piece in pieces]), weight[...])
            if not backward:
                result = result + ref[LEAVE_BIAS][...]
            result = turned(result)
            if not backward:
                cos, sin = (
                    joined([ref[name][:, chunk(*piece)] for piece in pieces], 1)
                    for name in (COSINE, SINE)
                )
                half, third = HD // 2, result.shape[0] // 3
                blocks = []
                for base in range(0, 2 * third, HD):
                    low, high = result[base : base + half], result[base + half : base + HD]
                    blocks += [low * cos - high * sin, high * cos + low * sin]
                result = jnp.concatenate(blocks + [result[2 * third :]], axis=0)
            result = result.astype(BF16)
            for index, piece in enumerate(pieces):
                target[:, chunk(*piece)] = result[:, index * step : (index + 1) * step]

        loaded(LEAVE_W)
        point(7)
        leaving([(0, part) for part in range(PARTS)])
        for part in range(PARTS):
            begun[part][0].wait()
        leaving([(1, part) for part in range(PARTS)])
        point(8)
        forwards = [forward_rows(rows2, part, begun[part][1]) for part in range(PARTS)]
        for part in range(PARTS):
            forwards[part].wait()
            leaving([(2, part), (3, part)])
        saves.append(local(rows2, ref[ROWS2_HBM]))
    else:
        for part in range(PARTS):
            ready(part)
    if REORDER in ref and COTANGENT not in ref:
        lowered = mat(state[...].astype(BF16), ref[REORDER][...]).astype(BF16)
        rows_out = ref[ROWS_OUT]
        rows_out[...] = lowered
        moved = courier.swap(rows_out, ref[MOVED_HBM])
    point(9)
    if MOVED_HBM in ref:
        moved()
    for save in saves:
        save.wait()
    courier.finish_all()


class Weight:
    def __init__(self, pack, begin, end):
        self.pack, self.begin, self.end = pack, begin, end


def chain_call(stages, backward, collective, operands, packs, jobs=()):
    enter, mix, leave = stages
    count, width = operands[VALUE].shape
    step = count // PARTS
    shape = jax.ShapeDtypeStruct
    vmem, anywhere = pl.BlockSpec(memory_space=pltpu.VMEM), pl.BlockSpec(memory_space=pl.ANY)
    outputs, scratch = {}, {}
    buffers = lambda kind: pltpu.VMEM((PARTS, step, width), kind)
    scratch[STATE] = pltpu.VMEM((count, width), F32)
    scratch[OWN] = buffers(F32)
    scratch[FAR_OWN] = buffers(F32)
    remote, here = 0, 0
    if backward:
        outputs[WIDE_SUMS] = shape((8, width), F32)
    flops = 0
    plan = []
    passed = {}
    needs, makes, job_scratch, job_remote, job_here = pack_buffers([job[1:] for job in jobs], packs)
    scratch.update(job_scratch)
    remote, here = remote + job_remote, here + job_here
    for name, value in operands.items():
        if not isinstance(value, Weight):
            passed[name] = value
            continue
        blocks, row = [], 0
        for part in (PAIR, LOW, HIGH, CORNER, ONE, OTHER, ALL):
            piece = (value.pack, part)
            if piece not in packs and piece not in makes:
                continue
            if piece not in makes:
                passed[piece] = packs[piece]
            array = makes.get(piece, packs.get(piece))
            for index in range(array.shape[0]):
                blocks.append((piece, index, row, array.shape[1], value.begin, value.end))
                row += array.shape[1]
        plan.append((name, blocks))
        scratch[name] = pltpu.VMEM((width, value.end - value.begin), BF16)
        here += len(blocks)
        flops += 8 * count * width * (value.end - value.begin)
    passed.update({name: value for name, value in needs.items() if name not in passed})
    outputs.update(makes)
    for stage, prefix in ((enter, ENTER), (mix, MIX)):
        if stage:
            for name in (FAR_OUT, FAR_IN, LINE_OUT, LINE_IN, NEAR_OUT, NEAR_IN):
                scratch[prefix, name] = buffers(BF16)
            remote += 2 * PARTS + 1
    if enter:
        outputs[ENTERED] = shape((count, width), F32)
    if mix:
        units = operands[FIRST].end - operands[FIRST].begin
        scratch[ROWS] = pltpu.VMEM((4 * count, width), BF16)
        scratch[ACT] = pltpu.VMEM((4 * count, units), BF16)
        scratch[SLOPE] = pltpu.VMEM((4 * count, units), BF16)
        outputs[MIXED] = shape((count, width), F32)
        outputs[ROWS_HBM] = shape((4 * count, width), BF16)
        outputs[ACT_HBM] = shape((4 * count, units), BF16)
        if backward:
            outputs[UNIT_SUMS] = shape((1, units), F32)
        else:
            outputs[SLOPE_HBM] = shape((4 * count, units), BF16)
        remote += 3 * PARTS
        here += 3
    if leave:
        columns = leave
        scratch[ROWS2] = pltpu.VMEM((4 * count, width), BF16)
        outputs[TARGET] = shape((columns, 4 * count), BF16)
        outputs[ROWS2_HBM] = shape((4 * count, width), BF16)
        remote += 3 * PARTS
        here += 1
    if REORDER in operands or COTANGENT_HBM in operands:
        if REORDER in operands:
            scratch[ROWS_OUT] = pltpu.VMEM((count, width), BF16)
        outputs[MOVED_HBM] = shape((count, width), BF16)
        remote, here = remote + 1, here + 1
    scratch[REMOTE] = pltpu.SemaphoreType.DMA((2, remote))
    scratch[HERE] = pltpu.SemaphoreType.DMA((here,))
    names = tuple(passed) + tuple(outputs) + tuple(scratch)
    spec = lambda name: anywhere if isinstance(name, tuple) or name >= FIRST_HBM else vmem
    results = pl.pallas_call(
        functools.partial(chain_kernel, stages, backward, names, plan, jobs),
        name="chain_backward" if backward else "chain_forward",
        out_shape=tuple(outputs.values()),
        in_specs=[spec(name) for name in passed],
        out_specs=tuple(spec(name) for name in outputs),
        scratch_shapes=list(scratch.values()),
        compiler_params=pltpu.CompilerParams(
            collective_id=collective, has_side_effects=True, vmem_limit_bytes=54 << 20
        ),
        cost_estimate=pl.CostEstimate(
            flops=flops, bytes_accessed=(16 << 20) * sum(map(bool, stages)), transcendentals=0
        ),
    )(*passed.values())
    results = dict(zip(outputs, results))
    packs.update({name: results[name] for name in makes})
    return results


def make_body(dp, mp):
    assert mp == 4 and dp >= 2 and dp & (dp - 1) == 0
    count = dp * mp
    high_bits = [1 << b for b in range(1, dp.bit_length() - 1)]

    def across(value, bit):
        return lax.ppermute(value, "dp", [(i, i ^ bit) for i in range(dp)])

    def core_side(value):
        return across(value, 1)

    def line_side(value):
        return lax.ppermute(value, "mp", [(i, i ^ 1) for i in range(mp)])

    def swapped(d, m):
        return (d & ~1 | m >> 1) * mp + ((d & 1) << 1 | m & 1)

    swap_pairs = [
        (d * mp + m, swapped(d, m)) for d in range(dp) for m in range(mp) if d & 1 != m >> 1
    ]

    def swap(value):
        stays = (lax.axis_index("dp") & 1) == (lax.axis_index("mp") >> 1)
        return jnp.where(stays, value, lax.ppermute(value, ("dp", "mp"), swap_pairs))

    balanced = len(high_bits) == 2

    def gather_pair(mine):
        return swap(jnp.stack([mine, core_side(mine)]))

    def gather_sides(pair):
        for bit in high_bits:
            pair = jnp.concatenate([pair, across(pair, bit)], axis=0)
        return (pair,)

    def add(*terms):
        total = terms[0].astype(F32)
        for term in terms[1:]:
            total = total + term.astype(F32)
        return total.astype(BF16)

    def scatter_blocks(grad):
        total = grad.reshape(dp, D // dp, -1)
        for bit in high_bits[::-1]:
            half = total.shape[0] // 2
            total = add(total[:half], across(total[half:], bit))
        total = swap(total)
        return total[0].astype(F32) + core_side(total[1]).astype(F32)

    def arranged(values):
        index = lax.axis_index("dp") * mp + lax.axis_index("mp")
        at = jnp.arange(count, dtype=jnp.int32)
        order = (at[:, None] ^ index) == at[None, :]
        return dot(order.astype(F32), values, 1, 0, precision=HIGHEST)

    def gather_vectors(mine):
        values = mine[None]
        bit = 1
        while bit < count:
            if bit >= mp:
                got = across(values, bit // mp)
            else:
                got = lax.ppermute(values, "mp", [(i, i ^ bit) for i in range(mp)])
            values = jnp.concatenate([values, got], axis=0)
            bit *= 2
        return arranged(values)

    def scatter_vectors(values):
        index = lax.axis_index("dp") * mp + lax.axis_index("mp")
        bit = count // 2
        while bit:
            half = values.shape[0] // 2
            top = (index & bit) != 0
            low, high = values[:half], values[half:]
            sent = jnp.where(top, low, high)
            if bit >= mp:
                got = across(sent, bit // mp)
            else:
                got = lax.ppermute(sent, "mp", [(i, i ^ bit) for i in range(mp)])
            values = jnp.where(top, high, low) + got
            bit //= 2
        return values[0]

    def body(
        hidden_in,
        pre_gain,
        pre_bias,
        qkv_weight,
        qkv_bias,
        proj_weight,
        proj_bias,
        mid_gain,
        mid_bias,
        up_weight,
        up_bias,
        down_weight,
        down_bias,
        picture_ids,
        positions,
        pad_mask,
        cotangent,
    ):
        dp_at, mp_at = lax.axis_index("dp"), lax.axis_index("mp")
        group_at = (dp_at & ~1) | (mp_at >> 1)
        quarter_at = ((dp_at & 1) << 1) | (mp_at & 1)
        depth = D // dp
        columns = qkv_weight.shape[3]
        units = up_weight.shape[2]
        heads = columns // HD

        place = jnp.arange(D, dtype=jnp.int32)
        moved = ((place // depth) ^ group_at) * depth + place % depth
        reorder = place[:, None] == moved[None, :]
        reorder_low = reorder.astype(BF16)
        reorder_full = reorder.astype(F32)

        def turn_low(values):
            return dot(values.astype(BF16), reorder_low, 1, 0)

        qkv_width, proj_width = 3 * columns, columns
        packs = {}
        for layer in range(LAYERS):
            mine = qkv_weight[layer].transpose(1, 0, 2).reshape(depth, qkv_width)
            packs[(QKV, layer), MINE] = mine
            packs[(PROJ, layer), MINE] = proj_weight[layer].T
            packs[(UP, layer), MINE] = up_weight[layer]
            packs[(DOWN, layer), MINE] = down_weight[layer].T

        wide = (pre_gain, pre_bias, proj_bias, mid_gain, mid_bias, down_bias)
        packed = jnp.concatenate(
            [item.reshape(-1) for item in wide] + [qkv_bias.reshape(-1), up_bias.reshape(-1)]
        )
        length = picture_ids.shape[0]
        quarter = length // mp
        row_at = jnp.arange(length, dtype=jnp.int32)
        codes = jnp.where(pad_mask == 1, picture_ids, 1024 + row_at)
        row_facts = jnp.concatenate([codes[None], positions], axis=0)
        hidden = hidden_in.astype(BF16)
        jobs = {}
        if balanced:
            space = -(-packed.shape[0] // 1024) * 1024
            late = packs[(QKV, 1), MINE], packs[(DOWN, 1), MINE], packs[(PROJ, 1), MINE]
            hidden, late = lax.optimization_barrier((hidden, late))
            packs[(QKV, 1), MINE], packs[(DOWN, 1), MINE], packs[(PROJ, 1), MINE] = late
            begun = start_call(
                3 * LAYERS + 1,
                hidden,
                jnp.pad(row_facts, ((0, 5), (0, 0))),
                jnp.pad(packed, (0, space - packed.shape[0])).reshape(-1, 128),
                (((QKV, 0), 1), ((QKV, 0), 2), ((PROJ, 0), 1), ((UP, 0), 1), ((QKV, 0), 3)),
                packs,
            )
            hidden, row_facts = begun[MOVED_HBM], begun[ROW_FACTS_HBM][:3]
            packed = arranged(begun[VECTORS_HBM].reshape(count, space))[:, : packed.shape[0]]
            schedule = {
                (LEAVE, 0): {
                    0: ((UP, 0, 2), (PROJ, 0, 2), (DOWN, 0, 1)),
                    8: ((PROJ, 0, 3),),
                },
                (FORWARD, 0): {
                    0: ((DOWN, 0, 3), (QKV, 1, 1)),
                    2: ((PROJ, 1, 1),),
                    4: ((QKV, 1, 2), (PROJ, 1, 2), (UP, 1, 1)),
                    6: ((QKV, 1, 3), (PROJ, 1, 3)),
                },
                (LEAVE, 1): {0: ((UP, 1, 2), (DOWN, 1, 1))},
                (FORWARD, 1): {0: ((DOWN, 1, 3),)},
                (BACKWARD, 0): {
                    0: ((UP, 1, 4), (DOWN, 1, 4)),
                    1: ((UP, 1, 5),),
                    4: ((DOWN, 1, 5), (QKV, 1, 4), (PROJ, 1, 4)),
                    5: ((UP, 1, 6),),
                    8: ((DOWN, 1, 6), (QKV, 1, 5), (PROJ, 1, 5)),
                },
                (BACKWARD, FINAL): {
                    0: ((UP, 0, 4), (DOWN, 0, 4)),
                    1: ((UP, 0, 5),),
                    2: ((QKV, 1, 6), (PROJ, 1, 6), (QKV, 0, 4), (PROJ, 0, 4)),
                    9: (
                        *((UP, 0, 6), (DOWN, 0, 5), (QKV, 0, 5), (UP, 1, 7), (DOWN, 1, 7)),
                        *((DOWN, 0, 6), (PROJ, 0, 5), (QKV, 1, 7), (PROJ, 1, 7), (UP, 0, 7)),
                        *((QKV, 0, 6), (PROJ, 0, 6), (DOWN, 0, 7), (QKV, 0, 7), (PROJ, 0, 7)),
                    ),
                },
            }
            jobs = {
                kernel: tuple(
                    (at, (name, layer), step)
                    for at, steps in points.items()
                    for name, layer, step in steps
                )
                for kernel, points in schedule.items()
            }
        else:
            for name in list(packs):
                packs[name[0], ALL] = gather_sides(gather_pair(packs[name]))[0].reshape(1, D, -1)
            hidden, row_facts, packed = swap(hidden), swap(row_facts), gather_vectors(packed)
        hidden = turn_low(hidden)
        each = D // count
        wide_count = len(wide) * LAYERS
        split = (wide_count + 3 * LAYERS) * each
        vectors = packed[:, :split].reshape(count, -1, each).transpose(1, 0, 2).reshape(-1, D)
        wide_all = dot(vectors[:wide_count], reorder_full, 1, 0, precision=HIGHEST)
        wide_all = wide_all.reshape(len(wide), LAYERS, D)
        pre_gain_all, pre_bias_all, proj_bias_all, mid_gain_all, mid_bias_all, down_bias_all = (
            wide_all[i] for i in range(len(wide))
        )
        qkv_bias_mine = lax.dynamic_slice_in_dim(
            vectors[wide_count:], quarter_at * columns, columns, 1
        ).reshape(LAYERS, 3 * columns)
        up_all = packed[:, split:].reshape(count, LAYERS, -1).transpose(1, 0, 2)
        up_bias_mine = lax.dynamic_slice_in_dim(
            up_all.reshape(LAYERS, -1), quarter_at * units, units, 1
        )

        row_facts = jnp.concatenate(
            [
                lax.dynamic_slice_in_dim(row_facts, (quarter_at ^ which) * quarter, quarter, 1)
                for which in (0, 2, 1, 3)
            ],
            axis=1,
        )
        codes = row_facts[0]
        facts = (tile_overlap(codes), *rotary_tables(row_facts[1:]), codes[None], codes[:, None])

        row = lambda vector: vector[None]
        weights = [
            (
                Weight((QKV, layer), 0, qkv_width),
                Weight((PROJ, layer), 0, proj_width),
                Weight((UP, layer), 0, units),
                Weight((DOWN, layer), 0, units),
            )
            for layer in range(LAYERS)
        ]

        def leave_forward(layer):
            return {
                LEAVE_W: weights[layer][0],
                LEAVE_GAIN: row(pre_gain_all[layer]),
                LEAVE_SHIFT: row(pre_bias_all[layer]),
                LEAVE_BIAS: row(qkv_bias_mine[layer]),
                COSINE: facts[1],
                SINE: facts[2],
            }

        def call_leave(layer, value):
            return chain_call(
                (False, False, qkv_width),
                False,
                layer,
                {VALUE: value, **leave_forward(layer)},
                packs,
                jobs.get((LEAVE, layer), ()),
            )

        def call_forward(layer, value, mixed, more):
            return chain_call(
                (True, True, False),
                False,
                LAYERS + layer,
                {
                    VALUE: value,
                    SOURCE: mixed,
                    ENTER_W: weights[layer][1],
                    ENTER_BIAS: row(proj_bias_all[layer]),
                    FIRST: weights[layer][2],
                    SECOND: weights[layer][3],
                    FIRST_BIAS: row(up_bias_mine[layer]),
                    SECOND_BIAS: row(down_bias_all[layer]),
                    MIX_GAIN: row(mid_gain_all[layer]),
                    MIX_SHIFT: row(mid_bias_all[layer]),
                    **more,
                },
                packs,
                jobs.get((FORWARD, layer), ()),
            )

        def call_backward(layer, value, entering, middle, slope, more):
            return chain_call(
                (bool(entering), True, proj_width),
                True,
                2 * LAYERS + layer,
                {
                    VALUE: value,
                    **entering,
                    **more,
                    FIRST: weights[layer][3],
                    SECOND: weights[layer][2],
                    SLOPE_HBM: slope,
                    MIX_AT: middle,
                    MIX_GAIN: row(mid_gain_all[layer]),
                    LEAVE_W: weights[layer][1],
                },
                packs,
                jobs.get((BACKWARD, layer), ()),
            )

        def entering(layer, grad_linear, start):
            return {
                SOURCE: grad_linear,
                ENTER_W: weights[layer][0],
                ENTER_AT: start,
                ENTER_GAIN: row(pre_gain_all[layer]),
            }

        def beside_forward(layer):
            if not balanced:
                return
            low, high = high_bits
            up, down = (UP, layer), (DOWN, layer)
            packs[up, ONE] = across(packs[up, LOW][:1], high)
            packs[up, OTHER] = across(packs[up, HIGH][1:], low)
            packs[down, LOW] = across(packs[down, PAIR], low)
            packs[down, HIGH] = across(packs[down, PAIR], high)

        hidden, wide_all, qkv_bias_mine, up_bias_mine, facts = lax.optimization_barrier(
            (hidden, wide_all, qkv_bias_mine, up_bias_mine, facts)
        )
        pre_gain_all, pre_bias_all, proj_bias_all, mid_gain_all, mid_bias_all, down_bias_all = (
            wide_all[i] for i in range(len(wide))
        )
        leave0 = call_leave(0, hidden)
        beside_forward(0)
        qkv0 = leave0[TARGET]
        mixed0, log_sum0 = attend_forward(qkv0, facts)
        state0 = call_forward(0, hidden, mixed0, {})
        start1 = state0[MIXED]
        leave1 = call_leave(1, start1)
        beside_forward(1)
        qkv1 = leave1[TARGET]
        mixed1, log_sum1 = attend_forward(qkv1, facts)
        cotangent = cotangent.astype(BF16)
        if balanced:
            state1 = call_forward(1, start1, mixed1, {COTANGENT_HBM: cotangent})
            back1 = call_backward(
                1,
                state1[MIXED],
                {},
                state1[ENTERED],
                state1[SLOPE_HBM],
                {COTANGENT: state1[MOVED_HBM], REORDER: reorder_low},
            )
            out_hidden = back1[MOVED_HBM]
        else:
            state1 = call_forward(1, start1, mixed1, {})
            out_hidden = swap(turn_low(state1[MIXED]).astype(BF16))
            gradient = turn_low(swap(cotangent))
            back1 = call_backward(1, gradient, {}, state1[ENTERED], state1[SLOPE_HBM], {})
        packs[(UP, 1), GRAD] = grad_dot(state1[ROWS_HBM], back1[ACT_HBM], 0, 0)
        packs[(DOWN, 1), GRAD] = grad_dot(back1[ROWS_HBM], state1[ACT_HBM], 0, 0)
        linear1 = attend_backward(qkv1, mixed1, back1[TARGET], log_sum1, facts)
        packs[(QKV, 1), GRAD] = grad_dot(leave1[ROWS2_HBM], linear1, 0, 1)
        packs[(PROJ, 1), GRAD] = grad_dot(back1[ROWS2_HBM], mixed1, 0, 1)
        back0 = call_backward(
            0,
            back1[MIXED],
            entering(1, linear1, start1),
            state0[ENTERED],
            state0[SLOPE_HBM],
            {},
        )
        packs[(UP, 0), GRAD] = grad_dot(state0[ROWS_HBM], back0[ACT_HBM], 0, 0)
        packs[(DOWN, 0), GRAD] = grad_dot(back0[ROWS_HBM], state0[ACT_HBM], 0, 0)
        target0, packs[(UP, 0), GRAD], packs[(DOWN, 0), GRAD] = lax.optimization_barrier(
            (back0[TARGET], packs[(UP, 0), GRAD], packs[(DOWN, 0), GRAD])
        )
        linear0 = attend_backward(qkv0, mixed0, target0, log_sum0, facts)
        packs[(QKV, 0), GRAD] = grad_dot(leave0[ROWS2_HBM], linear0, 0, 1)
        packs[(PROJ, 0), GRAD] = grad_dot(back0[ROWS2_HBM], mixed0, 0, 1)
        final = chain_call(
            (True, False, False),
            True,
            3 * LAYERS,
            {
                VALUE: back0[MIXED],
                **entering(0, linear0, hidden),
                **({REORDER: reorder_low} if balanced else {}),
            },
            packs,
            jobs.get((BACKWARD, FINAL), ()),
        )
        if balanced:
            grad_hidden = final[MOVED_HBM].astype(F32)
        else:
            grad_hidden = swap(turn_low(final[ENTERED]).astype(BF16)).astype(F32)
            for name in list(packs):
                if name[1] == GRAD:
                    packs[name[0], RESULT] = scatter_blocks(packs[name])
        out_hidden = out_hidden.astype(F32)
        grads, parts = [], []
        for layer, back, linear in ((0, back0, linear0), (1, back1, linear1)):
            result = lambda which: packs[(which, layer), RESULT]
            grads.append(
                (
                    result(QKV).reshape(depth, 3, columns).transpose(1, 0, 2),
                    result(PROJ).T,
                    result(UP),
                    result(DOWN).T,
                )
            )
            qkv_bias_part = jnp.sum(linear.astype(F32), axis=1)
            parts.append((qkv_bias_part.reshape(3, columns), back[UNIT_SUMS][0]))
        sums = [back1[WIDE_SUMS], back0[WIDE_SUMS], final[WIDE_SUMS]]

        stacked = jnp.stack(
            [
                sums[LAYERS - layer - which][at]
                for which, at in ((0, 0), (0, 1), (1, 5), (1, 3), (1, 4), (1, 2))
                for layer in range(LAYERS)
            ]
        )
        stacked = dot(stacked, reorder_full, 1, 0, precision=HIGHEST)
        qkv_padded = lax.dynamic_update_slice_in_dim(
            jnp.zeros((LAYERS * 3, D), F32),
            jnp.concatenate([part[0] for part in parts], axis=0),
            quarter_at * columns,
            1,
        )
        up_padded = lax.dynamic_update_slice_in_dim(
            jnp.zeros((LAYERS, units * mp), F32),
            jnp.stack([part[1] for part in parts]),
            quarter_at * units,
            1,
        )
        by_owner = jnp.concatenate([stacked, qkv_padded], axis=0).reshape(-1, count, each)
        by_owner = jnp.concatenate(
            [
                by_owner.transpose(1, 0, 2).reshape(count, -1),
                up_padded.reshape(LAYERS, count, -1).transpose(1, 0, 2).reshape(count, -1),
            ],
            axis=1,
        )
        mine = scatter_vectors(by_owner)
        wide_grads = mine[: wide_count * each].reshape(len(wide), LAYERS, each)
        qkv_bias_grad = mine[wide_count * each : split].reshape(LAYERS, 3, each)
        up_bias_grad = mine[split:].reshape(LAYERS, -1)
        matrices = [jnp.stack([entry[i] for entry in grads]) for i in range(4)]
        return (
            out_hidden,
            grad_hidden,
            wide_grads[0],
            wide_grads[1],
            matrices[0],
            qkv_bias_grad,
            matrices[1],
            wide_grads[2],
            wide_grads[3],
            wide_grads[4],
            matrices[2],
            up_bias_grad,
            matrices[3],
            wide_grads[5],
        )

    return body


def solution(mesh):
    rows = P(("dp", "mp"), None)
    vector = P(None, ("dp", "mp"))
    vectors = P(None, None, ("dp", "mp"))
    qkv = P(None, None, "dp", "mp")
    tall = P(None, "mp", "dp")
    broad = P(None, "dp", "mp")
    return jax.shard_map(
        make_body(mesh.shape["dp"], mesh.shape["mp"]),
        mesh=mesh,
        in_specs=(
            rows,
            vector,
            vector,
            qkv,
            vectors,
            tall,
            vector,
            vector,
            vector,
            broad,
            vector,
            tall,
            vector,
            P("dp"),
            P(None, "dp"),
            P("dp"),
            rows,
        ),
        out_specs=(
            rows,
            rows,
            vector,
            vector,
            qkv,
            vectors,
            tall,
            vector,
            vector,
            vector,
            broad,
            vector,
            tall,
            vector,
        ),
        check_vma=False,
    )
```

```python
import functools

import jax
import jax.numpy as jnp
from jax import lax
from jax.experimental import pallas as pl
from jax.experimental.layout import Layout, with_layout_constraint
from jax.experimental.pallas import tpu as pltpu
from jax.sharding import PartitionSpec as P

D = 1280
HD = 80
LAYERS = 2
EPSILON = 1e-06
AXES = ("dp", "mp")
F32 = jnp.float32
BF16 = jnp.bfloat16
HIGHEST = lax.Precision.HIGHEST


def normalise(values):
    centre = values - jnp.mean(values, axis=-1, keepdims=True)
    spread = jnp.mean(centre * centre, axis=-1, keepdims=True)
    scale = lax.rsqrt(spread + EPSILON)
    return centre * scale, scale


def norm_backward(values, gain, grad):
    normed, scale = normalise(values)
    inner = grad * gain
    mean_inner = jnp.mean(inner, axis=-1, keepdims=True)
    mean_cross = jnp.mean(inner * normed, axis=-1, keepdims=True)
    grad_values = scale * (inner - mean_inner - normed * mean_cross)
    return grad_values, jnp.sum(grad * normed, axis=0), jnp.sum(grad, axis=0)


def dot(left, right, left_dim, right_dim, kind=F32, precision=None):
    return lax.dot_general(
        left,
        right,
        (((left_dim,), (right_dim,)), ((), ())),
        preferred_element_type=F32,
        precision=precision,
    ).astype(kind)


def grad_dot(left, right, left_dim, right_dim):
    return with_layout_constraint(dot(left, right, left_dim, right_dim, BF16), Layout((0, 1)))


def rotary_tables(coords):
    quarter = HD // 4
    powers = jnp.arange(quarter, dtype=F32) * (4.0 / HD)
    inverse = 10000.0 ** (-powers)
    height_angle = inverse[:, None] * coords[0].astype(F32)[None, :]
    width_angle = inverse[:, None] * coords[1].astype(F32)[None, :]
    angles = jnp.concatenate([height_angle, width_angle], axis=0)
    return (jnp.cos(angles), jnp.sin(angles))


TILE = 256
MASKED = -1e30
LOG2E = 1.4426950408889634
SCORE_SCALE = HD**-0.5 * LOG2E


def mat(left, right):
    return lax.dot_general(left, right, (((1,), (0,)), ((), ())), preferred_element_type=F32)


def mat_turned(left, right):
    return lax.dot_general(left, right, (((1,), (1,)), ((), ())), preferred_element_type=F32)


def tile_bias(code_col, code_row, keys, queries):
    same = code_col[keys, :] == code_row[:, queries]
    return jnp.where(same, 0.0, MASKED)


def tiles(at):
    return pl.ds(pl.multiple_of(at * TILE, TILE), TILE)


def forward_kernel(active, qkv, code_row, code_col, mixed, log_sum, k_rows, top, total, acc):
    heads, length = k_rows.shape[0], k_rows.shape[1]
    blocks = length // TILE
    for head in range(heads):
        base = (heads + head) * HD
        k_rows[head] = turned(qkv[base : base + HD, :]).astype(BF16)

    def query_block(q_at, carry):
        queries = tiles(q_at)
        top[...] = jnp.full(top.shape, MASKED, F32)
        total[...] = jnp.zeros(total.shape, F32)
        acc[...] = jnp.zeros(acc.shape, F32)

        def key_block(k_at, carry):
            @pl.when(active[q_at * blocks + k_at] != 0)
            def _():
                keys = tiles(k_at)
                bias = tile_bias(code_col, code_row, keys, queries)
                every = range(heads)
                scores = [
                    mat(k_rows[head, keys, :], qkv[head * HD : (head + 1) * HD, queries]) + bias
                    for head in every
                ]
                old = [top[head] for head in every]
                new = [
                    jnp.maximum(old[head], jnp.max(scores[head], axis=0, keepdims=True))
                    for head in every
                ]
                chance = [jnp.exp2((scores[head] - new[head]) * SCORE_SCALE) for head in every]
                fade = [jnp.exp2((old[head] - new[head]) * SCORE_SCALE) for head in every]
                added = [jnp.sum(chance[head], axis=0, keepdims=True) for head in every]
                products = [
                    mat(
                        qkv[(2 * heads + head) * HD : (2 * heads + head + 1) * HD, keys],
                        chance[head].astype(BF16),
                    )
                    for head in every
                ]
                for head in every:
                    top[head] = new[head]
                    total[head] = total[head] * fade[head] + added[head]
                    acc[head] = acc[head] * fade[head] + products[head]

            return carry

        lax.fori_loop(0, blocks, key_block, 0)
        for head in range(heads):
            mixed[head * HD : (head + 1) * HD, queries] = (acc[head] / total[head]).astype(BF16)
            log_sum[head, :, queries] = top[head] * SCORE_SCALE + jnp.log2(total[head])
        return carry

    lax.fori_loop(0, blocks, query_block, 0)


def backward_kernel(active, qkv, mixed, grad_mixed, log_sum, cosine, sine, code_row, code_col, out, k_rows, v_rows, centre, grad_q, grad_k, grad_v):
    heads, length = k_rows.shape[0], k_rows.shape[1]
    blocks = length // TILE
    for head in range(heads):
        k_base, v_base = (heads + head) * HD, (2 * heads + head) * HD
        k_rows[head] = qkv[k_base : k_base + HD, :].astype(F32).T.astype(BF16)
        v_rows[head] = qkv[v_base : v_base + HD, :].astype(F32).T.astype(BF16)
        rows = slice(head * HD, (head + 1) * HD)
        centre[head] = jnp.sum(
            grad_mixed[rows, :].astype(F32) * mixed[rows, :].astype(F32), axis=0, keepdims=True
        )
    grad_q[...] = jnp.zeros(grad_q.shape, F32)
    grad_k[...] = jnp.zeros(grad_k.shape, F32)
    grad_v[...] = jnp.zeros(grad_v.shape, F32)

    def query_block(q_at, carry):
        queries = tiles(q_at)

        def key_block(k_at, carry):
            @pl.when(active[q_at * blocks + k_at] != 0)
            def _():
                keys = tiles(k_at)
                bias = tile_bias(code_col, code_row, keys, queries)
                every = range(heads)
                rows = [slice(head * HD, (head + 1) * HD) for head in every]
                scores = [mat(k_rows[h, keys, :], qkv[rows[h], queries]) + bias for h in every]
                raised = [mat(v_rows[h, keys, :], grad_mixed[rows[h], queries]) for h in every]
                chance = [
                    jnp.exp2(scores[h] * SCORE_SCALE - log_sum[h, :, queries]) for h in every
                ]
                pulled = [
                    (chance[h] * (raised[h] - centre[h, :, queries])).astype(BF16) for h in every
                ]
                for_v = [
                    mat_turned(grad_mixed[rows[h], queries], chance[h].astype(BF16)) for h in every
                ]
                for_k = [mat_turned(qkv[rows[h], queries], pulled[h]) for h in every]
                for_q = [
                    mat(qkv[(heads + h) * HD : (heads + h + 1) * HD, keys], pulled[h])
                    for h in every
                ]
                for h in every:
                    grad_v[h, :, keys] += for_v[h]
                    grad_k[h, :, keys] += for_k[h]
                    grad_q[h, :, queries] += for_q[h]

            return carry

        return lax.fori_loop(0, blocks, key_block, carry)

    lax.fori_loop(0, blocks, query_block, 0)
    half = HD // 2
    scale = HD**-0.5
    cos, sin = cosine[...] * scale, sine[...] * scale
    for head in range(heads):
        for which, grad in ((0, grad_q), (1, grad_k)):
            base = (which * heads + head) * HD
            low, high = grad[head, :half, :], grad[head, half:, :]
            turned = jnp.concatenate([low * cos + high * sin, high * cos - low * sin], axis=0)
            out[base : base + HD, :] = turned.astype(BF16)
        base = (2 * heads + head) * HD
        out[base : base + HD, :] = grad_v[head].astype(BF16)


def whole(count):
    return [pl.BlockSpec(memory_space=pltpu.VMEM)] * count


def attend_forward(qkv, facts):
    active, _, _, code_row, code_col = facts
    width, length = qkv.shape
    heads = width // (3 * HD)
    return pl.pallas_call(
        forward_kernel,
        name="attend_forward",
        out_shape=(
            jax.ShapeDtypeStruct((heads * HD, length), BF16),
            jax.ShapeDtypeStruct((heads, 1, length), F32),
        ),
        in_specs=[pl.BlockSpec(memory_space=pltpu.SMEM)] + whole(3),
        out_specs=tuple(whole(2)),
        scratch_shapes=[
            pltpu.VMEM((heads, length, HD), BF16),
            pltpu.VMEM((heads, 1, TILE), F32),
            pltpu.VMEM((heads, 1, TILE), F32),
            pltpu.VMEM((heads, HD, TILE), F32),
        ],
        compiler_params=pltpu.CompilerParams(vmem_limit_bytes=40 << 20),
        cost_estimate=pl.CostEstimate(
            flops=heads * length * length * HD * 4,
            bytes_accessed=4 << 20,
            transcendentals=heads * length * length,
        ),
    )(active, qkv, code_row, code_col)


def attend_backward(qkv, mixed, grad_mixed, log_sum, facts):
    active, cosine, sine, code_row, code_col = facts
    width, length = qkv.shape
    heads = width // (3 * HD)
    return pl.pallas_call(
        backward_kernel,
        name="attend_backward",
        out_shape=jax.ShapeDtypeStruct((width, length), BF16),
        in_specs=[pl.BlockSpec(memory_space=pltpu.SMEM)] + whole(8),
        out_specs=pl.BlockSpec(memory_space=pltpu.VMEM),
        scratch_shapes=[
            pltpu.VMEM((heads, length, HD), BF16),
            pltpu.VMEM((heads, length, HD), BF16),
            pltpu.VMEM((heads, 1, length), F32),
            pltpu.VMEM((heads, HD, length), F32),
            pltpu.VMEM((heads, HD, length), F32),
            pltpu.VMEM((heads, HD, length), F32),
        ],
        compiler_params=pltpu.CompilerParams(vmem_limit_bytes=40 << 20),
        cost_estimate=pl.CostEstimate(
            flops=heads * length * length * HD * 10, bytes_accessed=10 << 20, transcendentals=heads * length * length
        ),
    )(active, qkv, mixed, grad_mixed, log_sum, cosine, sine, code_row, code_col)


def tile_overlap(codes):
    blocks = codes.reshape(-1, TILE)
    least, most = jnp.min(blocks, axis=1), jnp.max(blocks, axis=1)
    meet = (least[:, None] <= most[None, :]) & (least[None, :] <= most[:, None])
    return meet.astype(jnp.int32).reshape(-1)


(
    ACT, ALL, ATTN, BACKWARD, CORE, CORNER, CORNERS, CROSS, DIAGONAL, DOWN, ENDS, ENTER, ENTERED,
    ENTER_AT, ENTER_BIAS, ENTER_GAIN, ENTER_W, FAR_IN, FAR_OUT, FAR_OWN, FINAL, FIRST,
    FIRST_BIAS, FORWARD, FROM_HIGH, FROM_LOW, GRAD, HELD, HERE, HIGH, LEAVE, LEAVE_BIAS,
    LEAVE_GAIN, LEAVE_SHIFT, LEAVE_W, LINE, LINE_IN, LINE_OUT, LOW, MINE, MIX, MIXED, MIX_AT,
    MIX_GAIN, MIX_SHIFT, NEAR_IN, NEAR_OUT, OWN, OWNED, PAIR, PROJ, QKV, REMOTE, REORDER, RESULT,
    ROWS, ROWS2, ROWS_OUT, SECOND, SECOND_BIAS, SLOPE, SOURCE, STATE, SUMS, TARGET, UNIT_SUMS,
    UP, VALUE, WIDE_SUMS,
) = range(69)
ONE, OTHER = 103, 104
COTANGENT, COSINE, SINE = 100, 101, 102
FIRST_HBM = 200
COTANGENT_HBM = FIRST_HBM + 50
(
    ACT_HBM, FACTS_HBM, HIDDEN_HBM, MOVED_HBM, ROWS2_HBM, ROWS_HBM, ROW_FACTS_HBM, SLOPE_HBM,
    VECTORS_HBM, VECTOR_HBM,
) = range(FIRST_HBM, FIRST_HBM + 10)


STRIP = 256
PARTS = 2
MESH_ID = pl.DeviceIdType.MESH


def strips(at):
    return pl.ds(pl.multiple_of(at * STRIP, STRIP), STRIP)


def partners():
    dp_at, mp_at = lax.axis_index("dp"), lax.axis_index("mp")
    core = dp_at + 1 - 2 * lax.rem(dp_at, 2)
    cross = mp_at + 2 - 4 * (mp_at // 2)
    return {
        CORE: {"dp": core},
        LINE: {"mp": mp_at + 1 - 2 * lax.rem(mp_at, 2)},
        CROSS: {"mp": cross},
        DIAGONAL: {"dp": core, "mp": cross},
        LOW: {"dp": dp_at + 2 - 4 * lax.rem(dp_at // 2, 2)},
        HIGH: {"dp": dp_at + 4 - 8 * lax.rem(dp_at // 4, 2)},
    }


def greet(names):
    barrier, devices = pltpu.get_barrier_semaphore(), partners()
    for name in names:
        pl.semaphore_signal(barrier, inc=1, device_id=devices[name], device_id_type=MESH_ID)
    return lambda: pl.semaphore_wait(barrier, len(names))


class Courier:
    def __init__(self, ref):
        self.ref, self.devices = ref, partners()
        self.remotes, self.locals = 0, 0
        self.open = {}
        self.aligned = lax.rem(lax.axis_index("dp"), 2) == lax.axis_index("mp") // 2

    def slot(self):
        self.remotes += 1
        return self.remotes - 1

    def remote(self, source, target, partner, at, received=None):
        sems = self.ref[REMOTE]
        received = at if received is None else received
        return pltpu.make_async_remote_copy(
            src_ref=source,
            dst_ref=target,
            send_sem=sems.at[0, at],
            recv_sem=sems.at[1, received],
            device_id=self.devices[partner],
            device_id_type=MESH_ID,
        )

    def send(self, source, target, partner):
        copy = self.remote(source, target, partner, self.slot())
        copy.start()
        return copy

    def near(self, source, target):
        return pltpu.make_async_copy(source, target, self.ref[HERE].at[self.locals])

    def local(self, source, target):
        copy = self.near(source, target)
        self.locals += 1
        copy.start()
        return copy

    def swap(self, source, target):
        at, copy = self.slot(), self.near(source, target)
        self.locals += 1
        away = lambda: self.remote(source, target, DIAGONAL, at)
        pl.when(self.aligned)(copy.start)
        pl.when(jnp.logical_not(self.aligned))(lambda: away().start())

        def finish():
            pl.when(self.aligned)(copy.wait)
            pl.when(jnp.logical_not(self.aligned))(lambda: away().wait())

        return finish

    def begin(self, pack, step):
        ref = self.ref
        buffer = lambda part: ref[(pack, part)]
        if step == 1:
            mine, pair = buffer(MINE), buffer(PAIR)
            first, second, copy = self.slot(), self.slot(), self.near(mine, pair.at[0])
            self.locals += 1
            across = lambda: self.remote(mine, pair.at[1], CROSS, first)
            beside = lambda: self.remote(mine, pair.at[1], CORE, first)
            over = lambda: self.remote(mine, pair.at[0], DIAGONAL, second)

            def start_aligned():
                copy.start()
                across().start()

            def start_other():
                beside().start()
                over().start()

            def wait_aligned():
                copy.wait()
                across().wait()

            def wait_other():
                beside().wait()
                over().wait()

            pl.when(self.aligned)(start_aligned)
            pl.when(jnp.logical_not(self.aligned))(start_other)

            def finish():
                pl.when(self.aligned)(wait_aligned)
                pl.when(jnp.logical_not(self.aligned))(wait_other)

        elif step > 4:
            self.finish(pack, step - 1)
            finish = self.reduce(pack, step)
        else:
            self.finish(pack, step - 1)
            if step == 4:
                depth = buffer(CORNERS).shape[1]
                block = lambda at: buffer(GRAD).at[at * depth : (at + 1) * depth]
                copies = [
                    self.send(block(6), buffer(CORNERS).at[0], HIGH),
                    self.send(block(7), buffer(CORNERS).at[1], LOW),
                ]
            elif step == 2:
                pair = buffer(PAIR)
                copies = [self.send(pair, buffer(side), side) for side in (LOW, HIGH)]
            else:
                copies = [
                    self.send(buffer(LOW).at[0], buffer(CORNER).at[0], HIGH),
                    self.send(buffer(HIGH).at[1], buffer(CORNER).at[1], LOW),
                ]

            def finish():
                for copy in copies:
                    copy.wait()

        self.open[pack, step] = finish

    def fetch(self, columns, terms):
        held = self.ref[HELD, columns]
        loads = [self.local(term, held.at[at]) for at, term in enumerate(terms)]
        for load in loads:
            load.wait()
        return lambda at: held[at].astype(F32)

    def reduce(self, pack, step):
        ref = self.ref
        buffer = lambda part: ref[pack, part]
        if step == 7:
            ends = buffer(ENDS)
            columns = ends.shape[2]
            term = self.fetch(columns, [ends.at[0], ends.at[1]])
            result = ref[RESULT, columns, pack]
            result[...] = term(0) + term(1)
            return self.local(result, buffer(RESULT)).wait
        depth, columns = buffer(GRAD).shape[0] // 8, buffer(GRAD).shape[1]
        block = lambda at: buffer(GRAD).at[at * depth : (at + 1) * depth]
        sums = ref[SUMS, pack]
        if step == 5:
            from_low, from_high = buffer(FROM_LOW), buffer(FROM_HIGH)
            corners = [buffer(CORNERS).at[at] for at in range(2)]
            copies = [
                self.send(block(3), from_low.at[1], LOW),
                self.send(block(4), from_high.at[0], HIGH),
            ]
            term = self.fetch(columns, [block(2), block(5), *corners])
            for at in range(2):
                sums[at] = (term(at) + term(2 + at)).astype(BF16)
            copies.append(self.send(sums.at[0], from_low.at[0], LOW))
            copies.append(self.send(sums.at[1], from_high.at[1], HIGH))

            def finish():
                for copy in copies:
                    copy.wait()

            return finish
        ends, sides = buffer(ENDS), (buffer(FROM_LOW), buffer(FROM_HIGH))
        term = self.fetch(
            columns, [block(0), block(1)] + [side.at[at] for side in sides for at in range(2)]
        )
        for at in range(2):
            sums[at] = (term(at) + term(2 + at) + term(4 + at)).astype(BF16)
        first, second = self.slot(), self.slot()
        copy = self.near(sums.at[0], ends.at[0])
        self.locals += 1
        beside = lambda: self.remote(sums.at[1], ends.at[0], CORE, first)
        over = lambda: self.remote(sums.at[0], ends.at[1], DIAGONAL, second)
        across = lambda: self.remote(sums.at[1], ends.at[1], CROSS, first, second)

        def start_aligned():
            copy.start()
            beside().start()

        def start_other():
            over().start()
            across().start()

        def wait_aligned():
            copy.wait()
            beside().wait_send()
            over().wait_recv()

        def wait_other():
            over().wait()
            across().wait_send()
            beside().wait_recv()

        pl.when(self.aligned)(start_aligned)
        pl.when(jnp.logical_not(self.aligned))(start_other)

        def finish():
            pl.when(self.aligned)(wait_aligned)
            pl.when(jnp.logical_not(self.aligned))(wait_other)

        return finish

    def finish(self, pack, step):
        finish = self.open.pop((pack, step), None)
        if finish is not None:
            finish()

    def finish_all(self):
        for finish in self.open.values():
            finish()
        self.open = {}


PACK_PARTS = {
    1: (PAIR,),
    2: (LOW, HIGH),
    3: (CORNER,),
    4: (CORNERS,),
    5: (FROM_LOW, FROM_HIGH),
    6: (ENDS,),
    7: (RESULT,),
}
PACK_NEEDS = {
    1: (MINE,),
    2: (PAIR,),
    3: (LOW, HIGH),
    4: (GRAD,),
    5: (GRAD, CORNERS),
    6: (GRAD, FROM_LOW, FROM_HIGH),
    7: (ENDS,),
}


def pack_buffers(jobs, packs):
    needs, makes, scratch = {}, {}, {}
    for pack, step in jobs:
        for part in PACK_NEEDS[step]:
            if (pack, part) not in makes:
                needs[pack, part] = packs[pack, part]
        if step < 4:
            depth, columns = packs[(pack, MINE)].shape
        else:
            depth, columns = packs[(pack, GRAD)].shape
            depth //= 8
            scratch[HELD, columns] = pltpu.VMEM((6, depth, columns), BF16)
            if step in (5, 6):
                scratch[SUMS, pack] = pltpu.VMEM((2, depth, columns), BF16)
        for part in PACK_PARTS[step]:
            made = jax.ShapeDtypeStruct((2, depth, columns), BF16)
            if part == RESULT:
                made = jax.ShapeDtypeStruct((depth, columns), F32)
                scratch[RESULT, columns, pack] = pltpu.VMEM((depth, columns), F32)
            makes[(pack, part)] = made
    return needs, makes, scratch, 4 * len(jobs), 9 * len(jobs)


def start_kernel(jobs, names, *refs):
    ref = dict(zip(names, refs))
    greeted = greet((CORE, LINE, CROSS, DIAGONAL, LOW, HIGH))
    courier = Courier(ref)
    greeted()
    facts = courier.swap(ref[FACTS_HBM], ref[ROW_FACTS_HBM])
    vector, vectors = ref[VECTOR_HBM], ref[VECTORS_HBM]
    courier.local(vector, vectors.at[0]).wait()
    rows = None
    size = 1
    for partner in (LINE, CROSS, CORE, LOW, HIGH):
        courier.send(vectors.at[0:size], vectors.at[size : 2 * size], partner).wait()
        size *= 2
        if partner == CROSS:
            courier.begin(*jobs[0])
            rows = courier.swap(ref[HIDDEN_HBM], ref[MOVED_HBM])
    for job in jobs[1:]:
        courier.begin(*job)
    rows()
    facts()
    courier.finish_all()


def start_call(collective, hidden, facts, vector, jobs, packs):
    anywhere = pl.BlockSpec(memory_space=pl.ANY)
    needs, makes, _, remote, here = pack_buffers(jobs, packs)
    shape = jax.ShapeDtypeStruct
    inputs = {HIDDEN_HBM: hidden, FACTS_HBM: facts, VECTOR_HBM: vector, **needs}
    outputs = {
        MOVED_HBM: shape(hidden.shape, hidden.dtype),
        ROW_FACTS_HBM: shape(facts.shape, facts.dtype),
        VECTORS_HBM: shape((32, *vector.shape), vector.dtype),
        **makes,
    }
    names = (*inputs, *outputs, REMOTE, HERE)
    results = pl.pallas_call(
        functools.partial(start_kernel, jobs, names),
        name="start_exchange",
        out_shape=tuple(outputs.values()),
        in_specs=[anywhere] * len(inputs),
        out_specs=(anywhere,) * len(outputs),
        scratch_shapes=[
            pltpu.SemaphoreType.DMA((2, remote + 7)),
            pltpu.SemaphoreType.DMA((here + 3,)),
        ],
        compiler_params=pltpu.CompilerParams(collective_id=collective, has_side_effects=True),
        cost_estimate=pl.CostEstimate(flops=0, bytes_accessed=64 << 20, transcendentals=0),
    )(*inputs.values())
    results = dict(zip(outputs, results))
    packs.update({name: results[name] for name in makes})
    return results


def turned(values):
    return values.astype(F32).T


def joined(pieces, axis=0):
    return pieces[0] if len(pieces) == 1 else jnp.concatenate(pieces, axis=axis)


def chain_kernel(stages, backward, names, plan, jobs, *refs):
    ref = dict(zip(names, refs))
    enter, mix, leave = stages
    value, state, own, far_own = ref[VALUE], ref[STATE], ref[OWN], ref[FAR_OWN]
    count, width = value.shape
    step = count // PARTS
    greeted = greet(tuple(partners()) if jobs or MOVED_HBM in ref else (CORE, LINE))
    courier = Courier(ref)
    send, local = courier.send, courier.local
    core, line = CORE, LINE
    waiting = list(jobs)

    def point(at):
        while waiting and waiting[0][0] <= at:
            courier.begin(*waiting.pop(0)[1:])

    def chunk(slot, part):
        return slice(slot * count + part * step, slot * count + (part + 1) * step)

    def place(part):
        return slice(part * step, (part + 1) * step)

    made = {(pack, part): (pack, at) for _, pack, at in jobs for part in PACK_PARTS[at]}
    loads = {}

    def load(name, blocks):
        return [
            local(ref[piece].at[index, :, begin:end], ref[name].at[row : row + depth, :])
            for piece, index, row, depth, begin, end in blocks
        ]

    for name, blocks in plan:
        loads[name] = load(name, [block for block in blocks if block[0] not in made])

    def loaded(name):
        late = [block for weight, blocks in plan if weight == name for block in blocks]
        late = [block for block in late if block[0] in made]
        for block in late:
            courier.finish(*made[block[0]])
        for copy in loads[name] + load(name, late):
            copy.wait()

    if mix and backward:
        loads[SLOPE] = [local(ref[SLOPE_HBM], ref[SLOPE])]
    saves = []
    if backward:
        ref[WIDE_SUMS][...] = jnp.zeros(ref[WIDE_SUMS].shape, F32)

    def add_wide(row, sums):
        if sums.ndim == 1:
            sums = sums[None]
        ref[WIDE_SUMS][row : row + 1, :] += sums

    def product(pieces, weight, stores, transposed_source=False):
        def strip(at, carry):
            columns = strips(at)
            result = mat_turned(pieces, weight[columns, : pieces.shape[1]])
            begin = 0
            for size, store in stores:
                store(columns, result[begin : begin + size])
                begin += size
            return carry

        lax.fori_loop(0, width // STRIP, strip, 0, unroll=True)

    def put(target, index):
        def store(columns, result):
            target[index, :, columns] = result.astype(target.dtype)

        return store

    def scatter(prefix, source, weight):
        far_out, far_in = ref[prefix, FAR_OUT], ref[prefix, FAR_IN]
        line_out, line_in = ref[prefix, LINE_OUT], ref[prefix, LINE_IN]
        near_out, near_in = ref[prefix, NEAR_OUT], ref[prefix, NEAR_IN]

        def far(part):
            product(
                source([(2, part), (3, part)]),
                weight,
                [(step, put(far_own, part)), (step, put(far_out, part))],
            )
            return send(far_out.at[part], far_in.at[part], core)

        def pass_on(part, passing):
            passing.wait()
            line_out[part] = (far_own[part] + far_in[part].astype(F32)).astype(BF16)
            return send(line_out.at[part], line_in.at[part], line)

        def near():
            product(
                source([(1, part) for part in range(PARTS)]),
                weight,
                [(step, put(near_out, part)) for part in range(PARTS)],
            )
            return send(near_out, near_in, core)

        def mine():
            product(
                source([(0, part) for part in range(PARTS)]),
                weight,
                [(step, put(own, part)) for part in range(PARTS)],
            )

        def total(part):
            return own[part] + near_in[part].astype(F32) + line_in[part].astype(F32)

        return far, pass_on, near, mine, total

    def lower(values, gain, shift):
        if backward:
            return values.astype(BF16)
        return (normalise(values)[0] * gain[...] + shift[...]).astype(BF16)

    def begin_rows(rows, part):
        near = send(rows.at[chunk(0, part)], rows.at[chunk(1, part)], core)
        far = send(rows.at[chunk(0, part)], rows.at[chunk(2, part)], line)
        return near, far

    def forward_rows(rows, part, far):
        far.wait()
        return send(rows.at[chunk(2, part)], rows.at[chunk(3, part)], core)

    ready = None
    if enter:
        source_t = ref[SOURCE]

        def entering(pieces):
            return turned(joined([source_t[:, chunk(*piece)] for piece in pieces], 1)).astype(BF16)

        far, pass_on, near, mine, total = scatter(ENTER, entering, ref[ENTER_W])
        loaded(ENTER_W)
        greeted()
        point(0)
        if COTANGENT_HBM in ref:
            moved = courier.swap(ref[COTANGENT_HBM], ref[MOVED_HBM])
        passing = [far(part) for part in range(PARTS)]
        lines = [pass_on(part, passing[part]) for part in range(PARTS)]
        near_sum = near()
        mine()
        point(1)
        near_sum.wait()
        point(2)

        def ready(part):
            lines[part].wait()
            at = place(part)
            if backward:
                grad, gains, shifts = norm_backward(
                    ref[ENTER_AT][at, :], ref[ENTER_GAIN][...], total(part)
                )
                state[at, :] = value[at, :] + grad
                add_wide(0, gains)
                add_wide(1, shifts)
            else:
                state[at, :] = value[at, :] + (total(part) + ref[ENTER_BIAS][...])
            ref[ENTERED][at, :] = state[at, :]

    else:
        greeted()
        point(0)

        if COTANGENT in ref:
            lowered = mat(value[...].astype(BF16), ref[REORDER][...])
            ref[ROWS_OUT][...] = lowered.astype(BF16)
            moved = courier.swap(ref[ROWS_OUT], ref[MOVED_HBM])
            state[...] = mat(ref[COTANGENT][...], ref[REORDER][...])

        def ready(part):
            at = place(part)
            if COTANGENT not in ref:
                state[at, :] = value[at, :]

    if mix:
        rows, act, slope = ref[ROWS], ref[ACT], ref[SLOPE]
        first, second = ref[FIRST], ref[SECOND]
        units = first.shape[1]
        if backward:
            ref[UNIT_SUMS][...] = jnp.zeros(ref[UNIT_SUMS].shape, F32)
        begun = []
        for part in range(PARTS):
            ready(part)
            lowered = lower(
                state[place(part), :], ref.get(MIX_GAIN), ref.get(MIX_SHIFT)
            )
            rows[chunk(0, part), :] = lowered
            begun.append(begin_rows(rows, part))
            if backward:
                add_wide(2, jnp.sum(lowered.astype(F32), axis=0))

        def expand(pieces):
            taken = joined([rows[chunk(*piece), :] for piece in pieces])

            def strip(at, carry):
                columns = strips(at)
                up = mat(taken, first[:, columns])
                tilt = None
                if backward:
                    slopes = joined([slope[chunk(*piece), columns] for piece in pieces])
                    out = (up * slopes.astype(F32)).astype(BF16)
                    ref[UNIT_SUMS][:, columns] += jnp.sum(
                        out.astype(F32), axis=0, keepdims=True
                    )
                else:
                    up = up + ref[FIRST_BIAS][:, columns]
                    sigmoid = 1.0 / (1.0 + jnp.exp(-1.702 * up))
                    out = (up * sigmoid).astype(BF16)
                    tilt = (sigmoid + 1.702 * up * sigmoid * (1.0 - sigmoid)).astype(BF16)
                for index, piece in enumerate(pieces):
                    at_rows = slice(index * step, (index + 1) * step)
                    act[chunk(*piece), columns] = out[at_rows]
                    if tilt is not None:
                        slope[chunk(*piece), columns] = tilt[at_rows]
                return carry

            lax.fori_loop(0, units // STRIP, strip, 0, unroll=True)

        def acting(pieces):
            return joined([act[chunk(*piece), :] for piece in pieces])

        far, pass_on, near, mine, total = scatter(MIX, acting, second)
        loaded(FIRST)
        if backward:
            loaded(SLOPE)
        expand([(0, part) for part in range(PARTS)])
        for part in range(PARTS):
            begun[part][0].wait()
        point(3)
        expand([(1, part) for part in range(PARTS)])
        loaded(SECOND)
        near_sum = near()
        point(4)
        forwards = [forward_rows(rows, 0, begun[0][1])]
        mine()
        lines = []
        for part in range(PARTS):
            forwards[part].wait()
            expand([(2, part), (3, part)])
            lines.append(pass_on(part, far(part)))
            if part + 1 < PARTS:
                forwards.append(forward_rows(rows, part + 1, begun[part + 1][1]))
            point(5 + part)
        saves.append(local(rows, ref[ROWS_HBM]))
        saves.append(local(act, ref[ACT_HBM]))
        if not backward:
            saves.append(local(slope, ref[SLOPE_HBM]))
        near_sum.wait()

        def ready(part):
            lines[part].wait()
            at = place(part)
            if backward:
                grad, gains, shifts = norm_backward(
                    ref[MIX_AT][at, :], ref[MIX_GAIN][...], total(part)
                )
                state[at, :] = state[at, :] + grad
                add_wide(3, gains)
                add_wide(4, shifts)
            else:
                state[at, :] = state[at, :] + (total(part) + ref[SECOND_BIAS][...])
            ref[MIXED][at, :] = state[at, :]

    if leave:
        rows2, weight, target = ref[ROWS2], ref[LEAVE_W], ref[TARGET]
        begun = []
        for part in range(PARTS):
            ready(part)
            lowered = lower(
                state[place(part), :], ref.get(LEAVE_GAIN), ref.get(LEAVE_SHIFT)
            )
            rows2[chunk(0, part), :] = lowered
            begun.append(begin_rows(rows2, part))
            if backward:
                add_wide(5, jnp.sum(lowered.astype(F32), axis=0))

        def leaving(pieces):
            result = mat(joined([rows2[chunk(*piece), :] for piece in pieces]), weight[...])
            if not backward:
                result = result + ref[LEAVE_BIAS][...]
            result = turned(result)
            if not backward:
                cos, sin = (
                    joined([ref[name][:, chunk(*piece)] for piece in pieces], 1)
                    for name in (COSINE, SINE)
                )
                half, third = HD // 2, result.shape[0] // 3
                blocks = []
                for base in range(0, 2 * third, HD):
                    low, high = result[base : base + half], result[base + half : base + HD]
                    blocks += [low * cos - high * sin, high * cos + low * sin]
                result = jnp.concatenate(blocks + [result[2 * third :]], axis=0)
            result = result.astype(BF16)
            for index, piece in enumerate(pieces):
                target[:, chunk(*piece)] = result[:, index * step : (index + 1) * step]

        loaded(LEAVE_W)
        point(7)
        leaving([(0, part) for part in range(PARTS)])
        for part in range(PARTS):
            begun[part][0].wait()
        leaving([(1, part) for part in range(PARTS)])
        point(8)
        forwards = [forward_rows(rows2, part, begun[part][1]) for part in range(PARTS)]
        for part in range(PARTS):
            forwards[part].wait()
            leaving([(2, part), (3, part)])
        saves.append(local(rows2, ref[ROWS2_HBM]))
    else:
        for part in range(PARTS):
            ready(part)
    if REORDER in ref and COTANGENT not in ref:
        lowered = mat(state[...].astype(BF16), ref[REORDER][...]).astype(BF16)
        rows_out = ref[ROWS_OUT]
        rows_out[...] = lowered
        moved = courier.swap(rows_out, ref[MOVED_HBM])
    point(9)
    if MOVED_HBM in ref:
        moved()
    for save in saves:
        save.wait()
    courier.finish_all()


class Weight:
    def __init__(self, pack, begin, end):
        self.pack, self.begin, self.end = pack, begin, end


def chain_call(stages, backward, collective, operands, packs, jobs=()):
    enter, mix, leave = stages
    count, width = operands[VALUE].shape
    step = count // PARTS
    shape = jax.ShapeDtypeStruct
    vmem, anywhere = pl.BlockSpec(memory_space=pltpu.VMEM), pl.BlockSpec(memory_space=pl.ANY)
    outputs, scratch = {}, {}
    buffers = lambda kind: pltpu.VMEM((PARTS, step, width), kind)
    scratch[STATE] = pltpu.VMEM((count, width), F32)
    scratch[OWN] = buffers(F32)
    scratch[FAR_OWN] = buffers(F32)
    remote, here = 0, 0
    if backward:
        outputs[WIDE_SUMS] = shape((8, width), F32)
    flops = 0
    plan = []
    passed = {}
    needs, makes, job_scratch, job_remote, job_here = pack_buffers([job[1:] for job in jobs], packs)
    scratch.update(job_scratch)
    remote, here = remote + job_remote, here + job_here
    for name, value in operands.items():
        if not isinstance(value, Weight):
            passed[name] = value
            continue
        blocks, row = [], 0
        for part in (PAIR, LOW, HIGH, CORNER, ONE, OTHER, ALL):
            piece = (value.pack, part)
            if piece not in packs and piece not in makes:
                continue
            if piece not in makes:
                passed[piece] = packs[piece]
            array = makes.get(piece, packs.get(piece))
            for index in range(array.shape[0]):
                blocks.append((piece, index, row, array.shape[1], value.begin, value.end))
                row += array.shape[1]
        plan.append((name, blocks))
        scratch[name] = pltpu.VMEM((width, value.end - value.begin), BF16)
        here += len(blocks)
        flops += 8 * count * width * (value.end - value.begin)
    passed.update({name: value for name, value in needs.items() if name not in passed})
    outputs.update(makes)
    for stage, prefix in ((enter, ENTER), (mix, MIX)):
        if stage:
            for name in (FAR_OUT, FAR_IN, LINE_OUT, LINE_IN, NEAR_OUT, NEAR_IN):
                scratch[prefix, name] = buffers(BF16)
            remote += 2 * PARTS + 1
    if enter:
        outputs[ENTERED] = shape((count, width), F32)
    if mix:
        units = operands[FIRST].end - operands[FIRST].begin
        scratch[ROWS] = pltpu.VMEM((4 * count, width), BF16)
        scratch[ACT] = pltpu.VMEM((4 * count, units), BF16)
        scratch[SLOPE] = pltpu.VMEM((4 * count, units), BF16)
        outputs[MIXED] = shape((count, width), F32)
        outputs[ROWS_HBM] = shape((4 * count, width), BF16)
        outputs[ACT_HBM] = shape((4 * count, units), BF16)
        if backward:
            outputs[UNIT_SUMS] = shape((1, units), F32)
        else:
            outputs[SLOPE_HBM] = shape((4 * count, units), BF16)
        remote += 3 * PARTS
        here += 3
    if leave:
        columns = leave
        scratch[ROWS2] = pltpu.VMEM((4 * count, width), BF16)
        outputs[TARGET] = shape((columns, 4 * count), BF16)
        outputs[ROWS2_HBM] = shape((4 * count, width), BF16)
        remote += 3 * PARTS
        here += 1
    if REORDER in operands or COTANGENT_HBM in operands:
        if REORDER in operands:
            scratch[ROWS_OUT] = pltpu.VMEM((count, width), BF16)
        outputs[MOVED_HBM] = shape((count, width), BF16)
        remote, here = remote + 1, here + 1
    scratch[REMOTE] = pltpu.SemaphoreType.DMA((2, remote))
    scratch[HERE] = pltpu.SemaphoreType.DMA((here,))
    names = tuple(passed) + tuple(outputs) + tuple(scratch)
    spec = lambda name: anywhere if isinstance(name, tuple) or name >= FIRST_HBM else vmem
    results = pl.pallas_call(
        functools.partial(chain_kernel, stages, backward, names, plan, jobs),
        name="chain_backward" if backward else "chain_forward",
        out_shape=tuple(outputs.values()),
        in_specs=[spec(name) for name in passed],
        out_specs=tuple(spec(name) for name in outputs),
        scratch_shapes=list(scratch.values()),
        compiler_params=pltpu.CompilerParams(
            collective_id=collective, has_side_effects=True, vmem_limit_bytes=54 << 20
        ),
        cost_estimate=pl.CostEstimate(
            flops=flops, bytes_accessed=(16 << 20) * sum(map(bool, stages)), transcendentals=0
        ),
    )(*passed.values())
    results = dict(zip(outputs, results))
    packs.update({name: results[name] for name in makes})
    return results


def make_body(dp, mp):
    assert mp == 4 and dp >= 2 and dp & (dp - 1) == 0
    count = dp * mp
    high_bits = [1 << b for b in range(1, dp.bit_length() - 1)]

    def across(value, bit):
        return lax.ppermute(value, "dp", [(i, i ^ bit) for i in range(dp)])

    def core_side(value):
        return across(value, 1)

    def line_side(value):
        return lax.ppermute(value, "mp", [(i, i ^ 1) for i in range(mp)])

    def swapped(d, m):
        return (d & ~1 | m >> 1) * mp + ((d & 1) << 1 | m & 1)

    swap_pairs = [
        (d * mp + m, swapped(d, m)) for d in range(dp) for m in range(mp) if d & 1 != m >> 1
    ]

    def swap(value):
        stays = (lax.axis_index("dp") & 1) == (lax.axis_index("mp") >> 1)
        return jnp.where(stays, value, lax.ppermute(value, ("dp", "mp"), swap_pairs))

    balanced = len(high_bits) == 2

    def gather_pair(mine):
        return swap(jnp.stack([mine, core_side(mine)]))

    def gather_sides(pair):
        for bit in high_bits:
            pair = jnp.concatenate([pair, across(pair, bit)], axis=0)
        return (pair,)

    def add(*terms):
        total = terms[0].astype(F32)
        for term in terms[1:]:
            total = total + term.astype(F32)
        return total.astype(BF16)

    def scatter_blocks(grad):
        total = grad.reshape(dp, D // dp, -1)
        for bit in high_bits[::-1]:
            half = total.shape[0] // 2
            total = add(total[:half], across(total[half:], bit))
        total = swap(total)
        return total[0].astype(F32) + core_side(total[1]).astype(F32)

    def arranged(values):
        index = lax.axis_index("dp") * mp + lax.axis_index("mp")
        at = jnp.arange(count, dtype=jnp.int32)
        order = (at[:, None] ^ index) == at[None, :]
        return dot(order.astype(F32), values, 1, 0, precision=HIGHEST)

    def gather_vectors(mine):
        values = mine[None]
        bit = 1
        while bit < count:
            if bit >= mp:
                got = across(values, bit // mp)
            else:
                got = lax.ppermute(values, "mp", [(i, i ^ bit) for i in range(mp)])
            values = jnp.concatenate([values, got], axis=0)
            bit *= 2
        return arranged(values)

    def scatter_vectors(values):
        index = lax.axis_index("dp") * mp + lax.axis_index("mp")
        bit = count // 2
        while bit:
            half = values.shape[0] // 2
            top = (index & bit) != 0
            low, high = values[:half], values[half:]
            sent = jnp.where(top, low, high)
            if bit >= mp:
                got = across(sent, bit // mp)
            else:
                got = lax.ppermute(sent, "mp", [(i, i ^ bit) for i in range(mp)])
            values = jnp.where(top, high, low) + got
            bit //= 2
        return values[0]

    def body(
        hidden_in,
        pre_gain,
        pre_bias,
        qkv_weight,
        qkv_bias,
        proj_weight,
        proj_bias,
        mid_gain,
        mid_bias,
        up_weight,
        up_bias,
        down_weight,
        down_bias,
        picture_ids,
        positions,
        pad_mask,
        cotangent,
    ):
        dp_at, mp_at = lax.axis_index("dp"), lax.axis_index("mp")
        group_at = (dp_at & ~1) | (mp_at >> 1)
        quarter_at = ((dp_at & 1) << 1) | (mp_at & 1)
        depth = D // dp
        columns = qkv_weight.shape[3]
        units = up_weight.shape[2]
        heads = columns // HD

        place = jnp.arange(D, dtype=jnp.int32)
        moved = ((place // depth) ^ group_at) * depth + place % depth
        reorder = place[:, None] == moved[None, :]
        reorder_low = reorder.astype(BF16)
        reorder_full = reorder.astype(F32)

        def turn_low(values):
            return dot(values.astype(BF16), reorder_low, 1, 0)

        qkv_width, proj_width = 3 * columns, columns
        packs = {}
        for layer in range(LAYERS):
            mine = qkv_weight[layer].transpose(1, 0, 2).reshape(depth, qkv_width)
            packs[(QKV, layer), MINE] = mine
            packs[(PROJ, layer), MINE] = proj_weight[layer].T
            packs[(UP, layer), MINE] = up_weight[layer]
            packs[(DOWN, layer), MINE] = down_weight[layer].T

        wide = (pre_gain, pre_bias, proj_bias, mid_gain, mid_bias, down_bias)
        packed = jnp.concatenate(
            [item.reshape(-1) for item in wide] + [qkv_bias.reshape(-1), up_bias.reshape(-1)]
        )
        length = picture_ids.shape[0]
        quarter = length // mp
        row_at = jnp.arange(length, dtype=jnp.int32)
        codes = jnp.where(pad_mask == 1, picture_ids, 1024 + row_at)
        row_facts = jnp.concatenate([codes[None], positions], axis=0)
        hidden = hidden_in.astype(BF16)
        jobs = {}
        if balanced:
            space = -(-packed.shape[0] // 1024) * 1024
            late = packs[(QKV, 1), MINE], packs[(DOWN, 1), MINE], packs[(PROJ, 1), MINE]
            hidden, late = lax.optimization_barrier((hidden, late))
            packs[(QKV, 1), MINE], packs[(DOWN, 1), MINE], packs[(PROJ, 1), MINE] = late
            begun = start_call(
                3 * LAYERS + 1,
                hidden,
                jnp.pad(row_facts, ((0, 5), (0, 0))),
                jnp.pad(packed, (0, space - packed.shape[0])).reshape(-1, 128),
                (((QKV, 0), 1), ((QKV, 0), 2), ((PROJ, 0), 1), ((UP, 0), 1), ((QKV, 0), 3)),
                packs,
            )
            hidden, row_facts = begun[MOVED_HBM], begun[ROW_FACTS_HBM][:3]
            packed = arranged(begun[VECTORS_HBM].reshape(count, space))[:, : packed.shape[0]]
            schedule = {
                (LEAVE, 0): {
                    0: ((UP, 0, 2), (PROJ, 0, 2), (DOWN, 0, 1)),
                    8: ((PROJ, 0, 3),),
                },
                (FORWARD, 0): {
                    0: ((DOWN, 0, 2), (QKV, 1, 1)),
                    2: ((DOWN, 0, 3), (PROJ, 1, 1)),
                    4: ((QKV, 1, 2), (PROJ, 1, 2), (UP, 1, 1)),
                    6: ((QKV, 1, 3), (PROJ, 1, 3)),
                },
                (LEAVE, 1): {0: ((UP, 1, 2), (DOWN, 1, 1))},
                (FORWARD, 1): {0: ((DOWN, 1, 2),), 2: ((DOWN, 1, 3),)},
                (BACKWARD, 0): {
                    0: ((UP, 1, 4), (DOWN, 1, 4)),
                    1: ((UP, 1, 5),),
                    4: ((DOWN, 1, 5), (QKV, 1, 4), (PROJ, 1, 4)),
                    5: ((UP, 1, 6),),
                    8: ((DOWN, 1, 6), (QKV, 1, 5), (PROJ, 1, 5)),
                },
                (BACKWARD, FINAL): {
                    0: ((UP, 0, 4), (DOWN, 0, 4)),
                    1: ((UP, 0, 5),),
                    2: ((QKV, 1, 6), (PROJ, 1, 6), (QKV, 0, 4), (PROJ, 0, 4)),
                    9: (
                        *((UP, 0, 6), (DOWN, 0, 5), (QKV, 0, 5), (UP, 1, 7), (DOWN, 1, 7)),
                        *((DOWN, 0, 6), (PROJ, 0, 5), (QKV, 1, 7), (PROJ, 1, 7), (UP, 0, 7)),
                        *((QKV, 0, 6), (PROJ, 0, 6), (DOWN, 0, 7), (QKV, 0, 7), (PROJ, 0, 7)),
                    ),
                },
            }
            jobs = {
                kernel: tuple(
                    (at, (name, layer), step)
                    for at, steps in points.items()
                    for name, layer, step in steps
                )
                for kernel, points in schedule.items()
            }
        else:
            for name in list(packs):
                packs[name[0], ALL] = gather_sides(gather_pair(packs[name]))[0].reshape(1, D, -1)
            hidden, row_facts, packed = swap(hidden), swap(row_facts), gather_vectors(packed)
        hidden = turn_low(hidden)
        each = D // count
        wide_count = len(wide) * LAYERS
        split = (wide_count + 3 * LAYERS) * each
        vectors = packed[:, :split].reshape(count, -1, each).transpose(1, 0, 2).reshape(-1, D)
        wide_all = dot(vectors[:wide_count], reorder_full, 1, 0, precision=HIGHEST)
        wide_all = wide_all.reshape(len(wide), LAYERS, D)
        pre_gain_all, pre_bias_all, proj_bias_all, mid_gain_all, mid_bias_all, down_bias_all = (
            wide_all[i] for i in range(len(wide))
        )
        qkv_bias_mine = lax.dynamic_slice_in_dim(
            vectors[wide_count:], quarter_at * columns, columns, 1
        ).reshape(LAYERS, 3 * columns)
        up_all = packed[:, split:].reshape(count, LAYERS, -1).transpose(1, 0, 2)
        up_bias_mine = lax.dynamic_slice_in_dim(
            up_all.reshape(LAYERS, -1), quarter_at * units, units, 1
        )

        row_facts = jnp.concatenate(
            [
                lax.dynamic_slice_in_dim(row_facts, (quarter_at ^ which) * quarter, quarter, 1)
                for which in (0, 2, 1, 3)
            ],
            axis=1,
        )
        codes = row_facts[0]
        facts = (tile_overlap(codes), *rotary_tables(row_facts[1:]), codes[None], codes[:, None])

        row = lambda vector: vector[None]
        weights = [
            (
                Weight((QKV, layer), 0, qkv_width),
                Weight((PROJ, layer), 0, proj_width),
                Weight((UP, layer), 0, units),
                Weight((DOWN, layer), 0, units),
            )
            for layer in range(LAYERS)
        ]

        def leave_forward(layer):
            return {
                LEAVE_W: weights[layer][0],
                LEAVE_GAIN: row(pre_gain_all[layer]),
                LEAVE_SHIFT: row(pre_bias_all[layer]),
                LEAVE_BIAS: row(qkv_bias_mine[layer]),
                COSINE: facts[1],
                SINE: facts[2],
            }

        def call_leave(layer, value):
            return chain_call(
                (False, False, qkv_width),
                False,
                layer,
                {VALUE: value, **leave_forward(layer)},
                packs,
                jobs.get((LEAVE, layer), ()),
            )

        def call_forward(layer, value, mixed, more):
            return chain_call(
                (True, True, False),
                False,
                LAYERS + layer,
                {
                    VALUE: value,
                    SOURCE: mixed,
                    ENTER_W: weights[layer][1],
                    ENTER_BIAS: row(proj_bias_all[layer]),
                    FIRST: weights[layer][2],
                    SECOND: weights[layer][3],
                    FIRST_BIAS: row(up_bias_mine[layer]),
                    SECOND_BIAS: row(down_bias_all[layer]),
                    MIX_GAIN: row(mid_gain_all[layer]),
                    MIX_SHIFT: row(mid_bias_all[layer]),
                    **more,
                },
                packs,
                jobs.get((FORWARD, layer), ()),
            )

        def call_backward(layer, value, entering, middle, slope, more):
            return chain_call(
                (bool(entering), True, proj_width),
                True,
                2 * LAYERS + layer,
                {
                    VALUE: value,
                    **entering,
                    **more,
                    FIRST: weights[layer][3],
                    SECOND: weights[layer][2],
                    SLOPE_HBM: slope,
                    MIX_AT: middle,
                    MIX_GAIN: row(mid_gain_all[layer]),
                    LEAVE_W: weights[layer][1],
                },
                packs,
                jobs.get((BACKWARD, layer), ()),
            )

        def entering(layer, grad_linear, start):
            return {
                SOURCE: grad_linear,
                ENTER_W: weights[layer][0],
                ENTER_AT: start,
                ENTER_GAIN: row(pre_gain_all[layer]),
            }

        def beside_forward(layer):
            if not balanced:
                return
            low, high = high_bits
            up = (UP, layer)
            packs[up, ONE] = across(packs[up, LOW][:1], high)
            packs[up, OTHER] = across(packs[up, HIGH][1:], low)

        hidden, wide_all, qkv_bias_mine, up_bias_mine, facts = lax.optimization_barrier(
            (hidden, wide_all, qkv_bias_mine, up_bias_mine, facts)
        )
        pre_gain_all, pre_bias_all, proj_bias_all, mid_gain_all, mid_bias_all, down_bias_all = (
            wide_all[i] for i in range(len(wide))
        )
        leave0 = call_leave(0, hidden)
        beside_forward(0)
        qkv0 = leave0[TARGET]
        mixed0, log_sum0 = attend_forward(qkv0, facts)
        state0 = call_forward(0, hidden, mixed0, {})
        start1 = state0[MIXED]
        leave1 = call_leave(1, start1)
        beside_forward(1)
        qkv1 = leave1[TARGET]
        mixed1, log_sum1 = attend_forward(qkv1, facts)
        cotangent = cotangent.astype(BF16)
        if balanced:
            state1 = call_forward(1, start1, mixed1, {COTANGENT_HBM: cotangent})
            back1 = call_backward(
                1,
                state1[MIXED],
                {},
                state1[ENTERED],
                state1[SLOPE_HBM],
                {COTANGENT: state1[MOVED_HBM], REORDER: reorder_low},
            )
            out_hidden = back1[MOVED_HBM]
        else:
            state1 = call_forward(1, start1, mixed1, {})
            out_hidden = swap(turn_low(state1[MIXED]).astype(BF16))
            gradient = turn_low(swap(cotangent))
            back1 = call_backward(1, gradient, {}, state1[ENTERED], state1[SLOPE_HBM], {})
        packs[(UP, 1), GRAD] = grad_dot(state1[ROWS_HBM], back1[ACT_HBM], 0, 0)
        packs[(DOWN, 1), GRAD] = grad_dot(back1[ROWS_HBM], state1[ACT_HBM], 0, 0)
        linear1 = attend_backward(qkv1, mixed1, back1[TARGET], log_sum1, facts)
        packs[(QKV, 1), GRAD] = grad_dot(leave1[ROWS2_HBM], linear1, 0, 1)
        packs[(PROJ, 1), GRAD] = grad_dot(back1[ROWS2_HBM], mixed1, 0, 1)
        back0 = call_backward(
            0,
            back1[MIXED],
            entering(1, linear1, start1),
            state0[ENTERED],
            state0[SLOPE_HBM],
            {},
        )
        packs[(UP, 0), GRAD] = grad_dot(state0[ROWS_HBM], back0[ACT_HBM], 0, 0)
        packs[(DOWN, 0), GRAD] = grad_dot(back0[ROWS_HBM], state0[ACT_HBM], 0, 0)
        target0, packs[(UP, 0), GRAD], packs[(DOWN, 0), GRAD] = lax.optimization_barrier(
            (back0[TARGET], packs[(UP, 0), GRAD], packs[(DOWN, 0), GRAD])
        )
        linear0 = attend_backward(qkv0, mixed0, target0, log_sum0, facts)
        packs[(QKV, 0), GRAD] = grad_dot(leave0[ROWS2_HBM], linear0, 0, 1)
        packs[(PROJ, 0), GRAD] = grad_dot(back0[ROWS2_HBM], mixed0, 0, 1)
        final = chain_call(
            (True, False, False),
            True,
            3 * LAYERS,
            {
                VALUE: back0[MIXED],
                **entering(0, linear0, hidden),
                **({REORDER: reorder_low} if balanced else {}),
            },
            packs,
            jobs.get((BACKWARD, FINAL), ()),
        )
        if balanced:
            grad_hidden = final[MOVED_HBM].astype(F32)
        else:
            grad_hidden = swap(turn_low(final[ENTERED]).astype(BF16)).astype(F32)
            for name in list(packs):
                if name[1] == GRAD:
                    packs[name[0], RESULT] = scatter_blocks(packs[name])
        out_hidden = out_hidden.astype(F32)
        grads, parts = [], []
        for layer, back, linear in ((0, back0, linear0), (1, back1, linear1)):
            result = lambda which: packs[(which, layer), RESULT]
            grads.append(
                (
                    result(QKV).reshape(depth, 3, columns).transpose(1, 0, 2),
                    result(PROJ).T,
                    result(UP),
                    result(DOWN).T,
                )
            )
            qkv_bias_part = jnp.sum(linear.astype(F32), axis=1)
            parts.append((qkv_bias_part.reshape(3, columns), back[UNIT_SUMS][0]))
        sums = [back1[WIDE_SUMS], back0[WIDE_SUMS], final[WIDE_SUMS]]

        stacked = jnp.stack(
            [
                sums[LAYERS - layer - which][at]
                for which, at in ((0, 0), (0, 1), (1, 5), (1, 3), (1, 4), (1, 2))
                for layer in range(LAYERS)
            ]
        )
        stacked = dot(stacked, reorder_full, 1, 0, precision=HIGHEST)
        qkv_padded = lax.dynamic_update_slice_in_dim(
            jnp.zeros((LAYERS * 3, D), F32),
            jnp.concatenate([part[0] for part in parts], axis=0),
            quarter_at * columns,
            1,
        )
        up_padded = lax.dynamic_update_slice_in_dim(
            jnp.zeros((LAYERS, units * mp), F32),
            jnp.stack([part[1] for part in parts]),
            quarter_at * units,
            1,
        )
        by_owner = jnp.concatenate([stacked, qkv_padded], axis=0).reshape(-1, count, each)
        by_owner = jnp.concatenate(
            [
                by_owner.transpose(1, 0, 2).reshape(count, -1),
                up_padded.reshape(LAYERS, count, -1).transpose(1, 0, 2).reshape(count, -1),
            ],
            axis=1,
        )
        mine = scatter_vectors(by_owner)
        wide_grads = mine[: wide_count * each].reshape(len(wide), LAYERS, each)
        qkv_bias_grad = mine[wide_count * each : split].reshape(LAYERS, 3, each)
        up_bias_grad = mine[split:].reshape(LAYERS, -1)
        matrices = [jnp.stack([entry[i] for entry in grads]) for i in range(4)]
        return (
            out_hidden,
            grad_hidden,
            wide_grads[0],
            wide_grads[1],
            matrices[0],
            qkv_bias_grad,
            matrices[1],
            wide_grads[2],
            wide_grads[3],
            wide_grads[4],
            matrices[2],
            up_bias_grad,
            matrices[3],
            wide_grads[5],
        )

    return body


def solution(mesh):
    rows = P(("dp", "mp"), None)
    vector = P(None, ("dp", "mp"))
    vectors = P(None, None, ("dp", "mp"))
    qkv = P(None, None, "dp", "mp")
    tall = P(None, "mp", "dp")
    broad = P(None, "dp", "mp")
    return jax.shard_map(
        make_body(mesh.shape["dp"], mesh.shape["mp"]),
        mesh=mesh,
        in_specs=(
            rows,
            vector,
            vector,
            qkv,
            vectors,
            tall,
            vector,
            vector,
            vector,
            broad,
            vector,
            tall,
            vector,
            P("dp"),
            P(None, "dp"),
            P("dp"),
            rows,
        ),
        out_specs=(
            rows,
            rows,
            vector,
            vector,
            qkv,
            vectors,
            tall,
            vector,
            vector,
            vector,
            broad,
            vector,
            tall,
            vector,
        ),
        check_vma=False,
    )
```

```python
import functools

import jax
import jax.numpy as jnp
from jax import lax
from jax.experimental import pallas as pl
from jax.experimental.layout import Layout, with_layout_constraint
from jax.experimental.pallas import tpu as pltpu
from jax.sharding import PartitionSpec as P

D = 1280
HD = 80
LAYERS = 2
EPSILON = 1e-06
AXES = ("dp", "mp")
F32 = jnp.float32
BF16 = jnp.bfloat16
HIGHEST = lax.Precision.HIGHEST


def normalise(values):
    centre = values - jnp.mean(values, axis=-1, keepdims=True)
    spread = jnp.mean(centre * centre, axis=-1, keepdims=True)
    scale = lax.rsqrt(spread + EPSILON)
    return centre * scale, scale


def norm_backward(values, gain, grad):
    normed, scale = normalise(values)
    inner = grad * gain
    mean_inner = jnp.mean(inner, axis=-1, keepdims=True)
    mean_cross = jnp.mean(inner * normed, axis=-1, keepdims=True)
    grad_values = scale * (inner - mean_inner - normed * mean_cross)
    return grad_values, jnp.sum(grad * normed, axis=0), jnp.sum(grad, axis=0)


def dot(left, right, left_dim, right_dim, kind=F32, precision=None):
    return lax.dot_general(
        left,
        right,
        (((left_dim,), (right_dim,)), ((), ())),
        preferred_element_type=F32,
        precision=precision,
    ).astype(kind)


def grad_dot(left, right, left_dim, right_dim):
    return with_layout_constraint(dot(left, right, left_dim, right_dim, BF16), Layout((0, 1)))


def rotary_tables(coords):
    quarter = HD // 4
    powers = jnp.arange(quarter, dtype=F32) * (4.0 / HD)
    inverse = 10000.0 ** (-powers)
    height_angle = inverse[:, None] * coords[0].astype(F32)[None, :]
    width_angle = inverse[:, None] * coords[1].astype(F32)[None, :]
    angles = jnp.concatenate([height_angle, width_angle], axis=0)
    return (jnp.cos(angles), jnp.sin(angles))


TILE = 256
MASKED = -1e30
LOG2E = 1.4426950408889634
SCORE_SCALE = HD**-0.5 * LOG2E


def mat(left, right):
    return lax.dot_general(left, right, (((1,), (0,)), ((), ())), preferred_element_type=F32)


def mat_turned(left, right):
    return lax.dot_general(left, right, (((1,), (1,)), ((), ())), preferred_element_type=F32)


def tile_bias(code_col, code_row, keys, queries):
    same = code_col[keys, :] == code_row[:, queries]
    return jnp.where(same, 0.0, MASKED)


def tiles(at):
    return pl.ds(pl.multiple_of(at * TILE, TILE), TILE)


def forward_kernel(active, qkv, code_row, code_col, mixed, log_sum, k_rows, top, total, acc):
    heads, length = k_rows.shape[0], k_rows.shape[1]
    blocks = length // TILE
    for head in range(heads):
        base = (heads + head) * HD
        k_rows[head] = turned(qkv[base : base + HD, :]).astype(BF16)

    def query_block(q_at, carry):
        queries = tiles(q_at)
        top[...] = jnp.full(top.shape, MASKED, F32)
        total[...] = jnp.zeros(total.shape, F32)
        acc[...] = jnp.zeros(acc.shape, F32)

        def key_block(k_at, carry):
            @pl.when(active[q_at * blocks + k_at] != 0)
            def _():
                keys = tiles(k_at)
                bias = tile_bias(code_col, code_row, keys, queries)
                every = range(heads)
                scores = [
                    mat(k_rows[head, keys, :], qkv[head * HD : (head + 1) * HD, queries]) + bias
                    for head in every
                ]
                old = [top[head] for head in every]
                new = [
                    jnp.maximum(old[head], jnp.max(scores[head], axis=0, keepdims=True))
                    for head in every
                ]
                chance = [jnp.exp2((scores[head] - new[head]) * SCORE_SCALE) for head in every]
                fade = [jnp.exp2((old[head] - new[head]) * SCORE_SCALE) for head in every]
                added = [jnp.sum(chance[head], axis=0, keepdims=True) for head in every]
                products = [
                    mat(
                        qkv[(2 * heads + head) * HD : (2 * heads + head + 1) * HD, keys],
                        chance[head].astype(BF16),
                    )
                    for head in every
                ]
                for head in every:
                    top[head] = new[head]
                    total[head] = total[head] * fade[head] + added[head]
                    acc[head] = acc[head] * fade[head] + products[head]

            return carry

        lax.fori_loop(0, blocks, key_block, 0)
        for head in range(heads):
            mixed[head * HD : (head + 1) * HD, queries] = (acc[head] / total[head]).astype(BF16)
            log_sum[head, :, queries] = top[head] * SCORE_SCALE + jnp.log2(total[head])
        return carry

    lax.fori_loop(0, blocks, query_block, 0)


def backward_kernel(active, qkv, mixed, grad_mixed, log_sum, cosine, sine, code_row, code_col, out, k_rows, v_rows, centre, grad_q, grad_k, grad_v):
    heads, length = k_rows.shape[0], k_rows.shape[1]
    blocks = length // TILE
    for head in range(heads):
        k_base, v_base = (heads + head) * HD, (2 * heads + head) * HD
        k_rows[head] = qkv[k_base : k_base + HD, :].astype(F32).T.astype(BF16)
        v_rows[head] = qkv[v_base : v_base + HD, :].astype(F32).T.astype(BF16)
        rows = slice(head * HD, (head + 1) * HD)
        centre[head] = jnp.sum(
            grad_mixed[rows, :].astype(F32) * mixed[rows, :].astype(F32), axis=0, keepdims=True
        )
    grad_q[...] = jnp.zeros(grad_q.shape, F32)
    grad_k[...] = jnp.zeros(grad_k.shape, F32)
    grad_v[...] = jnp.zeros(grad_v.shape, F32)

    def query_block(q_at, carry):
        queries = tiles(q_at)

        def key_block(k_at, carry):
            @pl.when(active[q_at * blocks + k_at] != 0)
            def _():
                keys = tiles(k_at)
                bias = tile_bias(code_col, code_row, keys, queries)
                every = range(heads)
                rows = [slice(head * HD, (head + 1) * HD) for head in every]
                scores = [mat(k_rows[h, keys, :], qkv[rows[h], queries]) + bias for h in every]
                raised = [mat(v_rows[h, keys, :], grad_mixed[rows[h], queries]) for h in every]
                chance = [
                    jnp.exp2(scores[h] * SCORE_SCALE - log_sum[h, :, queries]) for h in every
                ]
                pulled = [
                    (chance[h] * (raised[h] - centre[h, :, queries])).astype(BF16) for h in every
                ]
                for_v = [
                    mat_turned(grad_mixed[rows[h], queries], chance[h].astype(BF16)) for h in every
                ]
                for_k = [mat_turned(qkv[rows[h], queries], pulled[h]) for h in every]
                for_q = [
                    mat(qkv[(heads + h) * HD : (heads + h + 1) * HD, keys], pulled[h])
                    for h in every
                ]
                for h in every:
                    grad_v[h, :, keys] += for_v[h]
                    grad_k[h, :, keys] += for_k[h]
                    grad_q[h, :, queries] += for_q[h]

            return carry

        return lax.fori_loop(0, blocks, key_block, carry)

    lax.fori_loop(0, blocks, query_block, 0)
    half = HD // 2
    scale = HD**-0.5
    cos, sin = cosine[...] * scale, sine[...] * scale
    for head in range(heads):
        for which, grad in ((0, grad_q), (1, grad_k)):
            base = (which * heads + head) * HD
            low, high = grad[head, :half, :], grad[head, half:, :]
            turned = jnp.concatenate([low * cos + high * sin, high * cos - low * sin], axis=0)
            out[base : base + HD, :] = turned.astype(BF16)
        base = (2 * heads + head) * HD
        out[base : base + HD, :] = grad_v[head].astype(BF16)


def whole(count):
    return [pl.BlockSpec(memory_space=pltpu.VMEM)] * count


def attend_forward(qkv, facts):
    active, _, _, code_row, code_col = facts
    width, length = qkv.shape
    heads = width // (3 * HD)
    return pl.pallas_call(
        forward_kernel,
        name="attend_forward",
        out_shape=(
            jax.ShapeDtypeStruct((heads * HD, length), BF16),
            jax.ShapeDtypeStruct((heads, 1, length), F32),
        ),
        in_specs=[pl.BlockSpec(memory_space=pltpu.SMEM)] + whole(3),
        out_specs=tuple(whole(2)),
        scratch_shapes=[
            pltpu.VMEM((heads, length, HD), BF16),
            pltpu.VMEM((heads, 1, TILE), F32),
            pltpu.VMEM((heads, 1, TILE), F32),
            pltpu.VMEM((heads, HD, TILE), F32),
        ],
        compiler_params=pltpu.CompilerParams(vmem_limit_bytes=40 << 20),
        cost_estimate=pl.CostEstimate(
            flops=heads * length * length * HD * 4,
            bytes_accessed=4 << 20,
            transcendentals=heads * length * length,
        ),
    )(active, qkv, code_row, code_col)


def attend_backward(qkv, mixed, grad_mixed, log_sum, facts):
    active, cosine, sine, code_row, code_col = facts
    width, length = qkv.shape
    heads = width // (3 * HD)
    return pl.pallas_call(
        backward_kernel,
        name="attend_backward",
        out_shape=jax.ShapeDtypeStruct((width, length), BF16),
        in_specs=[pl.BlockSpec(memory_space=pltpu.SMEM)] + whole(8),
        out_specs=pl.BlockSpec(memory_space=pltpu.VMEM),
        scratch_shapes=[
            pltpu.VMEM((heads, length, HD), BF16),
            pltpu.VMEM((heads, length, HD), BF16),
            pltpu.VMEM((heads, 1, length), F32),
            pltpu.VMEM((heads, HD, length), F32),
            pltpu.VMEM((heads, HD, length), F32),
            pltpu.VMEM((heads, HD, length), F32),
        ],
        compiler_params=pltpu.CompilerParams(vmem_limit_bytes=40 << 20),
        cost_estimate=pl.CostEstimate(
            flops=heads * length * length * HD * 10, bytes_accessed=10 << 20, transcendentals=heads * length * length
        ),
    )(active, qkv, mixed, grad_mixed, log_sum, cosine, sine, code_row, code_col)


def tile_overlap(codes):
    blocks = codes.reshape(-1, TILE)
    least, most = jnp.min(blocks, axis=1), jnp.max(blocks, axis=1)
    meet = (least[:, None] <= most[None, :]) & (least[None, :] <= most[:, None])
    return meet.astype(jnp.int32).reshape(-1)


(
    ACT, ALL, ATTN, BACKWARD, CORE, CORNER, CORNERS, CROSS, DIAGONAL, DOWN, ENDS, ENTER, ENTERED,
    ENTER_AT, ENTER_BIAS, ENTER_GAIN, ENTER_W, FAR_IN, FAR_OUT, FAR_OWN, FINAL, FIRST,
    FIRST_BIAS, FORWARD, FROM_HIGH, FROM_LOW, GRAD, HELD, HERE, HIGH, LEAVE, LEAVE_BIAS,
    LEAVE_GAIN, LEAVE_SHIFT, LEAVE_W, LINE, LINE_IN, LINE_OUT, LOW, MINE, MIX, MIXED, MIX_AT,
    MIX_GAIN, MIX_SHIFT, NEAR_IN, NEAR_OUT, OWN, OWNED, PAIR, PROJ, QKV, REMOTE, REORDER, RESULT,
    ROWS, ROWS2, ROWS_OUT, SECOND, SECOND_BIAS, SLOPE, SOURCE, STATE, SUMS, TARGET, UNIT_SUMS,
    UP, VALUE, WIDE_SUMS,
) = range(69)
ONE, OTHER = 103, 104
COTANGENT, COSINE, SINE = 100, 101, 102
FIRST_HBM = 200
COTANGENT_HBM = FIRST_HBM + 50
(
    ACT_HBM, FACTS_HBM, HIDDEN_HBM, MOVED_HBM, ROWS2_HBM, ROWS_HBM, ROW_FACTS_HBM, SLOPE_HBM,
    VECTORS_HBM, VECTOR_HBM,
) = range(FIRST_HBM, FIRST_HBM + 10)


STRIP = 256
PARTS = 2
MESH_ID = pl.DeviceIdType.MESH


def strips(at):
    return pl.ds(pl.multiple_of(at * STRIP, STRIP), STRIP)


def partners():
    dp_at, mp_at = lax.axis_index("dp"), lax.axis_index("mp")
    core = dp_at + 1 - 2 * lax.rem(dp_at, 2)
    cross = mp_at + 2 - 4 * (mp_at // 2)
    return {
        CORE: {"dp": core},
        LINE: {"mp": mp_at + 1 - 2 * lax.rem(mp_at, 2)},
        CROSS: {"mp": cross},
        DIAGONAL: {"dp": core, "mp": cross},
        LOW: {"dp": dp_at + 2 - 4 * lax.rem(dp_at // 2, 2)},
        HIGH: {"dp": dp_at + 4 - 8 * lax.rem(dp_at // 4, 2)},
    }


def greet(names):
    barrier, devices = pltpu.get_barrier_semaphore(), partners()
    for name in names:
        pl.semaphore_signal(barrier, inc=1, device_id=devices[name], device_id_type=MESH_ID)
    return lambda: pl.semaphore_wait(barrier, len(names))


class Courier:
    def __init__(self, ref):
        self.ref, self.devices = ref, partners()
        self.remotes, self.locals = 0, 0
        self.open = {}
        self.aligned = lax.rem(lax.axis_index("dp"), 2) == lax.axis_index("mp") // 2

    def slot(self):
        self.remotes += 1
        return self.remotes - 1

    def remote(self, source, target, partner, at, received=None):
        sems = self.ref[REMOTE]
        received = at if received is None else received
        return pltpu.make_async_remote_copy(
            src_ref=source,
            dst_ref=target,
            send_sem=sems.at[0, at],
            recv_sem=sems.at[1, received],
            device_id=self.devices[partner],
            device_id_type=MESH_ID,
        )

    def send(self, source, target, partner):
        copy = self.remote(source, target, partner, self.slot())
        copy.start()
        return copy

    def near(self, source, target):
        return pltpu.make_async_copy(source, target, self.ref[HERE].at[self.locals])

    def local(self, source, target):
        copy = self.near(source, target)
        self.locals += 1
        copy.start()
        return copy

    def swap(self, source, target):
        at, copy = self.slot(), self.near(source, target)
        self.locals += 1
        away = lambda: self.remote(source, target, DIAGONAL, at)
        pl.when(self.aligned)(copy.start)
        pl.when(jnp.logical_not(self.aligned))(lambda: away().start())

        def finish():
            pl.when(self.aligned)(copy.wait)
            pl.when(jnp.logical_not(self.aligned))(lambda: away().wait())

        return finish

    def begin(self, pack, step):
        ref = self.ref
        buffer = lambda part: ref[(pack, part)]
        if step == 1:
            mine, pair = buffer(MINE), buffer(PAIR)
            first, second, copy = self.slot(), self.slot(), self.near(mine, pair.at[0])
            self.locals += 1
            across = lambda: self.remote(mine, pair.at[1], CROSS, first)
            beside = lambda: self.remote(mine, pair.at[1], CORE, first)
            over = lambda: self.remote(mine, pair.at[0], DIAGONAL, second)

            def start_aligned():
                copy.start()
                across().start()

            def start_other():
                beside().start()
                over().start()

            def wait_aligned():
                copy.wait()
                across().wait()

            def wait_other():
                beside().wait()
                over().wait()

            pl.when(self.aligned)(start_aligned)
            pl.when(jnp.logical_not(self.aligned))(start_other)

            def finish():
                pl.when(self.aligned)(wait_aligned)
                pl.when(jnp.logical_not(self.aligned))(wait_other)

        elif step > 4:
            self.finish(pack, step - 1)
            finish = self.reduce(pack, step)
        else:
            self.finish(pack, step - 1)
            if step == 4:
                depth = buffer(CORNERS).shape[1]
                block = lambda at: buffer(GRAD).at[at * depth : (at + 1) * depth]
                copies = [
                    self.send(block(6), buffer(CORNERS).at[0], HIGH),
                    self.send(block(7), buffer(CORNERS).at[1], LOW),
                ]
            elif step == 2:
                pair = buffer(PAIR)
                copies = [self.send(pair, buffer(side), side) for side in (LOW, HIGH)]
            else:
                copies = [
                    self.send(buffer(LOW).at[0], buffer(CORNER).at[0], HIGH),
                    self.send(buffer(HIGH).at[1], buffer(CORNER).at[1], LOW),
                ]

            def finish():
                for copy in copies:
                    copy.wait()

        self.open[pack, step] = finish

    def fetch(self, columns, terms):
        held = self.ref[HELD, columns]
        loads = [self.local(term, held.at[at]) for at, term in enumerate(terms)]
        for load in loads:
            load.wait()
        return lambda at: held[at].astype(F32)

    def reduce(self, pack, step):
        ref = self.ref
        buffer = lambda part: ref[pack, part]
        if step == 7:
            ends = buffer(ENDS)
            columns = ends.shape[2]
            term = self.fetch(columns, [ends.at[0], ends.at[1]])
            result = ref[RESULT, columns, pack]
            result[...] = term(0) + term(1)
            return self.local(result, buffer(RESULT)).wait
        depth, columns = buffer(GRAD).shape[0] // 8, buffer(GRAD).shape[1]
        block = lambda at: buffer(GRAD).at[at * depth : (at + 1) * depth]
        sums = ref[SUMS, pack]
        if step == 5:
            from_low, from_high = buffer(FROM_LOW), buffer(FROM_HIGH)
            corners = [buffer(CORNERS).at[at] for at in range(2)]
            copies = [
                self.send(block(3), from_low.at[1], LOW),
                self.send(block(4), from_high.at[0], HIGH),
            ]
            term = self.fetch(columns, [block(2), block(5), *corners])
            for at in range(2):
                sums[at] = (term(at) + term(2 + at)).astype(BF16)
            copies.append(self.send(sums.at[0], from_low.at[0], LOW))
            copies.append(self.send(sums.at[1], from_high.at[1], HIGH))

            def finish():
                for copy in copies:
                    copy.wait()

            return finish
        ends, sides = buffer(ENDS), (buffer(FROM_LOW), buffer(FROM_HIGH))
        term = self.fetch(
            columns, [block(0), block(1)] + [side.at[at] for side in sides for at in range(2)]
        )
        for at in range(2):
            sums[at] = (term(at) + term(2 + at) + term(4 + at)).astype(BF16)
        first, second = self.slot(), self.slot()
        copy = self.near(sums.at[0], ends.at[0])
        self.locals += 1
        beside = lambda: self.remote(sums.at[1], ends.at[0], CORE, first)
        over = lambda: self.remote(sums.at[0], ends.at[1], DIAGONAL, second)
        across = lambda: self.remote(sums.at[1], ends.at[1], CROSS, first, second)

        def start_aligned():
            copy.start()
            beside().start()

        def start_other():
            over().start()
            across().start()

        def wait_aligned():
            copy.wait()
            beside().wait_send()
            over().wait_recv()

        def wait_other():
            over().wait()
            across().wait_send()
            beside().wait_recv()

        pl.when(self.aligned)(start_aligned)
        pl.when(jnp.logical_not(self.aligned))(start_other)

        def finish():
            pl.when(self.aligned)(wait_aligned)
            pl.when(jnp.logical_not(self.aligned))(wait_other)

        return finish

    def finish(self, pack, step):
        finish = self.open.pop((pack, step), None)
        if finish is not None:
            finish()

    def finish_all(self):
        for finish in self.open.values():
            finish()
        self.open = {}


PACK_PARTS = {
    1: (PAIR,),
    2: (LOW, HIGH),
    3: (CORNER,),
    4: (CORNERS,),
    5: (FROM_LOW, FROM_HIGH),
    6: (ENDS,),
    7: (RESULT,),
}
PACK_NEEDS = {
    1: (MINE,),
    2: (PAIR,),
    3: (LOW, HIGH),
    4: (GRAD,),
    5: (GRAD, CORNERS),
    6: (GRAD, FROM_LOW, FROM_HIGH),
    7: (ENDS,),
}


def pack_buffers(jobs, packs):
    needs, makes, scratch = {}, {}, {}
    for pack, step in jobs:
        for part in PACK_NEEDS[step]:
            if (pack, part) not in makes:
                needs[pack, part] = packs[pack, part]
        if step < 4:
            depth, columns = packs[(pack, MINE)].shape
        else:
            depth, columns = packs[(pack, GRAD)].shape
            depth //= 8
            scratch[HELD, columns] = pltpu.VMEM((6, depth, columns), BF16)
            if step in (5, 6):
                scratch[SUMS, pack] = pltpu.VMEM((2, depth, columns), BF16)
        for part in PACK_PARTS[step]:
            made = jax.ShapeDtypeStruct((2, depth, columns), BF16)
            if part == RESULT:
                made = jax.ShapeDtypeStruct((depth, columns), F32)
                scratch[RESULT, columns, pack] = pltpu.VMEM((depth, columns), F32)
            makes[(pack, part)] = made
    return needs, makes, scratch, 4 * len(jobs), 9 * len(jobs)


def start_kernel(jobs, names, *refs):
    ref = dict(zip(names, refs))
    greeted = greet((CORE, LINE, CROSS, DIAGONAL, LOW, HIGH))
    courier = Courier(ref)
    greeted()
    facts = courier.swap(ref[FACTS_HBM], ref[ROW_FACTS_HBM])
    vector, vectors = ref[VECTOR_HBM], ref[VECTORS_HBM]
    courier.local(vector, vectors.at[0]).wait()
    rows = None
    size = 1
    for partner in (LINE, CROSS, CORE, LOW, HIGH):
        courier.send(vectors.at[0:size], vectors.at[size : 2 * size], partner).wait()
        size *= 2
        if partner == CROSS:
            courier.begin(*jobs[0])
            rows = courier.swap(ref[HIDDEN_HBM], ref[MOVED_HBM])
    for job in jobs[1:]:
        courier.begin(*job)
    rows()
    facts()
    courier.finish_all()


def start_call(collective, hidden, facts, vector, jobs, packs):
    anywhere = pl.BlockSpec(memory_space=pl.ANY)
    needs, makes, _, remote, here = pack_buffers(jobs, packs)
    shape = jax.ShapeDtypeStruct
    inputs = {HIDDEN_HBM: hidden, FACTS_HBM: facts, VECTOR_HBM: vector, **needs}
    outputs = {
        MOVED_HBM: shape(hidden.shape, hidden.dtype),
        ROW_FACTS_HBM: shape(facts.shape, facts.dtype),
        VECTORS_HBM: shape((32, *vector.shape), vector.dtype),
        **makes,
    }
    names = (*inputs, *outputs, REMOTE, HERE)
    results = pl.pallas_call(
        functools.partial(start_kernel, jobs, names),
        name="start_exchange",
        out_shape=tuple(outputs.values()),
        in_specs=[anywhere] * len(inputs),
        out_specs=(anywhere,) * len(outputs),
        scratch_shapes=[
            pltpu.SemaphoreType.DMA((2, remote + 7)),
            pltpu.SemaphoreType.DMA((here + 3,)),
        ],
        compiler_params=pltpu.CompilerParams(collective_id=collective, has_side_effects=True),
        cost_estimate=pl.CostEstimate(flops=0, bytes_accessed=64 << 20, transcendentals=0),
    )(*inputs.values())
    results = dict(zip(outputs, results))
    packs.update({name: results[name] for name in makes})
    return results


def turned(values):
    return values.astype(F32).T


def joined(pieces, axis=0):
    return pieces[0] if len(pieces) == 1 else jnp.concatenate(pieces, axis=axis)


def chain_kernel(stages, backward, names, plan, jobs, *refs):
    ref = dict(zip(names, refs))
    enter, mix, leave = stages
    value, state, own, far_own = ref[VALUE], ref[STATE], ref[OWN], ref[FAR_OWN]
    count, width = value.shape
    step = count // PARTS
    greeted = greet(tuple(partners()) if jobs or MOVED_HBM in ref else (CORE, LINE))
    courier = Courier(ref)
    send, local = courier.send, courier.local
    core, line = CORE, LINE
    waiting = list(jobs)

    def point(at):
        while waiting and waiting[0][0] <= at:
            courier.begin(*waiting.pop(0)[1:])

    def chunk(slot, part):
        return slice(slot * count + part * step, slot * count + (part + 1) * step)

    def place(part):
        return slice(part * step, (part + 1) * step)

    made = {(pack, part): (pack, at) for _, pack, at in jobs for part in PACK_PARTS[at]}
    loads = {}

    def load(name, blocks):
        return [
            local(ref[piece].at[index, :, begin:end], ref[name].at[row : row + depth, :])
            for piece, index, row, depth, begin, end in blocks
        ]

    for name, blocks in plan:
        loads[name] = load(name, [block for block in blocks if block[0] not in made])

    def loaded(name):
        late = [block for weight, blocks in plan if weight == name for block in blocks]
        late = [block for block in late if block[0] in made]
        for block in late:
            courier.finish(*made[block[0]])
        for copy in loads[name] + load(name, late):
            copy.wait()

    if mix and backward:
        loads[SLOPE] = [local(ref[SLOPE_HBM], ref[SLOPE])]
    saves = []
    if backward:
        ref[WIDE_SUMS][...] = jnp.zeros(ref[WIDE_SUMS].shape, F32)

    def add_wide(row, sums):
        if sums.ndim == 1:
            sums = sums[None]
        ref[WIDE_SUMS][row : row + 1, :] += sums

    def product(pieces, weight, stores, transposed_source=False):
        def strip(at, carry):
            columns = strips(at)
            result = mat_turned(pieces, weight[columns, : pieces.shape[1]])
            begin = 0
            for size, store in stores:
                store(columns, result[begin : begin + size])
                begin += size
            return carry

        lax.fori_loop(0, width // STRIP, strip, 0, unroll=True)

    def put(target, index):
        def store(columns, result):
            target[index, :, columns] = result.astype(target.dtype)

        return store

    def scatter(prefix, source, weight):
        far_out, far_in = ref[prefix, FAR_OUT], ref[prefix, FAR_IN]
        line_out, line_in = ref[prefix, LINE_OUT], ref[prefix, LINE_IN]
        near_out, near_in = ref[prefix, NEAR_OUT], ref[prefix, NEAR_IN]

        def far(part):
            product(
                source([(2, part), (3, part)]),
                weight,
                [(step, put(far_own, part)), (step, put(far_out, part))],
            )
            return send(far_out.at[part], far_in.at[part], core)

        def pass_on(part, passing):
            passing.wait()
            line_out[part] = (far_own[part] + far_in[part].astype(F32)).astype(BF16)
            return send(line_out.at[part], line_in.at[part], line)

        def near():
            product(
                source([(1, part) for part in range(PARTS)]),
                weight,
                [(step, put(near_out, part)) for part in range(PARTS)],
            )
            return send(near_out, near_in, core)

        def mine():
            product(
                source([(0, part) for part in range(PARTS)]),
                weight,
                [(step, put(own, part)) for part in range(PARTS)],
            )

        def total(part):
            return own[part] + near_in[part].astype(F32) + line_in[part].astype(F32)

        return far, pass_on, near, mine, total

    def lower(values, gain, shift):
        if backward:
            return values.astype(BF16)
        return (normalise(values)[0] * gain[...] + shift[...]).astype(BF16)

    def begin_rows(rows, part):
        near = send(rows.at[chunk(0, part)], rows.at[chunk(1, part)], core)
        far = send(rows.at[chunk(0, part)], rows.at[chunk(2, part)], line)
        return near, far

    def forward_rows(rows, part, far):
        far.wait()
        return send(rows.at[chunk(2, part)], rows.at[chunk(3, part)], core)

    ready = None
    if enter:
        source_t = ref[SOURCE]

        def entering(pieces):
            return turned(joined([source_t[:, chunk(*piece)] for piece in pieces], 1)).astype(BF16)

        far, pass_on, near, mine, total = scatter(ENTER, entering, ref[ENTER_W])
        loaded(ENTER_W)
        greeted()
        point(0)
        if COTANGENT_HBM in ref:
            moved = courier.swap(ref[COTANGENT_HBM], ref[MOVED_HBM])
        passing = [far(part) for part in range(PARTS)]
        lines = [pass_on(part, passing[part]) for part in range(PARTS)]
        near_sum = near()
        mine()
        point(1)
        near_sum.wait()
        point(2)

        def ready(part):
            lines[part].wait()
            at = place(part)
            if backward:
                grad, gains, shifts = norm_backward(
                    ref[ENTER_AT][at, :], ref[ENTER_GAIN][...], total(part)
                )
                state[at, :] = value[at, :] + grad
                add_wide(0, gains)
                add_wide(1, shifts)
            else:
                state[at, :] = value[at, :] + (total(part) + ref[ENTER_BIAS][...])
            ref[ENTERED][at, :] = state[at, :]

    else:
        greeted()
        point(0)

        if COTANGENT in ref:
            lowered = mat(value[...].astype(BF16), ref[REORDER][...])
            ref[ROWS_OUT][...] = lowered.astype(BF16)
            moved = courier.swap(ref[ROWS_OUT], ref[MOVED_HBM])
            state[...] = mat(ref[COTANGENT][...], ref[REORDER][...])

        def ready(part):
            at = place(part)
            if COTANGENT not in ref:
                state[at, :] = value[at, :]

    if mix:
        rows, act, slope = ref[ROWS], ref[ACT], ref[SLOPE]
        first, second = ref[FIRST], ref[SECOND]
        units = first.shape[1]
        if backward:
            ref[UNIT_SUMS][...] = jnp.zeros(ref[UNIT_SUMS].shape, F32)
        begun = []
        for part in range(PARTS):
            ready(part)
            lowered = lower(
                state[place(part), :], ref.get(MIX_GAIN), ref.get(MIX_SHIFT)
            )
            rows[chunk(0, part), :] = lowered
            begun.append(begin_rows(rows, part))
            if backward:
                add_wide(2, jnp.sum(lowered.astype(F32), axis=0))

        def expand(pieces):
            taken = joined([rows[chunk(*piece), :] for piece in pieces])

            def strip(at, carry):
                columns = strips(at)
                up = mat(taken, first[:, columns])
                tilt = None
                if backward:
                    slopes = joined([slope[chunk(*piece), columns] for piece in pieces])
                    out = (up * slopes.astype(F32)).astype(BF16)
                    ref[UNIT_SUMS][:, columns] += jnp.sum(
                        out.astype(F32), axis=0, keepdims=True
                    )
                else:
                    up = up + ref[FIRST_BIAS][:, columns]
                    sigmoid = 1.0 / (1.0 + jnp.exp(-1.702 * up))
                    out = (up * sigmoid).astype(BF16)
                    tilt = (sigmoid + 1.702 * up * sigmoid * (1.0 - sigmoid)).astype(BF16)
                for index, piece in enumerate(pieces):
                    at_rows = slice(index * step, (index + 1) * step)
                    act[chunk(*piece), columns] = out[at_rows]
                    if tilt is not None:
                        slope[chunk(*piece), columns] = tilt[at_rows]
                return carry

            lax.fori_loop(0, units // STRIP, strip, 0, unroll=True)

        def acting(pieces):
            return joined([act[chunk(*piece), :] for piece in pieces])

        far, pass_on, near, mine, total = scatter(MIX, acting, second)
        loaded(FIRST)
        if backward:
            loaded(SLOPE)
        expand([(0, part) for part in range(PARTS)])
        for part in range(PARTS):
            begun[part][0].wait()
        point(3)
        expand([(1, part) for part in range(PARTS)])
        loaded(SECOND)
        near_sum = near()
        point(4)
        forwards = [forward_rows(rows, 0, begun[0][1])]
        mine()
        lines = []
        for part in range(PARTS):
            forwards[part].wait()
            expand([(2, part), (3, part)])
            lines.append(pass_on(part, far(part)))
            if part + 1 < PARTS:
                forwards.append(forward_rows(rows, part + 1, begun[part + 1][1]))
            point(5 + part)
        saves.append(local(rows, ref[ROWS_HBM]))
        saves.append(local(act, ref[ACT_HBM]))
        if not backward:
            saves.append(local(slope, ref[SLOPE_HBM]))
        near_sum.wait()

        def ready(part):
            lines[part].wait()
            at = place(part)
            if backward:
                grad, gains, shifts = norm_backward(
                    ref[MIX_AT][at, :], ref[MIX_GAIN][...], total(part)
                )
                state[at, :] = state[at, :] + grad
                add_wide(3, gains)
                add_wide(4, shifts)
            else:
                state[at, :] = state[at, :] + (total(part) + ref[SECOND_BIAS][...])
            ref[MIXED][at, :] = state[at, :]

    if leave:
        rows2, weight, target = ref[ROWS2], ref[LEAVE_W], ref[TARGET]
        begun = []
        for part in range(PARTS):
            ready(part)
            lowered = lower(
                state[place(part), :], ref.get(LEAVE_GAIN), ref.get(LEAVE_SHIFT)
            )
            rows2[chunk(0, part), :] = lowered
            begun.append(begin_rows(rows2, part))
            if backward:
                add_wide(5, jnp.sum(lowered.astype(F32), axis=0))

        def leaving(pieces):
            result = mat(joined([rows2[chunk(*piece), :] for piece in pieces]), weight[...])
            if not backward:
                result = result + ref[LEAVE_BIAS][...]
            result = turned(result)
            if not backward:
                cos, sin = (
                    joined([ref[name][:, chunk(*piece)] for piece in pieces], 1)
                    for name in (COSINE, SINE)
                )
                half, third = HD // 2, result.shape[0] // 3
                blocks = []
                for base in range(0, 2 * third, HD):
                    low, high = result[base : base + half], result[base + half : base + HD]
                    blocks += [low * cos - high * sin, high * cos + low * sin]
                result = jnp.concatenate(blocks + [result[2 * third :]], axis=0)
            result = result.astype(BF16)
            for index, piece in enumerate(pieces):
                target[:, chunk(*piece)] = result[:, index * step : (index + 1) * step]

        loaded(LEAVE_W)
        point(7)
        leaving([(0, part) for part in range(PARTS)])
        for part in range(PARTS):
            begun[part][0].wait()
        leaving([(1, part) for part in range(PARTS)])
        point(8)
        forwards = [forward_rows(rows2, part, begun[part][1]) for part in range(PARTS)]
        for part in range(PARTS):
            forwards[part].wait()
            leaving([(2, part), (3, part)])
        saves.append(local(rows2, ref[ROWS2_HBM]))
    else:
        for part in range(PARTS):
            ready(part)
    if REORDER in ref and COTANGENT not in ref:
        lowered = mat(state[...].astype(BF16), ref[REORDER][...]).astype(BF16)
        rows_out = ref[ROWS_OUT]
        rows_out[...] = lowered
        moved = courier.swap(rows_out, ref[MOVED_HBM])
    point(9)
    if MOVED_HBM in ref:
        moved()
    for save in saves:
        save.wait()
    courier.finish_all()


class Weight:
    def __init__(self, pack, begin, end):
        self.pack, self.begin, self.end = pack, begin, end


def chain_call(stages, backward, collective, operands, packs, jobs=()):
    enter, mix, leave = stages
    count, width = operands[VALUE].shape
    step = count // PARTS
    shape = jax.ShapeDtypeStruct
    vmem, anywhere = pl.BlockSpec(memory_space=pltpu.VMEM), pl.BlockSpec(memory_space=pl.ANY)
    outputs, scratch = {}, {}
    buffers = lambda kind: pltpu.VMEM((PARTS, step, width), kind)
    scratch[STATE] = pltpu.VMEM((count, width), F32)
    scratch[OWN] = buffers(F32)
    scratch[FAR_OWN] = buffers(F32)
    remote, here = 0, 0
    if backward:
        outputs[WIDE_SUMS] = shape((8, width), F32)
    flops = 0
    plan = []
    passed = {}
    needs, makes, job_scratch, job_remote, job_here = pack_buffers([job[1:] for job in jobs], packs)
    scratch.update(job_scratch)
    remote, here = remote + job_remote, here + job_here
    for name, value in operands.items():
        if not isinstance(value, Weight):
            passed[name] = value
            continue
        blocks, row = [], 0
        for part in (PAIR, LOW, HIGH, CORNER, ONE, OTHER, ALL):
            piece = (value.pack, part)
            if piece not in packs and piece not in makes:
                continue
            if piece not in makes:
                passed[piece] = packs[piece]
            array = makes.get(piece, packs.get(piece))
            for index in range(array.shape[0]):
                blocks.append((piece, index, row, array.shape[1], value.begin, value.end))
                row += array.shape[1]
        plan.append((name, blocks))
        scratch[name] = pltpu.VMEM((width, value.end - value.begin), BF16)
        here += len(blocks)
        flops += 8 * count * width * (value.end - value.begin)
    passed.update({name: value for name, value in needs.items() if name not in passed})
    outputs.update(makes)
    for stage, prefix in ((enter, ENTER), (mix, MIX)):
        if stage:
            for name in (FAR_OUT, FAR_IN, LINE_OUT, LINE_IN, NEAR_OUT, NEAR_IN):
                scratch[prefix, name] = buffers(BF16)
            remote += 2 * PARTS + 1
    if enter:
        outputs[ENTERED] = shape((count, width), F32)
    if mix:
        units = operands[FIRST].end - operands[FIRST].begin
        scratch[ROWS] = pltpu.VMEM((4 * count, width), BF16)
        scratch[ACT] = pltpu.VMEM((4 * count, units), BF16)
        scratch[SLOPE] = pltpu.VMEM((4 * count, units), BF16)
        outputs[MIXED] = shape((count, width), F32)
        outputs[ROWS_HBM] = shape((4 * count, width), BF16)
        outputs[ACT_HBM] = shape((4 * count, units), BF16)
        if backward:
            outputs[UNIT_SUMS] = shape((1, units), F32)
        else:
            outputs[SLOPE_HBM] = shape((4 * count, units), BF16)
        remote += 3 * PARTS
        here += 3
    if leave:
        columns = leave
        scratch[ROWS2] = pltpu.VMEM((4 * count, width), BF16)
        outputs[TARGET] = shape((columns, 4 * count), BF16)
        outputs[ROWS2_HBM] = shape((4 * count, width), BF16)
        remote += 3 * PARTS
        here += 1
    if REORDER in operands or COTANGENT_HBM in operands:
        if REORDER in operands:
            scratch[ROWS_OUT] = pltpu.VMEM((count, width), BF16)
        outputs[MOVED_HBM] = shape((count, width), BF16)
        remote, here = remote + 1, here + 1
    scratch[REMOTE] = pltpu.SemaphoreType.DMA((2, remote))
    scratch[HERE] = pltpu.SemaphoreType.DMA((here,))
    names = tuple(passed) + tuple(outputs) + tuple(scratch)
    spec = lambda name: anywhere if isinstance(name, tuple) or name >= FIRST_HBM else vmem
    results = pl.pallas_call(
        functools.partial(chain_kernel, stages, backward, names, plan, jobs),
        name="chain_backward" if backward else "chain_forward",
        out_shape=tuple(outputs.values()),
        in_specs=[spec(name) for name in passed],
        out_specs=tuple(spec(name) for name in outputs),
        scratch_shapes=list(scratch.values()),
        compiler_params=pltpu.CompilerParams(
            collective_id=collective, has_side_effects=True, vmem_limit_bytes=54 << 20
        ),
        cost_estimate=pl.CostEstimate(
            flops=flops, bytes_accessed=(16 << 20) * sum(map(bool, stages)), transcendentals=0
        ),
    )(*passed.values())
    results = dict(zip(outputs, results))
    packs.update({name: results[name] for name in makes})
    return results


def make_body(dp, mp):
    assert mp == 4 and dp >= 2 and dp & (dp - 1) == 0
    count = dp * mp
    high_bits = [1 << b for b in range(1, dp.bit_length() - 1)]

    def across(value, bit):
        return lax.ppermute(value, "dp", [(i, i ^ bit) for i in range(dp)])

    def core_side(value):
        return across(value, 1)

    def line_side(value):
        return lax.ppermute(value, "mp", [(i, i ^ 1) for i in range(mp)])

    def swapped(d, m):
        return (d & ~1 | m >> 1) * mp + ((d & 1) << 1 | m & 1)

    swap_pairs = [
        (d * mp + m, swapped(d, m)) for d in range(dp) for m in range(mp) if d & 1 != m >> 1
    ]

    def swap(value):
        stays = (lax.axis_index("dp") & 1) == (lax.axis_index("mp") >> 1)
        return jnp.where(stays, value, lax.ppermute(value, ("dp", "mp"), swap_pairs))

    balanced = len(high_bits) == 2

    def gather_pair(mine):
        return swap(jnp.stack([mine, core_side(mine)]))

    def gather_sides(pair):
        for bit in high_bits:
            pair = jnp.concatenate([pair, across(pair, bit)], axis=0)
        return (pair,)

    def add(*terms):
        total = terms[0].astype(F32)
        for term in terms[1:]:
            total = total + term.astype(F32)
        return total.astype(BF16)

    def scatter_blocks(grad):
        total = grad.reshape(dp, D // dp, -1)
        for bit in high_bits[::-1]:
            half = total.shape[0] // 2
            total = add(total[:half], across(total[half:], bit))
        total = swap(total)
        return total[0].astype(F32) + core_side(total[1]).astype(F32)

    def arranged(values):
        index = lax.axis_index("dp") * mp + lax.axis_index("mp")
        at = jnp.arange(count, dtype=jnp.int32)
        order = (at[:, None] ^ index) == at[None, :]
        return dot(order.astype(F32), values, 1, 0, precision=HIGHEST)

    def gather_vectors(mine):
        values = mine[None]
        bit = 1
        while bit < count:
            if bit >= mp:
                got = across(values, bit // mp)
            else:
                got = lax.ppermute(values, "mp", [(i, i ^ bit) for i in range(mp)])
            values = jnp.concatenate([values, got], axis=0)
            bit *= 2
        return arranged(values)

    def scatter_vectors(values):
        index = lax.axis_index("dp") * mp + lax.axis_index("mp")
        bit = count // 2
        while bit:
            half = values.shape[0] // 2
            top = (index & bit) != 0
            low, high = values[:half], values[half:]
            sent = jnp.where(top, low, high)
            if bit >= mp:
                got = across(sent, bit // mp)
            else:
                got = lax.ppermute(sent, "mp", [(i, i ^ bit) for i in range(mp)])
            values = jnp.where(top, high, low) + got
            bit //= 2
        return values[0]

    def body(
        hidden_in,
        pre_gain,
        pre_bias,
        qkv_weight,
        qkv_bias,
        proj_weight,
        proj_bias,
        mid_gain,
        mid_bias,
        up_weight,
        up_bias,
        down_weight,
        down_bias,
        picture_ids,
        positions,
        pad_mask,
        cotangent,
    ):
        dp_at, mp_at = lax.axis_index("dp"), lax.axis_index("mp")
        group_at = (dp_at & ~1) | (mp_at >> 1)
        quarter_at = ((dp_at & 1) << 1) | (mp_at & 1)
        depth = D // dp
        columns = qkv_weight.shape[3]
        units = up_weight.shape[2]
        heads = columns // HD

        place = jnp.arange(D, dtype=jnp.int32)
        moved = ((place // depth) ^ group_at) * depth + place % depth
        reorder = place[:, None] == moved[None, :]
        reorder_low = reorder.astype(BF16)
        reorder_full = reorder.astype(F32)

        def turn_low(values):
            return dot(values.astype(BF16), reorder_low, 1, 0)

        qkv_width, proj_width = 3 * columns, columns
        packs = {}
        for layer in range(LAYERS):
            mine = qkv_weight[layer].transpose(1, 0, 2).reshape(depth, qkv_width)
            packs[(QKV, layer), MINE] = mine
            packs[(PROJ, layer), MINE] = proj_weight[layer].T
            packs[(UP, layer), MINE] = up_weight[layer]
            packs[(DOWN, layer), MINE] = down_weight[layer].T

        wide = (pre_gain, pre_bias, proj_bias, mid_gain, mid_bias, down_bias)
        packed = jnp.concatenate(
            [item.reshape(-1) for item in wide] + [qkv_bias.reshape(-1), up_bias.reshape(-1)]
        )
        length = picture_ids.shape[0]
        quarter = length // mp
        row_at = jnp.arange(length, dtype=jnp.int32)
        codes = jnp.where(pad_mask == 1, picture_ids, 1024 + row_at)
        row_facts = jnp.concatenate([codes[None], positions], axis=0)
        hidden = hidden_in.astype(BF16)
        jobs = {}
        if balanced:
            space = -(-packed.shape[0] // 1024) * 1024
            late = packs[(QKV, 1), MINE], packs[(DOWN, 1), MINE], packs[(PROJ, 1), MINE]
            hidden, late = lax.optimization_barrier((hidden, late))
            packs[(QKV, 1), MINE], packs[(DOWN, 1), MINE], packs[(PROJ, 1), MINE] = late
            begun = start_call(
                3 * LAYERS + 1,
                hidden,
                jnp.pad(row_facts, ((0, 5), (0, 0))),
                jnp.pad(packed, (0, space - packed.shape[0])).reshape(-1, 128),
                (((QKV, 0), 1), ((QKV, 0), 2), ((PROJ, 0), 1), ((UP, 0), 1), ((QKV, 0), 3)),
                packs,
            )
            hidden, row_facts = begun[MOVED_HBM], begun[ROW_FACTS_HBM][:3]
            packed = arranged(begun[VECTORS_HBM].reshape(count, space))[:, : packed.shape[0]]
            schedule = {
                (LEAVE, 0): {
                    0: ((UP, 0, 2), (PROJ, 0, 2)),
                    7: ((DOWN, 0, 1),),
                    8: ((PROJ, 0, 3),),
                },
                (FORWARD, 0): {
                    0: ((DOWN, 0, 2), (QKV, 1, 1)),
                    2: ((DOWN, 0, 3), (PROJ, 1, 1)),
                    4: ((QKV, 1, 2), (PROJ, 1, 2), (UP, 1, 1)),
                    6: ((QKV, 1, 3), (PROJ, 1, 3)),
                },
                (LEAVE, 1): {0: ((UP, 1, 2),), 7: ((DOWN, 1, 1),)},
                (FORWARD, 1): {0: ((DOWN, 1, 2),), 2: ((DOWN, 1, 3),)},
                (BACKWARD, 0): {
                    0: ((UP, 1, 4), (DOWN, 1, 4)),
                    1: ((UP, 1, 5),),
                    4: ((DOWN, 1, 5), (QKV, 1, 4), (PROJ, 1, 4)),
                    5: ((UP, 1, 6),),
                    8: ((DOWN, 1, 6), (QKV, 1, 5), (PROJ, 1, 5)),
                },
                (BACKWARD, FINAL): {
                    0: ((UP, 0, 4), (DOWN, 0, 4)),
                    1: ((UP, 0, 5),),
                    2: ((QKV, 1, 6), (PROJ, 1, 6), (QKV, 0, 4), (PROJ, 0, 4)),
                    9: (
                        *((UP, 0, 6), (DOWN, 0, 5), (QKV, 0, 5), (UP, 1, 7), (DOWN, 1, 7)),
                        *((DOWN, 0, 6), (PROJ, 0, 5), (QKV, 1, 7), (PROJ, 1, 7), (UP, 0, 7)),
                        *((QKV, 0, 6), (PROJ, 0, 6), (DOWN, 0, 7), (QKV, 0, 7), (PROJ, 0, 7)),
                    ),
                },
            }
            jobs = {
                kernel: tuple(
                    (at, (name, layer), step)
                    for at, steps in points.items()
                    for name, layer, step in steps
                )
                for kernel, points in schedule.items()
            }
        else:
            for name in list(packs):
                packs[name[0], ALL] = gather_sides(gather_pair(packs[name]))[0].reshape(1, D, -1)
            hidden, row_facts, packed = swap(hidden), swap(row_facts), gather_vectors(packed)
        hidden = turn_low(hidden)
        each = D // count
        wide_count = len(wide) * LAYERS
        split = (wide_count + 3 * LAYERS) * each
        vectors = packed[:, :split].reshape(count, -1, each).transpose(1, 0, 2).reshape(-1, D)
        wide_all = dot(vectors[:wide_count], reorder_full, 1, 0, precision=HIGHEST)
        wide_all = wide_all.reshape(len(wide), LAYERS, D)
        pre_gain_all, pre_bias_all, proj_bias_all, mid_gain_all, mid_bias_all, down_bias_all = (
            wide_all[i] for i in range(len(wide))
        )
        qkv_bias_mine = lax.dynamic_slice_in_dim(
            vectors[wide_count:], quarter_at * columns, columns, 1
        ).reshape(LAYERS, 3 * columns)
        up_all = packed[:, split:].reshape(count, LAYERS, -1).transpose(1, 0, 2)
        up_bias_mine = lax.dynamic_slice_in_dim(
            up_all.reshape(LAYERS, -1), quarter_at * units, units, 1
        )

        row_facts = jnp.concatenate(
            [
                lax.dynamic_slice_in_dim(row_facts, (quarter_at ^ which) * quarter, quarter, 1)
                for which in (0, 2, 1, 3)
            ],
            axis=1,
        )
        codes = row_facts[0]
        facts = (tile_overlap(codes), *rotary_tables(row_facts[1:]), codes[None], codes[:, None])

        row = lambda vector: vector[None]
        weights = [
            (
                Weight((QKV, layer), 0, qkv_width),
                Weight((PROJ, layer), 0, proj_width),
                Weight((UP, layer), 0, units),
                Weight((DOWN, layer), 0, units),
            )
            for layer in range(LAYERS)
        ]

        def leave_forward(layer):
            return {
                LEAVE_W: weights[layer][0],
                LEAVE_GAIN: row(pre_gain_all[layer]),
                LEAVE_SHIFT: row(pre_bias_all[layer]),
                LEAVE_BIAS: row(qkv_bias_mine[layer]),
                COSINE: facts[1],
                SINE: facts[2],
            }

        def call_leave(layer, value):
            return chain_call(
                (False, False, qkv_width),
                False,
                layer,
                {VALUE: value, **leave_forward(layer)},
                packs,
                jobs.get((LEAVE, layer), ()),
            )

        def call_forward(layer, value, mixed, more):
            return chain_call(
                (True, True, False),
                False,
                LAYERS + layer,
                {
                    VALUE: value,
                    SOURCE: mixed,
                    ENTER_W: weights[layer][1],
                    ENTER_BIAS: row(proj_bias_all[layer]),
                    FIRST: weights[layer][2],
                    SECOND: weights[layer][3],
                    FIRST_BIAS: row(up_bias_mine[layer]),
                    SECOND_BIAS: row(down_bias_all[layer]),
                    MIX_GAIN: row(mid_gain_all[layer]),
                    MIX_SHIFT: row(mid_bias_all[layer]),
                    **more,
                },
                packs,
                jobs.get((FORWARD, layer), ()),
            )

        def call_backward(layer, value, entering, middle, slope, more):
            return chain_call(
                (bool(entering), True, proj_width),
                True,
                2 * LAYERS + layer,
                {
                    VALUE: value,
                    **entering,
                    **more,
                    FIRST: weights[layer][3],
                    SECOND: weights[layer][2],
                    SLOPE_HBM: slope,
                    MIX_AT: middle,
                    MIX_GAIN: row(mid_gain_all[layer]),
                    LEAVE_W: weights[layer][1],
                },
                packs,
                jobs.get((BACKWARD, layer), ()),
            )

        def entering(layer, grad_linear, start):
            return {
                SOURCE: grad_linear,
                ENTER_W: weights[layer][0],
                ENTER_AT: start,
                ENTER_GAIN: row(pre_gain_all[layer]),
            }

        def beside_forward(layer):
            if not balanced:
                return
            low, high = high_bits
            up = (UP, layer)
            packs[up, ONE] = across(packs[up, LOW][:1], high)
            packs[up, OTHER] = across(packs[up, HIGH][1:], low)

        hidden, wide_all, qkv_bias_mine, up_bias_mine, facts = lax.optimization_barrier(
            (hidden, wide_all, qkv_bias_mine, up_bias_mine, facts)
        )
        pre_gain_all, pre_bias_all, proj_bias_all, mid_gain_all, mid_bias_all, down_bias_all = (
            wide_all[i] for i in range(len(wide))
        )
        leave0 = call_leave(0, hidden)
        beside_forward(0)
        qkv0 = leave0[TARGET]
        mixed0, log_sum0 = attend_forward(qkv0, facts)
        state0 = call_forward(0, hidden, mixed0, {})
        start1 = state0[MIXED]
        leave1 = call_leave(1, start1)
        beside_forward(1)
        qkv1 = leave1[TARGET]
        mixed1, log_sum1 = attend_forward(qkv1, facts)
        cotangent = cotangent.astype(BF16)
        if balanced:
            state1 = call_forward(1, start1, mixed1, {COTANGENT_HBM: cotangent})
            back1 = call_backward(
                1,
                state1[MIXED],
                {},
                state1[ENTERED],
                state1[SLOPE_HBM],
                {COTANGENT: state1[MOVED_HBM], REORDER: reorder_low},
            )
            out_hidden = back1[MOVED_HBM]
        else:
            state1 = call_forward(1, start1, mixed1, {})
            out_hidden = swap(turn_low(state1[MIXED]).astype(BF16))
            gradient = turn_low(swap(cotangent))
            back1 = call_backward(1, gradient, {}, state1[ENTERED], state1[SLOPE_HBM], {})
        packs[(UP, 1), GRAD] = grad_dot(state1[ROWS_HBM], back1[ACT_HBM], 0, 0)
        packs[(DOWN, 1), GRAD] = grad_dot(back1[ROWS_HBM], state1[ACT_HBM], 0, 0)
        linear1 = attend_backward(qkv1, mixed1, back1[TARGET], log_sum1, facts)
        packs[(QKV, 1), GRAD] = grad_dot(leave1[ROWS2_HBM], linear1, 0, 1)
        packs[(PROJ, 1), GRAD] = grad_dot(back1[ROWS2_HBM], mixed1, 0, 1)
        back0 = call_backward(
            0,
            back1[MIXED],
            entering(1, linear1, start1),
            state0[ENTERED],
            state0[SLOPE_HBM],
            {},
        )
        packs[(UP, 0), GRAD] = grad_dot(state0[ROWS_HBM], back0[ACT_HBM], 0, 0)
        packs[(DOWN, 0), GRAD] = grad_dot(back0[ROWS_HBM], state0[ACT_HBM], 0, 0)
        target0, packs[(UP, 0), GRAD], packs[(DOWN, 0), GRAD] = lax.optimization_barrier(
            (back0[TARGET], packs[(UP, 0), GRAD], packs[(DOWN, 0), GRAD])
        )
        linear0 = attend_backward(qkv0, mixed0, target0, log_sum0, facts)
        packs[(QKV, 0), GRAD] = grad_dot(leave0[ROWS2_HBM], linear0, 0, 1)
        packs[(PROJ, 0), GRAD] = grad_dot(back0[ROWS2_HBM], mixed0, 0, 1)
        final = chain_call(
            (True, False, False),
            True,
            3 * LAYERS,
            {
                VALUE: back0[MIXED],
                **entering(0, linear0, hidden),
                **({REORDER: reorder_low} if balanced else {}),
            },
            packs,
            jobs.get((BACKWARD, FINAL), ()),
        )
        if balanced:
            grad_hidden = final[MOVED_HBM].astype(F32)
        else:
            grad_hidden = swap(turn_low(final[ENTERED]).astype(BF16)).astype(F32)
            for name in list(packs):
                if name[1] == GRAD:
                    packs[name[0], RESULT] = scatter_blocks(packs[name])
        out_hidden = out_hidden.astype(F32)
        grads, parts = [], []
        for layer, back, linear in ((0, back0, linear0), (1, back1, linear1)):
            result = lambda which: packs[(which, layer), RESULT]
            grads.append(
                (
                    result(QKV).reshape(depth, 3, columns).transpose(1, 0, 2),
                    result(PROJ).T,
                    result(UP),
                    result(DOWN).T,
                )
            )
            qkv_bias_part = jnp.sum(linear.astype(F32), axis=1)
            parts.append((qkv_bias_part.reshape(3, columns), back[UNIT_SUMS][0]))
        sums = [back1[WIDE_SUMS], back0[WIDE_SUMS], final[WIDE_SUMS]]

        stacked = jnp.stack(
            [
                sums[LAYERS - layer - which][at]
                for which, at in ((0, 0), (0, 1), (1, 5), (1, 3), (1, 4), (1, 2))
                for layer in range(LAYERS)
            ]
        )
        stacked = dot(stacked, reorder_full, 1, 0, precision=HIGHEST)
        qkv_padded = lax.dynamic_update_slice_in_dim(
            jnp.zeros((LAYERS * 3, D), F32),
            jnp.concatenate([part[0] for part in parts], axis=0),
            quarter_at * columns,
            1,
        )
        up_padded = lax.dynamic_update_slice_in_dim(
            jnp.zeros((LAYERS, units * mp), F32),
            jnp.stack([part[1] for part in parts]),
            quarter_at * units,
            1,
        )
        by_owner = jnp.concatenate([stacked, qkv_padded], axis=0).reshape(-1, count, each)
        by_owner = jnp.concatenate(
            [
                by_owner.transpose(1, 0, 2).reshape(count, -1),
                up_padded.reshape(LAYERS, count, -1).transpose(1, 0, 2).reshape(count, -1),
            ],
            axis=1,
        )
        mine = scatter_vectors(by_owner)
        wide_grads = mine[: wide_count * each].reshape(len(wide), LAYERS, each)
        qkv_bias_grad = mine[wide_count * each : split].reshape(LAYERS, 3, each)
        up_bias_grad = mine[split:].reshape(LAYERS, -1)
        matrices = [jnp.stack([entry[i] for entry in grads]) for i in range(4)]
        return (
            out_hidden,
            grad_hidden,
            wide_grads[0],
            wide_grads[1],
            matrices[0],
            qkv_bias_grad,
            matrices[1],
            wide_grads[2],
            wide_grads[3],
            wide_grads[4],
            matrices[2],
            up_bias_grad,
            matrices[3],
            wide_grads[5],
        )

    return body


def solution(mesh):
    rows = P(("dp", "mp"), None)
    vector = P(None, ("dp", "mp"))
    vectors = P(None, None, ("dp", "mp"))
    qkv = P(None, None, "dp", "mp")
    tall = P(None, "mp", "dp")
    broad = P(None, "dp", "mp")
    return jax.shard_map(
        make_body(mesh.shape["dp"], mesh.shape["mp"]),
        mesh=mesh,
        in_specs=(
            rows,
            vector,
            vector,
            qkv,
            vectors,
            tall,
            vector,
            vector,
            vector,
            broad,
            vector,
            tall,
            vector,
            P("dp"),
            P(None, "dp"),
            P("dp"),
            rows,
        ),
        out_specs=(
            rows,
            rows,
            vector,
            vector,
            qkv,
            vectors,
            tall,
            vector,
            vector,
            vector,
            broad,
            vector,
            tall,
            vector,
        ),
        check_vma=False,
    )
```

```python
import functools

import jax
import jax.numpy as jnp
from jax import lax
from jax.experimental import pallas as pl
from jax.experimental.layout import Layout, with_layout_constraint
from jax.experimental.pallas import tpu as pltpu
from jax.sharding import PartitionSpec as P

D = 1280
HD = 80
LAYERS = 2
EPSILON = 1e-06
AXES = ("dp", "mp")
F32 = jnp.float32
BF16 = jnp.bfloat16
HIGHEST = lax.Precision.HIGHEST


def normalise(values):
    centre = values - jnp.mean(values, axis=-1, keepdims=True)
    spread = jnp.mean(centre * centre, axis=-1, keepdims=True)
    scale = lax.rsqrt(spread + EPSILON)
    return centre * scale, scale


def norm_backward(values, gain, grad):
    normed, scale = normalise(values)
    inner = grad * gain
    mean_inner = jnp.mean(inner, axis=-1, keepdims=True)
    mean_cross = jnp.mean(inner * normed, axis=-1, keepdims=True)
    grad_values = scale * (inner - mean_inner - normed * mean_cross)
    return grad_values, jnp.sum(grad * normed, axis=0), jnp.sum(grad, axis=0)


def dot(left, right, left_dim, right_dim, kind=F32, precision=None):
    return lax.dot_general(
        left,
        right,
        (((left_dim,), (right_dim,)), ((), ())),
        preferred_element_type=F32,
        precision=precision,
    ).astype(kind)


def grad_dot(left, right, left_dim, right_dim):
    return with_layout_constraint(dot(left, right, left_dim, right_dim, BF16), Layout((0, 1)))


def rotary_tables(coords):
    quarter = HD // 4
    powers = jnp.arange(quarter, dtype=F32) * (4.0 / HD)
    inverse = 10000.0 ** (-powers)
    height_angle = inverse[:, None] * coords[0].astype(F32)[None, :]
    width_angle = inverse[:, None] * coords[1].astype(F32)[None, :]
    angles = jnp.concatenate([height_angle, width_angle], axis=0)
    return (jnp.cos(angles), jnp.sin(angles))


TILE = 256
MASKED = -1e30
LOG2E = 1.4426950408889634
SCORE_SCALE = HD**-0.5 * LOG2E


def mat(left, right):
    return lax.dot_general(left, right, (((1,), (0,)), ((), ())), preferred_element_type=F32)


def mat_turned(left, right):
    return lax.dot_general(left, right, (((1,), (1,)), ((), ())), preferred_element_type=F32)


def tile_bias(code_col, code_row, keys, queries):
    same = code_col[keys, :] == code_row[:, queries]
    return jnp.where(same, 0.0, MASKED)


def tiles(at):
    return pl.ds(pl.multiple_of(at * TILE, TILE), TILE)


def forward_kernel(active, qkv, code_row, code_col, mixed, log_sum, k_rows, top, total, acc):
    heads, length = k_rows.shape[0], k_rows.shape[1]
    blocks = length // TILE
    for head in range(heads):
        base = (heads + head) * HD
        k_rows[head] = turned(qkv[base : base + HD, :]).astype(BF16)

    def query_block(q_at, carry):
        queries = tiles(q_at)
        top[...] = jnp.full(top.shape, MASKED, F32)
        total[...] = jnp.zeros(total.shape, F32)
        acc[...] = jnp.zeros(acc.shape, F32)

        def key_block(k_at, carry):
            @pl.when(active[q_at * blocks + k_at] != 0)
            def _():
                keys = tiles(k_at)
                bias = tile_bias(code_col, code_row, keys, queries)
                every = range(heads)
                scores = [
                    mat(k_rows[head, keys, :], qkv[head * HD : (head + 1) * HD, queries]) + bias
                    for head in every
                ]
                old = [top[head] for head in every]
                new = [
                    jnp.maximum(old[head], jnp.max(scores[head], axis=0, keepdims=True))
                    for head in every
                ]
                chance = [jnp.exp2((scores[head] - new[head]) * SCORE_SCALE) for head in every]
                fade = [jnp.exp2((old[head] - new[head]) * SCORE_SCALE) for head in every]
                added = [jnp.sum(chance[head], axis=0, keepdims=True) for head in every]
                products = [
                    mat(
                        qkv[(2 * heads + head) * HD : (2 * heads + head + 1) * HD, keys],
                        chance[head].astype(BF16),
                    )
                    for head in every
                ]
                for head in every:
                    top[head] = new[head]
                    total[head] = total[head] * fade[head] + added[head]
                    acc[head] = acc[head] * fade[head] + products[head]

            return carry

        lax.fori_loop(0, blocks, key_block, 0)
        for head in range(heads):
            mixed[head * HD : (head + 1) * HD, queries] = (acc[head] / total[head]).astype(BF16)
            log_sum[head, :, queries] = top[head] * SCORE_SCALE + jnp.log2(total[head])
        return carry

    lax.fori_loop(0, blocks, query_block, 0)


def backward_kernel(active, qkv, mixed, grad_mixed, log_sum, cosine, sine, code_row, code_col, out, k_rows, v_rows, centre, grad_q, grad_k, grad_v):
    heads, length = k_rows.shape[0], k_rows.shape[1]
    blocks = length // TILE
    for head in range(heads):
        k_base, v_base = (heads + head) * HD, (2 * heads + head) * HD
        k_rows[head] = qkv[k_base : k_base + HD, :].astype(F32).T.astype(BF16)
        v_rows[head] = qkv[v_base : v_base + HD, :].astype(F32).T.astype(BF16)
        rows = slice(head * HD, (head + 1) * HD)
        centre[head] = jnp.sum(
            grad_mixed[rows, :].astype(F32) * mixed[rows, :].astype(F32), axis=0, keepdims=True
        )
    grad_q[...] = jnp.zeros(grad_q.shape, F32)
    grad_k[...] = jnp.zeros(grad_k.shape, F32)
    grad_v[...] = jnp.zeros(grad_v.shape, F32)

    def query_block(q_at, carry):
        queries = tiles(q_at)

        def key_block(k_at, carry):
            @pl.when(active[q_at * blocks + k_at] != 0)
            def _():
                keys = tiles(k_at)
                bias = tile_bias(code_col, code_row, keys, queries)
                every = range(heads)
                rows = [slice(head * HD, (head + 1) * HD) for head in every]
                scores = [mat(k_rows[h, keys, :], qkv[rows[h], queries]) + bias for h in every]
                raised = [mat(v_rows[h, keys, :], grad_mixed[rows[h], queries]) for h in every]
                chance = [
                    jnp.exp2(scores[h] * SCORE_SCALE - log_sum[h, :, queries]) for h in every
                ]
                pulled = [
                    (chance[h] * (raised[h] - centre[h, :, queries])).astype(BF16) for h in every
                ]
                for_v = [
                    mat_turned(grad_mixed[rows[h], queries], chance[h].astype(BF16)) for h in every
                ]
                for_k = [mat_turned(qkv[rows[h], queries], pulled[h]) for h in every]
                for_q = [
                    mat(qkv[(heads + h) * HD : (heads + h + 1) * HD, keys], pulled[h])
                    for h in every
                ]
                for h in every:
                    grad_v[h, :, keys] += for_v[h]
                    grad_k[h, :, keys] += for_k[h]
                    grad_q[h, :, queries] += for_q[h]

            return carry

        return lax.fori_loop(0, blocks, key_block, carry)

    lax.fori_loop(0, blocks, query_block, 0)
    half = HD // 2
    scale = HD**-0.5
    cos, sin = cosine[...] * scale, sine[...] * scale
    for head in range(heads):
        for which, grad in ((0, grad_q), (1, grad_k)):
            base = (which * heads + head) * HD
            low, high = grad[head, :half, :], grad[head, half:, :]
            turned = jnp.concatenate([low * cos + high * sin, high * cos - low * sin], axis=0)
            out[base : base + HD, :] = turned.astype(BF16)
        base = (2 * heads + head) * HD
        out[base : base + HD, :] = grad_v[head].astype(BF16)


def whole(count):
    return [pl.BlockSpec(memory_space=pltpu.VMEM)] * count


def attend_forward(qkv, facts):
    active, _, _, code_row, code_col = facts
    width, length = qkv.shape
    heads = width // (3 * HD)
    return pl.pallas_call(
        forward_kernel,
        name="attend_forward",
        out_shape=(
            jax.ShapeDtypeStruct((heads * HD, length), BF16),
            jax.ShapeDtypeStruct((heads, 1, length), F32),
        ),
        in_specs=[pl.BlockSpec(memory_space=pltpu.SMEM)] + whole(3),
        out_specs=tuple(whole(2)),
        scratch_shapes=[
            pltpu.VMEM((heads, length, HD), BF16),
            pltpu.VMEM((heads, 1, TILE), F32),
            pltpu.VMEM((heads, 1, TILE), F32),
            pltpu.VMEM((heads, HD, TILE), F32),
        ],
        compiler_params=pltpu.CompilerParams(vmem_limit_bytes=40 << 20),
        cost_estimate=pl.CostEstimate(
            flops=heads * length * length * HD * 4,
            bytes_accessed=4 << 20,
            transcendentals=heads * length * length,
        ),
    )(active, qkv, code_row, code_col)


def attend_backward(qkv, mixed, grad_mixed, log_sum, facts):
    active, cosine, sine, code_row, code_col = facts
    width, length = qkv.shape
    heads = width // (3 * HD)
    return pl.pallas_call(
        backward_kernel,
        name="attend_backward",
        out_shape=jax.ShapeDtypeStruct((width, length), BF16),
        in_specs=[pl.BlockSpec(memory_space=pltpu.SMEM)] + whole(8),
        out_specs=pl.BlockSpec(memory_space=pltpu.VMEM),
        scratch_shapes=[
            pltpu.VMEM((heads, length, HD), BF16),
            pltpu.VMEM((heads, length, HD), BF16),
            pltpu.VMEM((heads, 1, length), F32),
            pltpu.VMEM((heads, HD, length), F32),
            pltpu.VMEM((heads, HD, length), F32),
            pltpu.VMEM((heads, HD, length), F32),
        ],
        compiler_params=pltpu.CompilerParams(vmem_limit_bytes=40 << 20),
        cost_estimate=pl.CostEstimate(
            flops=heads * length * length * HD * 10, bytes_accessed=10 << 20, transcendentals=heads * length * length
        ),
    )(active, qkv, mixed, grad_mixed, log_sum, cosine, sine, code_row, code_col)


def tile_overlap(codes):
    blocks = codes.reshape(-1, TILE)
    least, most = jnp.min(blocks, axis=1), jnp.max(blocks, axis=1)
    meet = (least[:, None] <= most[None, :]) & (least[None, :] <= most[:, None])
    return meet.astype(jnp.int32).reshape(-1)


(
    ACT, ALL, ATTN, BACKWARD, CORE, CORNER, CORNERS, CROSS, DIAGONAL, DOWN, ENDS, ENTER, ENTERED,
    ENTER_AT, ENTER_BIAS, ENTER_GAIN, ENTER_W, FAR_IN, FAR_OUT, FAR_OWN, FINAL, FIRST,
    FIRST_BIAS, FORWARD, FROM_HIGH, FROM_LOW, GRAD, HELD, HERE, HIGH, LEAVE, LEAVE_BIAS,
    LEAVE_GAIN, LEAVE_SHIFT, LEAVE_W, LINE, LINE_IN, LINE_OUT, LOW, MINE, MIX, MIXED, MIX_AT,
    MIX_GAIN, MIX_SHIFT, NEAR_IN, NEAR_OUT, OWN, OWNED, PAIR, PROJ, QKV, REMOTE, REORDER, RESULT,
    ROWS, ROWS2, ROWS_OUT, SECOND, SECOND_BIAS, SLOPE, SOURCE, STATE, SUMS, TARGET, UNIT_SUMS,
    UP, VALUE, WIDE_SUMS,
) = range(69)
ONE, OTHER = 103, 104
COTANGENT, COSINE, SINE = 100, 101, 102
FIRST_HBM = 200
COTANGENT_HBM = FIRST_HBM + 50
(
    ACT_HBM, FACTS_HBM, HIDDEN_HBM, MOVED_HBM, ROWS2_HBM, ROWS_HBM, ROW_FACTS_HBM, SLOPE_HBM,
    VECTORS_HBM, VECTOR_HBM,
) = range(FIRST_HBM, FIRST_HBM + 10)


STRIP = 256
PARTS = 2
MESH_ID = pl.DeviceIdType.MESH


def strips(at):
    return pl.ds(pl.multiple_of(at * STRIP, STRIP), STRIP)


def partners():
    dp_at, mp_at = lax.axis_index("dp"), lax.axis_index("mp")
    core = dp_at + 1 - 2 * lax.rem(dp_at, 2)
    cross = mp_at + 2 - 4 * (mp_at // 2)
    return {
        CORE: {"dp": core},
        LINE: {"mp": mp_at + 1 - 2 * lax.rem(mp_at, 2)},
        CROSS: {"mp": cross},
        DIAGONAL: {"dp": core, "mp": cross},
        LOW: {"dp": dp_at + 2 - 4 * lax.rem(dp_at // 2, 2)},
        HIGH: {"dp": dp_at + 4 - 8 * lax.rem(dp_at // 4, 2)},
    }


def greet(names):
    barrier, devices = pltpu.get_barrier_semaphore(), partners()
    for name in names:
        pl.semaphore_signal(barrier, inc=1, device_id=devices[name], device_id_type=MESH_ID)
    return lambda: pl.semaphore_wait(barrier, len(names))


class Courier:
    def __init__(self, ref):
        self.ref, self.devices = ref, partners()
        self.remotes, self.locals = 0, 0
        self.open = {}
        self.aligned = lax.rem(lax.axis_index("dp"), 2) == lax.axis_index("mp") // 2

    def slot(self):
        self.remotes += 1
        return self.remotes - 1

    def remote(self, source, target, partner, at, received=None):
        sems = self.ref[REMOTE]
        received = at if received is None else received
        return pltpu.make_async_remote_copy(
            src_ref=source,
            dst_ref=target,
            send_sem=sems.at[0, at],
            recv_sem=sems.at[1, received],
            device_id=self.devices[partner],
            device_id_type=MESH_ID,
        )

    def send(self, source, target, partner):
        copy = self.remote(source, target, partner, self.slot())
        copy.start()
        return copy

    def near(self, source, target):
        return pltpu.make_async_copy(source, target, self.ref[HERE].at[self.locals])

    def local(self, source, target):
        copy = self.near(source, target)
        self.locals += 1
        copy.start()
        return copy

    def swap(self, source, target):
        at, copy = self.slot(), self.near(source, target)
        self.locals += 1
        away = lambda: self.remote(source, target, DIAGONAL, at)
        pl.when(self.aligned)(copy.start)
        pl.when(jnp.logical_not(self.aligned))(lambda: away().start())

        def finish():
            pl.when(self.aligned)(copy.wait)
            pl.when(jnp.logical_not(self.aligned))(lambda: away().wait())

        return finish

    def begin(self, pack, step):
        ref = self.ref
        buffer = lambda part: ref[(pack, part)]
        if step == 1:
            mine, pair = buffer(MINE), buffer(PAIR)
            first, second, copy = self.slot(), self.slot(), self.near(mine, pair.at[0])
            self.locals += 1
            across = lambda: self.remote(mine, pair.at[1], CROSS, first)
            beside = lambda: self.remote(mine, pair.at[1], CORE, first)
            over = lambda: self.remote(mine, pair.at[0], DIAGONAL, second)

            def start_aligned():
                copy.start()
                across().start()

            def start_other():
                beside().start()
                over().start()

            def wait_aligned():
                copy.wait()
                across().wait()

            def wait_other():
                beside().wait()
                over().wait()

            pl.when(self.aligned)(start_aligned)
            pl.when(jnp.logical_not(self.aligned))(start_other)

            def finish():
                pl.when(self.aligned)(wait_aligned)
                pl.when(jnp.logical_not(self.aligned))(wait_other)

        elif step > 4:
            self.finish(pack, step - 1)
            finish = self.reduce(pack, step)
        else:
            self.finish(pack, step - 1)
            if step == 4:
                depth = buffer(CORNERS).shape[1]
                block = lambda at: buffer(GRAD).at[at * depth : (at + 1) * depth]
                copies = [
                    self.send(block(6), buffer(CORNERS).at[0], HIGH),
                    self.send(block(7), buffer(CORNERS).at[1], LOW),
                ]
            elif step == 2:
                pair = buffer(PAIR)
                copies = [self.send(pair, buffer(side), side) for side in (LOW, HIGH)]
            else:
                copies = [
                    self.send(buffer(LOW).at[0], buffer(CORNER).at[0], HIGH),
                    self.send(buffer(HIGH).at[1], buffer(CORNER).at[1], LOW),
                ]

            def finish():
                for copy in copies:
                    copy.wait()

        self.open[pack, step] = finish

    def fetch(self, columns, terms):
        held = self.ref[HELD, columns]
        loads = [self.local(term, held.at[at]) for at, term in enumerate(terms)]
        for load in loads:
            load.wait()
        return lambda at: held[at].astype(F32)

    def reduce(self, pack, step):
        ref = self.ref
        buffer = lambda part: ref[pack, part]
        if step == 7:
            ends = buffer(ENDS)
            columns = ends.shape[2]
            term = self.fetch(columns, [ends.at[0], ends.at[1]])
            result = ref[RESULT, columns, pack]
            result[...] = term(0) + term(1)
            return self.local(result, buffer(RESULT)).wait
        depth, columns = buffer(GRAD).shape[0] // 8, buffer(GRAD).shape[1]
        block = lambda at: buffer(GRAD).at[at * depth : (at + 1) * depth]
        sums = ref[SUMS, pack]
        if step == 5:
            from_low, from_high = buffer(FROM_LOW), buffer(FROM_HIGH)
            corners = [buffer(CORNERS).at[at] for at in range(2)]
            copies = [
                self.send(block(3), from_low.at[1], LOW),
                self.send(block(4), from_high.at[0], HIGH),
            ]
            term = self.fetch(columns, [block(2), block(5), *corners])
            for at in range(2):
                sums[at] = (term(at) + term(2 + at)).astype(BF16)
            copies.append(self.send(sums.at[0], from_low.at[0], LOW))
            copies.append(self.send(sums.at[1], from_high.at[1], HIGH))

            def finish():
                for copy in copies:
                    copy.wait()

            return finish
        ends, sides = buffer(ENDS), (buffer(FROM_LOW), buffer(FROM_HIGH))
        term = self.fetch(
            columns, [block(0), block(1)] + [side.at[at] for side in sides for at in range(2)]
        )
        for at in range(2):
            sums[at] = (term(at) + term(2 + at) + term(4 + at)).astype(BF16)
        first, second = self.slot(), self.slot()
        copy = self.near(sums.at[0], ends.at[0])
        self.locals += 1
        beside = lambda: self.remote(sums.at[1], ends.at[0], CORE, first)
        over = lambda: self.remote(sums.at[0], ends.at[1], DIAGONAL, second)
        across = lambda: self.remote(sums.at[1], ends.at[1], CROSS, first, second)

        def start_aligned():
            copy.start()
            beside().start()

        def start_other():
            over().start()
            across().start()

        def wait_aligned():
            copy.wait()
            beside().wait_send()
            over().wait_recv()

        def wait_other():
            over().wait()
            across().wait_send()
            beside().wait_recv()

        pl.when(self.aligned)(start_aligned)
        pl.when(jnp.logical_not(self.aligned))(start_other)

        def finish():
            pl.when(self.aligned)(wait_aligned)
            pl.when(jnp.logical_not(self.aligned))(wait_other)

        return finish

    def finish(self, pack, step):
        finish = self.open.pop((pack, step), None)
        if finish is not None:
            finish()

    def finish_all(self):
        for finish in self.open.values():
            finish()
        self.open = {}


PACK_PARTS = {
    1: (PAIR,),
    2: (LOW, HIGH),
    3: (CORNER,),
    4: (CORNERS,),
    5: (FROM_LOW, FROM_HIGH),
    6: (ENDS,),
    7: (RESULT,),
}
PACK_NEEDS = {
    1: (MINE,),
    2: (PAIR,),
    3: (LOW, HIGH),
    4: (GRAD,),
    5: (GRAD, CORNERS),
    6: (GRAD, FROM_LOW, FROM_HIGH),
    7: (ENDS,),
}


def pack_buffers(jobs, packs):
    needs, makes, scratch = {}, {}, {}
    for pack, step in jobs:
        for part in PACK_NEEDS[step]:
            if (pack, part) not in makes:
                needs[pack, part] = packs[pack, part]
        if step < 4:
            depth, columns = packs[(pack, MINE)].shape
        else:
            depth, columns = packs[(pack, GRAD)].shape
            depth //= 8
            scratch[HELD, columns] = pltpu.VMEM((6, depth, columns), BF16)
            if step in (5, 6):
                scratch[SUMS, pack] = pltpu.VMEM((2, depth, columns), BF16)
        for part in PACK_PARTS[step]:
            made = jax.ShapeDtypeStruct((2, depth, columns), BF16)
            if part == RESULT:
                made = jax.ShapeDtypeStruct((depth, columns), F32)
                scratch[RESULT, columns, pack] = pltpu.VMEM((depth, columns), F32)
            makes[(pack, part)] = made
    return needs, makes, scratch, 4 * len(jobs), 9 * len(jobs)


def start_kernel(jobs, names, *refs):
    ref = dict(zip(names, refs))
    greeted = greet((CORE, LINE, CROSS, DIAGONAL, LOW, HIGH))
    courier = Courier(ref)
    greeted()
    facts = courier.swap(ref[FACTS_HBM], ref[ROW_FACTS_HBM])
    vector, vectors = ref[VECTOR_HBM], ref[VECTORS_HBM]
    courier.local(vector, vectors.at[0]).wait()
    rows = None
    size = 1
    for partner in (LINE, CROSS, CORE, LOW, HIGH):
        courier.send(vectors.at[0:size], vectors.at[size : 2 * size], partner).wait()
        size *= 2
        if partner == CROSS:
            courier.begin(*jobs[0])
            rows = courier.swap(ref[HIDDEN_HBM], ref[MOVED_HBM])
    for job in jobs[1:]:
        courier.begin(*job)
    rows()
    facts()
    courier.finish_all()


def start_call(collective, hidden, facts, vector, jobs, packs):
    anywhere = pl.BlockSpec(memory_space=pl.ANY)
    needs, makes, _, remote, here = pack_buffers(jobs, packs)
    shape = jax.ShapeDtypeStruct
    inputs = {HIDDEN_HBM: hidden, FACTS_HBM: facts, VECTOR_HBM: vector, **needs}
    outputs = {
        MOVED_HBM: shape(hidden.shape, hidden.dtype),
        ROW_FACTS_HBM: shape(facts.shape, facts.dtype),
        VECTORS_HBM: shape((32, *vector.shape), vector.dtype),
        **makes,
    }
    names = (*inputs, *outputs, REMOTE, HERE)
    results = pl.pallas_call(
        functools.partial(start_kernel, jobs, names),
        name="start_exchange",
        out_shape=tuple(outputs.values()),
        in_specs=[anywhere] * len(inputs),
        out_specs=(anywhere,) * len(outputs),
        scratch_shapes=[
            pltpu.SemaphoreType.DMA((2, remote + 7)),
            pltpu.SemaphoreType.DMA((here + 3,)),
        ],
        compiler_params=pltpu.CompilerParams(collective_id=collective, has_side_effects=True),
        cost_estimate=pl.CostEstimate(flops=0, bytes_accessed=64 << 20, transcendentals=0),
    )(*inputs.values())
    results = dict(zip(outputs, results))
    packs.update({name: results[name] for name in makes})
    return results


def turned(values):
    return values.astype(F32).T


def joined(pieces, axis=0):
    return pieces[0] if len(pieces) == 1 else jnp.concatenate(pieces, axis=axis)


def chain_kernel(stages, backward, names, plan, jobs, *refs):
    ref = dict(zip(names, refs))
    enter, mix, leave = stages
    value, state, own, far_own = ref[VALUE], ref[STATE], ref[OWN], ref[FAR_OWN]
    count, width = value.shape
    step = count // PARTS
    greeted = greet(tuple(partners()) if jobs or MOVED_HBM in ref else (CORE, LINE))
    courier = Courier(ref)
    send, local = courier.send, courier.local
    core, line = CORE, LINE
    waiting = list(jobs)

    def point(at):
        while waiting and waiting[0][0] <= at:
            courier.begin(*waiting.pop(0)[1:])

    def chunk(slot, part):
        return slice(slot * count + part * step, slot * count + (part + 1) * step)

    def place(part):
        return slice(part * step, (part + 1) * step)

    made = {(pack, part): (pack, at) for _, pack, at in jobs for part in PACK_PARTS[at]}
    loads = {}

    def load(name, blocks):
        return [
            local(ref[piece].at[index, :, begin:end], ref[name].at[row : row + depth, :])
            for piece, index, row, depth, begin, end in blocks
        ]

    for name, blocks in plan:
        loads[name] = load(name, [block for block in blocks if block[0] not in made])

    def loaded(name):
        late = [block for weight, blocks in plan if weight == name for block in blocks]
        late = [block for block in late if block[0] in made]
        for block in late:
            courier.finish(*made[block[0]])
        for copy in loads[name] + load(name, late):
            copy.wait()

    if mix and backward:
        loads[SLOPE] = [local(ref[SLOPE_HBM], ref[SLOPE])]
    saves = []
    if backward:
        ref[WIDE_SUMS][...] = jnp.zeros(ref[WIDE_SUMS].shape, F32)

    def add_wide(row, sums):
        if sums.ndim == 1:
            sums = sums[None]
        ref[WIDE_SUMS][row : row + 1, :] += sums

    def product(pieces, weight, stores, transposed_source=False):
        def strip(at, carry):
            columns = strips(at)
            result = mat_turned(pieces, weight[columns, : pieces.shape[1]])
            begin = 0
            for size, store in stores:
                store(columns, result[begin : begin + size])
                begin += size
            return carry

        lax.fori_loop(0, width // STRIP, strip, 0, unroll=True)

    def put(target, index):
        def store(columns, result):
            target[index, :, columns] = result.astype(target.dtype)

        return store

    def scatter(prefix, source, weight):
        far_out, far_in = ref[prefix, FAR_OUT], ref[prefix, FAR_IN]
        line_out, line_in = ref[prefix, LINE_OUT], ref[prefix, LINE_IN]
        near_out, near_in = ref[prefix, NEAR_OUT], ref[prefix, NEAR_IN]

        def far(part):
            product(
                source([(2, part), (3, part)]),
                weight,
                [(step, put(far_own, part)), (step, put(far_out, part))],
            )
            return send(far_out.at[part], far_in.at[part], core)

        def pass_on(part, passing):
            passing.wait()
            line_out[part] = (far_own[part] + far_in[part].astype(F32)).astype(BF16)
            return send(line_out.at[part], line_in.at[part], line)

        def near():
            product(
                source([(1, part) for part in range(PARTS)]),
                weight,
                [(step, put(near_out, part)) for part in range(PARTS)],
            )
            return send(near_out, near_in, core)

        def mine():
            product(
                source([(0, part) for part in range(PARTS)]),
                weight,
                [(step, put(own, part)) for part in range(PARTS)],
            )

        def total(part):
            return own[part] + near_in[part].astype(F32) + line_in[part].astype(F32)

        return far, pass_on, near, mine, total

    def lower(values, gain, shift):
        if backward:
            return values.astype(BF16)
        return (normalise(values)[0] * gain[...] + shift[...]).astype(BF16)

    def begin_rows(rows, part):
        near = send(rows.at[chunk(0, part)], rows.at[chunk(1, part)], core)
        far = send(rows.at[chunk(0, part)], rows.at[chunk(2, part)], line)
        return near, far

    def forward_rows(rows, part, far):
        far.wait()
        return send(rows.at[chunk(2, part)], rows.at[chunk(3, part)], core)

    ready = None
    if enter:
        source_t = ref[SOURCE]

        def entering(pieces):
            return turned(joined([source_t[:, chunk(*piece)] for piece in pieces], 1)).astype(BF16)

        far, pass_on, near, mine, total = scatter(ENTER, entering, ref[ENTER_W])
        loaded(ENTER_W)
        greeted()
        point(0)
        if COTANGENT_HBM in ref:
            moved = courier.swap(ref[COTANGENT_HBM], ref[MOVED_HBM])
        passing = [far(part) for part in range(PARTS)]
        lines = [pass_on(part, passing[part]) for part in range(PARTS)]
        near_sum = near()
        mine()
        point(1)
        near_sum.wait()
        point(2)

        def ready(part):
            lines[part].wait()
            at = place(part)
            if backward:
                grad, gains, shifts = norm_backward(
                    ref[ENTER_AT][at, :], ref[ENTER_GAIN][...], total(part)
                )
                state[at, :] = value[at, :] + grad
                add_wide(0, gains)
                add_wide(1, shifts)
            else:
                state[at, :] = value[at, :] + (total(part) + ref[ENTER_BIAS][...])
            ref[ENTERED][at, :] = state[at, :]

    else:
        greeted()
        point(0)

        if COTANGENT in ref:
            lowered = mat(value[...].astype(BF16), ref[REORDER][...])
            ref[ROWS_OUT][...] = lowered.astype(BF16)
            moved = courier.swap(ref[ROWS_OUT], ref[MOVED_HBM])
            state[...] = mat(ref[COTANGENT][...], ref[REORDER][...])

        def ready(part):
            at = place(part)
            if COTANGENT not in ref:
                state[at, :] = value[at, :]

    if mix:
        rows, act, slope = ref[ROWS], ref[ACT], ref[SLOPE]
        first, second = ref[FIRST], ref[SECOND]
        units = first.shape[1]
        if backward:
            ref[UNIT_SUMS][...] = jnp.zeros(ref[UNIT_SUMS].shape, F32)
        begun = []
        for part in range(PARTS):
            ready(part)
            lowered = lower(
                state[place(part), :], ref.get(MIX_GAIN), ref.get(MIX_SHIFT)
            )
            rows[chunk(0, part), :] = lowered
            begun.append(begin_rows(rows, part))
            if backward:
                add_wide(2, jnp.sum(lowered.astype(F32), axis=0))

        def expand(pieces):
            taken = joined([rows[chunk(*piece), :] for piece in pieces])

            def strip(at, carry):
                columns = strips(at)
                up = mat(taken, first[:, columns])
                tilt = None
                if backward:
                    slopes = joined([slope[chunk(*piece), columns] for piece in pieces])
                    out = (up * slopes.astype(F32)).astype(BF16)
                    ref[UNIT_SUMS][:, columns] += jnp.sum(
                        out.astype(F32), axis=0, keepdims=True
                    )
                else:
                    up = up + ref[FIRST_BIAS][:, columns]
                    sigmoid = 1.0 / (1.0 + jnp.exp(-1.702 * up))
                    gated = up * sigmoid
                    out = gated.astype(BF16)
                    tilt = (sigmoid + 1.702 * gated * (1.0 - sigmoid)).astype(BF16)
                for index, piece in enumerate(pieces):
                    at_rows = slice(index * step, (index + 1) * step)
                    act[chunk(*piece), columns] = out[at_rows]
                    if tilt is not None:
                        slope[chunk(*piece), columns] = tilt[at_rows]
                return carry

            lax.fori_loop(0, units // STRIP, strip, 0, unroll=True)

        def acting(pieces):
            return joined([act[chunk(*piece), :] for piece in pieces])

        far, pass_on, near, mine, total = scatter(MIX, acting, second)
        loaded(FIRST)
        if backward:
            loaded(SLOPE)
        expand([(0, part) for part in range(PARTS)])
        for part in range(PARTS):
            begun[part][0].wait()
        point(3)
        expand([(1, part) for part in range(PARTS)])
        loaded(SECOND)
        near_sum = near()
        point(4)
        forwards = [forward_rows(rows, 0, begun[0][1])]
        mine()
        lines = []
        for part in range(PARTS):
            forwards[part].wait()
            expand([(2, part), (3, part)])
            lines.append(pass_on(part, far(part)))
            if part + 1 < PARTS:
                forwards.append(forward_rows(rows, part + 1, begun[part + 1][1]))
            point(5 + part)
        saves.append(local(rows, ref[ROWS_HBM]))
        saves.append(local(act, ref[ACT_HBM]))
        if not backward:
            saves.append(local(slope, ref[SLOPE_HBM]))
        near_sum.wait()

        def ready(part):
            lines[part].wait()
            at = place(part)
            if backward:
                grad, gains, shifts = norm_backward(
                    ref[MIX_AT][at, :], ref[MIX_GAIN][...], total(part)
                )
                state[at, :] = state[at, :] + grad
                add_wide(3, gains)
                add_wide(4, shifts)
            else:
                state[at, :] = state[at, :] + (total(part) + ref[SECOND_BIAS][...])
            ref[MIXED][at, :] = state[at, :]

    if leave:
        rows2, weight, target = ref[ROWS2], ref[LEAVE_W], ref[TARGET]
        begun = []
        for part in range(PARTS):
            ready(part)
            lowered = lower(
                state[place(part), :], ref.get(LEAVE_GAIN), ref.get(LEAVE_SHIFT)
            )
            rows2[chunk(0, part), :] = lowered
            begun.append(begin_rows(rows2, part))
            if backward:
                add_wide(5, jnp.sum(lowered.astype(F32), axis=0))

        def leaving(pieces):
            result = mat(joined([rows2[chunk(*piece), :] for piece in pieces]), weight[...])
            if not backward:
                result = result + ref[LEAVE_BIAS][...]
            result = turned(result)
            if not backward:
                cos, sin = (
                    joined([ref[name][:, chunk(*piece)] for piece in pieces], 1)
                    for name in (COSINE, SINE)
                )
                half, third = HD // 2, result.shape[0] // 3
                blocks = []
                for base in range(0, 2 * third, HD):
                    low, high = result[base : base + half], result[base + half : base + HD]
                    blocks += [low * cos - high * sin, high * cos + low * sin]
                result = jnp.concatenate(blocks + [result[2 * third :]], axis=0)
            result = result.astype(BF16)
            for index, piece in enumerate(pieces):
                target[:, chunk(*piece)] = result[:, index * step : (index + 1) * step]

        loaded(LEAVE_W)
        point(7)
        leaving([(0, part) for part in range(PARTS)])
        for part in range(PARTS):
            begun[part][0].wait()
        leaving([(1, part) for part in range(PARTS)])
        point(8)
        forwards = [forward_rows(rows2, part, begun[part][1]) for part in range(PARTS)]
        for part in range(PARTS):
            forwards[part].wait()
            leaving([(2, part), (3, part)])
        saves.append(local(rows2, ref[ROWS2_HBM]))
    else:
        for part in range(PARTS):
            ready(part)
    if REORDER in ref and COTANGENT not in ref:
        lowered = mat(state[...].astype(BF16), ref[REORDER][...]).astype(BF16)
        rows_out = ref[ROWS_OUT]
        rows_out[...] = lowered
        moved = courier.swap(rows_out, ref[MOVED_HBM])
    point(9)
    if MOVED_HBM in ref:
        moved()
    for save in saves:
        save.wait()
    courier.finish_all()


class Weight:
    def __init__(self, pack, begin, end):
        self.pack, self.begin, self.end = pack, begin, end


def chain_call(stages, backward, collective, operands, packs, jobs=()):
    enter, mix, leave = stages
    count, width = operands[VALUE].shape
    step = count // PARTS
    shape = jax.ShapeDtypeStruct
    vmem, anywhere = pl.BlockSpec(memory_space=pltpu.VMEM), pl.BlockSpec(memory_space=pl.ANY)
    outputs, scratch = {}, {}
    buffers = lambda kind: pltpu.VMEM((PARTS, step, width), kind)
    scratch[STATE] = pltpu.VMEM((count, width), F32)
    scratch[OWN] = buffers(F32)
    scratch[FAR_OWN] = buffers(F32)
    remote, here = 0, 0
    if backward:
        outputs[WIDE_SUMS] = shape((8, width), F32)
    flops = 0
    plan = []
    passed = {}
    needs, makes, job_scratch, job_remote, job_here = pack_buffers([job[1:] for job in jobs], packs)
    scratch.update(job_scratch)
    remote, here = remote + job_remote, here + job_here
    for name, value in operands.items():
        if not isinstance(value, Weight):
            passed[name] = value
            continue
        blocks, row = [], 0
        for part in (PAIR, LOW, HIGH, CORNER, ONE, OTHER, ALL):
            piece = (value.pack, part)
            if piece not in packs and piece not in makes:
                continue
            if piece not in makes:
                passed[piece] = packs[piece]
            array = makes.get(piece, packs.get(piece))
            for index in range(array.shape[0]):
                blocks.append((piece, index, row, array.shape[1], value.begin, value.end))
                row += array.shape[1]
        plan.append((name, blocks))
        scratch[name] = pltpu.VMEM((width, value.end - value.begin), BF16)
        here += len(blocks)
        flops += 8 * count * width * (value.end - value.begin)
    passed.update({name: value for name, value in needs.items() if name not in passed})
    outputs.update(makes)
    for stage, prefix in ((enter, ENTER), (mix, MIX)):
        if stage:
            for name in (FAR_OUT, FAR_IN, LINE_OUT, LINE_IN, NEAR_OUT, NEAR_IN):
                scratch[prefix, name] = buffers(BF16)
            remote += 2 * PARTS + 1
    if enter:
        outputs[ENTERED] = shape((count, width), F32)
    if mix:
        units = operands[FIRST].end - operands[FIRST].begin
        scratch[ROWS] = pltpu.VMEM((4 * count, width), BF16)
        scratch[ACT] = pltpu.VMEM((4 * count, units), BF16)
        scratch[SLOPE] = pltpu.VMEM((4 * count, units), BF16)
        outputs[MIXED] = shape((count, width), F32)
        outputs[ROWS_HBM] = shape((4 * count, width), BF16)
        outputs[ACT_HBM] = shape((4 * count, units), BF16)
        if backward:
            outputs[UNIT_SUMS] = shape((1, units), F32)
        else:
            outputs[SLOPE_HBM] = shape((4 * count, units), BF16)
        remote += 3 * PARTS
        here += 3
    if leave:
        columns = leave
        scratch[ROWS2] = pltpu.VMEM((4 * count, width), BF16)
        outputs[TARGET] = shape((columns, 4 * count), BF16)
        outputs[ROWS2_HBM] = shape((4 * count, width), BF16)
        remote += 3 * PARTS
        here += 1
    if REORDER in operands or COTANGENT_HBM in operands:
        if REORDER in operands:
            scratch[ROWS_OUT] = pltpu.VMEM((count, width), BF16)
        outputs[MOVED_HBM] = shape((count, width), BF16)
        remote, here = remote + 1, here + 1
    scratch[REMOTE] = pltpu.SemaphoreType.DMA((2, remote))
    scratch[HERE] = pltpu.SemaphoreType.DMA((here,))
    names = tuple(passed) + tuple(outputs) + tuple(scratch)
    spec = lambda name: anywhere if isinstance(name, tuple) or name >= FIRST_HBM else vmem
    results = pl.pallas_call(
        functools.partial(chain_kernel, stages, backward, names, plan, jobs),
        name="chain_backward" if backward else "chain_forward",
        out_shape=tuple(outputs.values()),
        in_specs=[spec(name) for name in passed],
        out_specs=tuple(spec(name) for name in outputs),
        scratch_shapes=list(scratch.values()),
        compiler_params=pltpu.CompilerParams(
            collective_id=collective, has_side_effects=True, vmem_limit_bytes=54 << 20
        ),
        cost_estimate=pl.CostEstimate(
            flops=flops, bytes_accessed=(16 << 20) * sum(map(bool, stages)), transcendentals=0
        ),
    )(*passed.values())
    results = dict(zip(outputs, results))
    packs.update({name: results[name] for name in makes})
    return results


def make_body(dp, mp):
    assert mp == 4 and dp >= 2 and dp & (dp - 1) == 0
    count = dp * mp
    high_bits = [1 << b for b in range(1, dp.bit_length() - 1)]

    def across(value, bit):
        return lax.ppermute(value, "dp", [(i, i ^ bit) for i in range(dp)])

    def core_side(value):
        return across(value, 1)

    def line_side(value):
        return lax.ppermute(value, "mp", [(i, i ^ 1) for i in range(mp)])

    def swapped(d, m):
        return (d & ~1 | m >> 1) * mp + ((d & 1) << 1 | m & 1)

    swap_pairs = [
        (d * mp + m, swapped(d, m)) for d in range(dp) for m in range(mp) if d & 1 != m >> 1
    ]

    def swap(value):
        stays = (lax.axis_index("dp") & 1) == (lax.axis_index("mp") >> 1)
        return jnp.where(stays, value, lax.ppermute(value, ("dp", "mp"), swap_pairs))

    balanced = len(high_bits) == 2

    def gather_pair(mine):
        return swap(jnp.stack([mine, core_side(mine)]))

    def gather_sides(pair):
        for bit in high_bits:
            pair = jnp.concatenate([pair, across(pair, bit)], axis=0)
        return (pair,)

    def add(*terms):
        total = terms[0].astype(F32)
        for term in terms[1:]:
            total = total + term.astype(F32)
        return total.astype(BF16)

    def scatter_blocks(grad):
        total = grad.reshape(dp, D // dp, -1)
        for bit in high_bits[::-1]:
            half = total.shape[0] // 2
            total = add(total[:half], across(total[half:], bit))
        total = swap(total)
        return total[0].astype(F32) + core_side(total[1]).astype(F32)

    def arranged(values):
        index = lax.axis_index("dp") * mp + lax.axis_index("mp")
        at = jnp.arange(count, dtype=jnp.int32)
        order = (at[:, None] ^ index) == at[None, :]
        return dot(order.astype(F32), values, 1, 0, precision=HIGHEST)

    def gather_vectors(mine):
        values = mine[None]
        bit = 1
        while bit < count:
            if bit >= mp:
                got = across(values, bit // mp)
            else:
                got = lax.ppermute(values, "mp", [(i, i ^ bit) for i in range(mp)])
            values = jnp.concatenate([values, got], axis=0)
            bit *= 2
        return arranged(values)

    def scatter_vectors(values):
        index = lax.axis_index("dp") * mp + lax.axis_index("mp")
        bit = count // 2
        while bit:
            half = values.shape[0] // 2
            top = (index & bit) != 0
            low, high = values[:half], values[half:]
            sent = jnp.where(top, low, high)
            if bit >= mp:
                got = across(sent, bit // mp)
            else:
                got = lax.ppermute(sent, "mp", [(i, i ^ bit) for i in range(mp)])
            values = jnp.where(top, high, low) + got
            bit //= 2
        return values[0]

    def body(
        hidden_in,
        pre_gain,
        pre_bias,
        qkv_weight,
        qkv_bias,
        proj_weight,
        proj_bias,
        mid_gain,
        mid_bias,
        up_weight,
        up_bias,
        down_weight,
        down_bias,
        picture_ids,
        positions,
        pad_mask,
        cotangent,
    ):
        dp_at, mp_at = lax.axis_index("dp"), lax.axis_index("mp")
        group_at = (dp_at & ~1) | (mp_at >> 1)
        quarter_at = ((dp_at & 1) << 1) | (mp_at & 1)
        depth = D // dp
        columns = qkv_weight.shape[3]
        units = up_weight.shape[2]
        heads = columns // HD

        place = jnp.arange(D, dtype=jnp.int32)
        moved = ((place // depth) ^ group_at) * depth + place % depth
        reorder = place[:, None] == moved[None, :]
        reorder_low = reorder.astype(BF16)
        reorder_full = reorder.astype(F32)

        def turn_low(values):
            return dot(values.astype(BF16), reorder_low, 1, 0)

        qkv_width, proj_width = 3 * columns, columns
        packs = {}
        for layer in range(LAYERS):
            mine = qkv_weight[layer].transpose(1, 0, 2).reshape(depth, qkv_width)
            packs[(QKV, layer), MINE] = mine
            packs[(PROJ, layer), MINE] = proj_weight[layer].T
            packs[(UP, layer), MINE] = up_weight[layer]
            packs[(DOWN, layer), MINE] = down_weight[layer].T

        wide = (pre_gain, pre_bias, proj_bias, mid_gain, mid_bias, down_bias)
        packed = jnp.concatenate(
            [item.reshape(-1) for item in wide] + [qkv_bias.reshape(-1), up_bias.reshape(-1)]
        )
        length = picture_ids.shape[0]
        quarter = length // mp
        row_at = jnp.arange(length, dtype=jnp.int32)
        codes = jnp.where(pad_mask == 1, picture_ids, 1024 + row_at)
        row_facts = jnp.concatenate([codes[None], positions], axis=0)
        hidden = hidden_in.astype(BF16)
        jobs = {}
        if balanced:
            space = -(-packed.shape[0] // 1024) * 1024
            late = packs[(QKV, 1), MINE], packs[(DOWN, 1), MINE], packs[(PROJ, 1), MINE]
            hidden, late = lax.optimization_barrier((hidden, late))
            packs[(QKV, 1), MINE], packs[(DOWN, 1), MINE], packs[(PROJ, 1), MINE] = late
            begun = start_call(
                3 * LAYERS + 1,
                hidden,
                jnp.pad(row_facts, ((0, 5), (0, 0))),
                jnp.pad(packed, (0, space - packed.shape[0])).reshape(-1, 128),
                (((QKV, 0), 1), ((QKV, 0), 2), ((PROJ, 0), 1), ((UP, 0), 1), ((QKV, 0), 3)),
                packs,
            )
            hidden, row_facts = begun[MOVED_HBM], begun[ROW_FACTS_HBM][:3]
            packed = arranged(begun[VECTORS_HBM].reshape(count, space))[:, : packed.shape[0]]
            schedule = {
                (LEAVE, 0): {
                    0: ((UP, 0, 2), (PROJ, 0, 2), (DOWN, 0, 1)),
                    8: ((PROJ, 0, 3),),
                },
                (FORWARD, 0): {
                    0: ((DOWN, 0, 2), (QKV, 1, 1)),
                    2: ((DOWN, 0, 3), (PROJ, 1, 1)),
                    4: ((QKV, 1, 2), (PROJ, 1, 2), (UP, 1, 1)),
                    6: ((QKV, 1, 3), (PROJ, 1, 3)),
                },
                (LEAVE, 1): {0: ((UP, 1, 2), (DOWN, 1, 1))},
                (FORWARD, 1): {0: ((DOWN, 1, 2),), 2: ((DOWN, 1, 3),)},
                (BACKWARD, 0): {
                    0: ((UP, 1, 4), (DOWN, 1, 4)),
                    1: ((UP, 1, 5),),
                    4: ((DOWN, 1, 5), (QKV, 1, 4), (PROJ, 1, 4)),
                    5: ((UP, 1, 6),),
                    8: ((DOWN, 1, 6), (QKV, 1, 5), (PROJ, 1, 5)),
                },
                (BACKWARD, FINAL): {
                    0: ((UP, 0, 4), (DOWN, 0, 4)),
                    1: ((UP, 0, 5),),
                    2: ((QKV, 1, 6), (PROJ, 1, 6), (QKV, 0, 4), (PROJ, 0, 4)),
                    9: (
                        *((UP, 0, 6), (DOWN, 0, 5), (QKV, 0, 5), (UP, 1, 7), (DOWN, 1, 7)),
                        *((DOWN, 0, 6), (PROJ, 0, 5), (QKV, 1, 7), (PROJ, 1, 7), (UP, 0, 7)),
                        *((QKV, 0, 6), (PROJ, 0, 6), (DOWN, 0, 7), (QKV, 0, 7), (PROJ, 0, 7)),
                    ),
                },
            }
            jobs = {
                kernel: tuple(
                    (at, (name, layer), step)
                    for at, steps in points.items()
                    for name, layer, step in steps
                )
                for kernel, points in schedule.items()
            }
        else:
            for name in list(packs):
                packs[name[0], ALL] = gather_sides(gather_pair(packs[name]))[0].reshape(1, D, -1)
            hidden, row_facts, packed = swap(hidden), swap(row_facts), gather_vectors(packed)
        hidden = turn_low(hidden)
        each = D // count
        wide_count = len(wide) * LAYERS
        split = (wide_count + 3 * LAYERS) * each
        vectors = packed[:, :split].reshape(count, -1, each).transpose(1, 0, 2).reshape(-1, D)
        wide_all = dot(vectors[:wide_count], reorder_full, 1, 0, precision=HIGHEST)
        wide_all = wide_all.reshape(len(wide), LAYERS, D)
        pre_gain_all, pre_bias_all, proj_bias_all, mid_gain_all, mid_bias_all, down_bias_all = (
            wide_all[i] for i in range(len(wide))
        )
        qkv_bias_mine = lax.dynamic_slice_in_dim(
            vectors[wide_count:], quarter_at * columns, columns, 1
        ).reshape(LAYERS, 3 * columns)
        up_all = packed[:, split:].reshape(count, LAYERS, -1).transpose(1, 0, 2)
        up_bias_mine = lax.dynamic_slice_in_dim(
            up_all.reshape(LAYERS, -1), quarter_at * units, units, 1
        )

        row_facts = jnp.concatenate(
            [
                lax.dynamic_slice_in_dim(row_facts, (quarter_at ^ which) * quarter, quarter, 1)
                for which in (0, 2, 1, 3)
            ],
            axis=1,
        )
        codes = row_facts[0]
        facts = (tile_overlap(codes), *rotary_tables(row_facts[1:]), codes[None], codes[:, None])

        row = lambda vector: vector[None]
        weights = [
            (
                Weight((QKV, layer), 0, qkv_width),
                Weight((PROJ, layer), 0, proj_width),
                Weight((UP, layer), 0, units),
                Weight((DOWN, layer), 0, units),
            )
            for layer in range(LAYERS)
        ]

        def leave_forward(layer):
            return {
                LEAVE_W: weights[layer][0],
                LEAVE_GAIN: row(pre_gain_all[layer]),
                LEAVE_SHIFT: row(pre_bias_all[layer]),
                LEAVE_BIAS: row(qkv_bias_mine[layer]),
                COSINE: facts[1],
                SINE: facts[2],
            }

        def call_leave(layer, value):
            return chain_call(
                (False, False, qkv_width),
                False,
                layer,
                {VALUE: value, **leave_forward(layer)},
                packs,
                jobs.get((LEAVE, layer), ()),
            )

        def call_forward(layer, value, mixed, more):
            return chain_call(
                (True, True, False),
                False,
                LAYERS + layer,
                {
                    VALUE: value,
                    SOURCE: mixed,
                    ENTER_W: weights[layer][1],
                    ENTER_BIAS: row(proj_bias_all[layer]),
                    FIRST: weights[layer][2],
                    SECOND: weights[layer][3],
                    FIRST_BIAS: row(up_bias_mine[layer]),
                    SECOND_BIAS: row(down_bias_all[layer]),
                    MIX_GAIN: row(mid_gain_all[layer]),
                    MIX_SHIFT: row(mid_bias_all[layer]),
                    **more,
                },
                packs,
                jobs.get((FORWARD, layer), ()),
            )

        def call_backward(layer, value, entering, middle, slope, more):
            return chain_call(
                (bool(entering), True, proj_width),
                True,
                2 * LAYERS + layer,
                {
                    VALUE: value,
                    **entering,
                    **more,
                    FIRST: weights[layer][3],
                    SECOND: weights[layer][2],
                    SLOPE_HBM: slope,
                    MIX_AT: middle,
                    MIX_GAIN: row(mid_gain_all[layer]),
                    LEAVE_W: weights[layer][1],
                },
                packs,
                jobs.get((BACKWARD, layer), ()),
            )

        def entering(layer, grad_linear, start):
            return {
                SOURCE: grad_linear,
                ENTER_W: weights[layer][0],
                ENTER_AT: start,
                ENTER_GAIN: row(pre_gain_all[layer]),
            }

        def beside_forward(layer):
            if not balanced:
                return
            low, high = high_bits
            up = (UP, layer)
            packs[up, ONE] = across(packs[up, LOW][:1], high)
            packs[up, OTHER] = across(packs[up, HIGH][1:], low)

        hidden, wide_all, qkv_bias_mine, up_bias_mine, facts = lax.optimization_barrier(
            (hidden, wide_all, qkv_bias_mine, up_bias_mine, facts)
        )
        pre_gain_all, pre_bias_all, proj_bias_all, mid_gain_all, mid_bias_all, down_bias_all = (
            wide_all[i] for i in range(len(wide))
        )
        leave0 = call_leave(0, hidden)
        beside_forward(0)
        qkv0 = leave0[TARGET]
        mixed0, log_sum0 = attend_forward(qkv0, facts)
        state0 = call_forward(0, hidden, mixed0, {})
        start1 = state0[MIXED]
        leave1 = call_leave(1, start1)
        beside_forward(1)
        qkv1 = leave1[TARGET]
        mixed1, log_sum1 = attend_forward(qkv1, facts)
        cotangent = cotangent.astype(BF16)
        if balanced:
            state1 = call_forward(1, start1, mixed1, {COTANGENT_HBM: cotangent})
            back1 = call_backward(
                1,
                state1[MIXED],
                {},
                state1[ENTERED],
                state1[SLOPE_HBM],
                {COTANGENT: state1[MOVED_HBM], REORDER: reorder_low},
            )
            out_hidden = back1[MOVED_HBM]
        else:
            state1 = call_forward(1, start1, mixed1, {})
            out_hidden = swap(turn_low(state1[MIXED]).astype(BF16))
            gradient = turn_low(swap(cotangent))
            back1 = call_backward(1, gradient, {}, state1[ENTERED], state1[SLOPE_HBM], {})
        packs[(UP, 1), GRAD] = grad_dot(state1[ROWS_HBM], back1[ACT_HBM], 0, 0)
        packs[(DOWN, 1), GRAD] = grad_dot(back1[ROWS_HBM], state1[ACT_HBM], 0, 0)
        linear1 = attend_backward(qkv1, mixed1, back1[TARGET], log_sum1, facts)
        packs[(QKV, 1), GRAD] = grad_dot(leave1[ROWS2_HBM], linear1, 0, 1)
        packs[(PROJ, 1), GRAD] = grad_dot(back1[ROWS2_HBM], mixed1, 0, 1)
        back0 = call_backward(
            0,
            back1[MIXED],
            entering(1, linear1, start1),
            state0[ENTERED],
            state0[SLOPE_HBM],
            {},
        )
        packs[(UP, 0), GRAD] = grad_dot(state0[ROWS_HBM], back0[ACT_HBM], 0, 0)
        packs[(DOWN, 0), GRAD] = grad_dot(back0[ROWS_HBM], state0[ACT_HBM], 0, 0)
        target0, packs[(UP, 0), GRAD], packs[(DOWN, 0), GRAD] = lax.optimization_barrier(
            (back0[TARGET], packs[(UP, 0), GRAD], packs[(DOWN, 0), GRAD])
        )
        linear0 = attend_backward(qkv0, mixed0, target0, log_sum0, facts)
        packs[(QKV, 0), GRAD] = grad_dot(leave0[ROWS2_HBM], linear0, 0, 1)
        packs[(PROJ, 0), GRAD] = grad_dot(back0[ROWS2_HBM], mixed0, 0, 1)
        final = chain_call(
            (True, False, False),
            True,
            3 * LAYERS,
            {
                VALUE: back0[MIXED],
                **entering(0, linear0, hidden),
                **({REORDER: reorder_low} if balanced else {}),
            },
            packs,
            jobs.get((BACKWARD, FINAL), ()),
        )
        if balanced:
            grad_hidden = final[MOVED_HBM].astype(F32)
        else:
            grad_hidden = swap(turn_low(final[ENTERED]).astype(BF16)).astype(F32)
            for name in list(packs):
                if name[1] == GRAD:
                    packs[name[0], RESULT] = scatter_blocks(packs[name])
        out_hidden = out_hidden.astype(F32)
        grads, parts = [], []
        for layer, back, linear in ((0, back0, linear0), (1, back1, linear1)):
            result = lambda which: packs[(which, layer), RESULT]
            grads.append(
                (
                    result(QKV).reshape(depth, 3, columns).transpose(1, 0, 2),
                    result(PROJ).T,
                    result(UP),
                    result(DOWN).T,
                )
            )
            qkv_bias_part = jnp.sum(linear.astype(F32), axis=1)
            parts.append((qkv_bias_part.reshape(3, columns), back[UNIT_SUMS][0]))
        sums = [back1[WIDE_SUMS], back0[WIDE_SUMS], final[WIDE_SUMS]]

        stacked = jnp.stack(
            [
                sums[LAYERS - layer - which][at]
                for which, at in ((0, 0), (0, 1), (1, 5), (1, 3), (1, 4), (1, 2))
                for layer in range(LAYERS)
            ]
        )
        stacked = dot(stacked, reorder_full, 1, 0, precision=HIGHEST)
        qkv_padded = lax.dynamic_update_slice_in_dim(
            jnp.zeros((LAYERS * 3, D), F32),
            jnp.concatenate([part[0] for part in parts], axis=0),
            quarter_at * columns,
            1,
        )
        up_padded = lax.dynamic_update_slice_in_dim(
            jnp.zeros((LAYERS, units * mp), F32),
            jnp.stack([part[1] for part in parts]),
            quarter_at * units,
            1,
        )
        by_owner = jnp.concatenate([stacked, qkv_padded], axis=0).reshape(-1, count, each)
        by_owner = jnp.concatenate(
            [
                by_owner.transpose(1, 0, 2).reshape(count, -1),
                up_padded.reshape(LAYERS, count, -1).transpose(1, 0, 2).reshape(count, -1),
            ],
            axis=1,
        )
        mine = scatter_vectors(by_owner)
        wide_grads = mine[: wide_count * each].reshape(len(wide), LAYERS, each)
        qkv_bias_grad = mine[wide_count * each : split].reshape(LAYERS, 3, each)
        up_bias_grad = mine[split:].reshape(LAYERS, -1)
        matrices = [jnp.stack([entry[i] for entry in grads]) for i in range(4)]
        return (
            out_hidden,
            grad_hidden,
            wide_grads[0],
            wide_grads[1],
            matrices[0],
            qkv_bias_grad,
            matrices[1],
            wide_grads[2],
            wide_grads[3],
            wide_grads[4],
            matrices[2],
            up_bias_grad,
            matrices[3],
            wide_grads[5],
        )

    return body


def solution(mesh):
    rows = P(("dp", "mp"), None)
    vector = P(None, ("dp", "mp"))
    vectors = P(None, None, ("dp", "mp"))
    qkv = P(None, None, "dp", "mp")
    tall = P(None, "mp", "dp")
    broad = P(None, "dp", "mp")
    return jax.shard_map(
        make_body(mesh.shape["dp"], mesh.shape["mp"]),
        mesh=mesh,
        in_specs=(
            rows,
            vector,
            vector,
            qkv,
            vectors,
            tall,
            vector,
            vector,
            vector,
            broad,
            vector,
            tall,
            vector,
            P("dp"),
            P(None, "dp"),
            P("dp"),
            rows,
        ),
        out_specs=(
            rows,
            rows,
            vector,
            vector,
            qkv,
            vectors,
            tall,
            vector,
            vector,
            vector,
            broad,
            vector,
            tall,
            vector,
        ),
        check_vma=False,
    )
```
